256 devices in a mesh: space: 64 (over z, y, core), view: 4 (over x).
Axes of the slice: x: 4, y: 4, z: 8, core: 2. Of those that a mesh axis runs over, the one named last changes fastest.
Arguments:
- params: float32 [59, 131072], P(None, 'space'), may hold values from -8 to 1026, as said below
- visible: int32 [64, 128, 16], P('space'), may hold values from 0 to 2047, as said below
- blocks: int32 [64, 128], P('space'), may hold values from 0 to 63, as said below
- counts: int32 [64, 64], P('space'), may hold values from 1 to 2
- depth_rank: int32 [4, 64], P('view'), may hold values from 0 to 63, each once within a row
- camera: float32 [4, 3], P('view'), may hold values from -0.006 to 0.006
- background: float32 [4, 3], P('view'), may hold values from 0 to 1
- target: float32 [4, 3, 1024, 512], P('view', None, 'space'), may hold values from 0 to 1
Outputs:
- grad_params: float32 [59, 131072], P(None, 'space')
- rendered: float32 [4, 3, 1024, 512], P('view', None, 'space')
- loss: float32 [4], P('view')
The draws below stay inside these ranges and needn't reach their ends.
Inputs may be any that keep to these rules, and one draw needn't show every extreme that they name: `visible`: each row of a subspace's table lists 16 different splats of that subspace in increasing order; every splat of the subspace is listed exactly once. Slot j of a subspace goes to owner j // 2; the 2 slots that one subspace sends to one owner name different blocks. counts[s, o] live slots lead the 2 slots that subspace s sends to owner o. `params`: rows 6 to 9 of a column hold a quaternion whose first component lies in [1, 2].
All inputs are finite; a program needn't handle non-finite values.
Results may differ from the reference program's by a relative error of at most 0.0003.
Values sent between devices are 32-bit elements; how exact they have to be, the bound alone decides.
No kernel may reach another device: no remote copies, remote signals or barrier semaphores. Data moves between devices by JAX's collectives and lax.ppermute only.
A program may use at most 64 MiB of HBM per device.

```python
import math
import jax
import jax.numpy as jnp
from jax import lax

K = 16
SEG_DEV = 128
ROWS_DEV = 16
IMG_W = 512
SUBS = 64
VIEWS = 4
CAP = 2
SPL = 2048
HEIGHT = 1024
BLK_DEV = 64
N_VIEW = 4


def layout(key):
    base_key = jax.random.fold_in(key, 7)
    key_blocks, key_lists = jax.random.split(base_key)
    scores = jax.random.randint(key_blocks, (SUBS, SUBS, BLK_DEV), 0, 1 << 20) * BLK_DEV + jnp.arange(BLK_DEV)[None, None, :]
    chosen = jnp.argsort(scores, axis=-1)[:, :, :CAP].astype(jnp.int32).reshape(SUBS, SEG_DEV)
    rank_keys = jax.random.randint(key_lists, (SUBS, SPL), 0, 1 << 16) * SPL + jnp.arange(SPL)[None, :]
    listing = jnp.argsort(rank_keys, axis=-1).astype(jnp.int32)
    return (chosen, listing)


def draw_visible(key, part):
    chosen, listing = layout(key)
    return jnp.sort(listing.reshape(SUBS, SEG_DEV, K), axis=-1).astype(jnp.int32)


def draw_blocks(key, part):
    chosen, listing = layout(key)
    return chosen


def draw_params(key, part):
    chosen, listing = layout(key)
    home_slot = jnp.argsort(listing, axis=-1).astype(jnp.int32) // K
    home_owner = home_slot // CAP
    home_block = jnp.take_along_axis(chosen, home_slot, axis=1)
    corner_y = (home_owner * ROWS_DEV + home_block // (IMG_W // 16) * 8).astype(jnp.float32)
    corner_x = (home_block % (IMG_W // 16) * 16).astype(jnp.float32)
    subkeys = jax.random.split(jax.random.fold_in(key, 3), 8)
    grid_shape = (SUBS, SPL)
    pos_x = corner_x + jax.random.uniform(subkeys[0], grid_shape, jnp.float32, -2.0, 18.0)
    pos_y = corner_y + jax.random.uniform(subkeys[1], grid_shape, jnp.float32, -2.0, 10.0)
    depths = jax.random.uniform(subkeys[2], grid_shape, jnp.float32, -8.0, 8.0)
    log_scale = jax.random.uniform(subkeys[3], (3, SUBS, SPL), jnp.float32, 0.0, 1.8)
    quat_real = jax.random.uniform(subkeys[4], grid_shape, jnp.float32, 1.0, 2.0)
    quat_rest = jax.random.uniform(subkeys[5], (3, SUBS, SPL), jnp.float32, -1.0, 1.0)
    logits = jax.random.uniform(subkeys[6], grid_shape, jnp.float32, -2.0, 3.0)
    harmonic = jnp.clip(0.3 * jax.random.normal(subkeys[7], (48, SUBS, SPL), jnp.float32), -1.2, 1.2)
    stacked = jnp.concatenate([pos_x[None], pos_y[None], depths[None], log_scale, quat_real[None], quat_rest, logits[None], harmonic], axis=0)
    return stacked.reshape(59, SUBS * SPL).astype(jnp.float32)


def with_ends(values, own_key, least, top_value):
    dims = values.shape
    index_at = [jax.random.randint(jax.random.fold_in(own_key, axis), (), 0, dims[axis]) for axis in range(len(dims))]
    values = values.at[tuple(index_at)].set(least)
    longest = dims.index(max(dims))
    index_at[longest] = (index_at[longest] + 1) % dims[longest]
    return values.at[tuple(index_at)].set(top_value)


def level_of(stream_key, dims, cuts, low, largest):
    gain = 1.0
    for axis_at, parts in cuts:
        steps = jax.random.uniform(jax.random.fold_in(jax.random.fold_in(stream_key, 6), axis_at), (parts,), jnp.float32, low / len(cuts), largest / len(cuts))
        gain = gain * jnp.repeat(jnp.exp(steps), dims[axis_at] // parts).reshape((-1,) + (1,) * (len(dims) - 1 - axis_at))
    return gain


def setup_inputs(seed: int = 0) -> dict:
    key_list = jax.random.split(jax.random.key(seed), 9)
    return {
        "params": draw_params(jax.random.fold_in(key_list[8], 71), 0),
        "visible": draw_visible(jax.random.fold_in(key_list[8], 71), 0),
        "blocks": draw_blocks(jax.random.fold_in(key_list[8], 71), 0),
        "counts": with_ends(jax.random.randint(key_list[3], (SUBS, SUBS), 1, CAP + 1), jax.random.fold_in(key_list[3], 1), 1, CAP).astype(jnp.int32),
        "depth_rank": jax.vmap(lambda own: jax.random.permutation(own, SUBS))(jax.random.split(key_list[4], VIEWS)).reshape((VIEWS, SUBS)).astype(jnp.int32),
        "camera": jnp.clip(jax.random.uniform(key_list[5], (VIEWS, 3), jnp.float32, -0.006, 0.006) * level_of(key_list[5], (VIEWS, 3), ((0, 4),), -0.4, 0.0), -0.006, 0.006),
        "background": jnp.clip(1.0 * jax.random.uniform(key_list[6], (VIEWS, 3), jnp.float32) ** level_of(key_list[6], (VIEWS, 3), ((0, 4),), -0.2, 0.2), 0.0, 1.0),
        "target": jnp.clip(1.0 * jax.random.uniform(key_list[7], (VIEWS, 3, HEIGHT, IMG_W), jnp.float32) ** level_of(key_list[7], (VIEWS, 3, HEIGHT, IMG_W), ((0, 4), (2, 64)), -0.2, 0.2), 0.0, 1.0),
    }


HIGHEST = lax.Precision.HIGHEST
SH_ZERO = 0.28209479177387814
SH_ONE = 0.4886025119029199
SH_TWO = (1.0925484305920792, -1.0925484305920792, 0.31539156525252005, -1.0925484305920792, 0.5462742152960396)
SH_THREE = (-0.5900435899266435, 2.890611442640554, -0.4570457994644658, 0.3731763325901154, -0.4570457994644658, 1.445305721320277, -0.5900435899266435)
DILATION = 0.3
SMOOTHING = 0.0001
SSIM_FIRST = 0.0001
SSIM_SECOND = 0.0009

def camera_rotation(angles):
    cos_a, sin_a = (jnp.cos(angles[0]), jnp.sin(angles[0]))
    cos_b, sin_b = (jnp.cos(angles[1]), jnp.sin(angles[1]))
    cos_c, sin_c = (jnp.cos(angles[2]), jnp.sin(angles[2]))
    unity = jnp.ones_like(cos_a)
    nought = jnp.zeros_like(cos_a)
    turn_x = jnp.stack([jnp.stack([unity, nought, nought]), jnp.stack([nought, cos_a, -sin_a]), jnp.stack([nought, sin_a, cos_a])])
    turn_y = jnp.stack([jnp.stack([cos_b, nought, sin_b]), jnp.stack([nought, unity, nought]), jnp.stack([-sin_b, nought, cos_b])])
    turn_z = jnp.stack([jnp.stack([cos_c, -sin_c, nought]), jnp.stack([sin_c, cos_c, nought]), jnp.stack([nought, nought, unity])])
    return jnp.dot(jnp.dot(turn_z, turn_y, precision=HIGHEST), turn_x, precision=HIGHEST)

def harmonics(view_axis):
    axis_x, axis_y, axis_z = (view_axis[0], view_axis[1], view_axis[2])
    sq_x, sq_y, sq_z = (axis_x * axis_x, axis_y * axis_y, axis_z * axis_z)
    values = [SH_ZERO * jnp.ones_like(axis_x), -SH_ONE * axis_y, SH_ONE * axis_z, -SH_ONE * axis_x, SH_TWO[0] * axis_x * axis_y, SH_TWO[1] * axis_y * axis_z, SH_TWO[2] * (2.0 * sq_z - sq_x - sq_y), SH_TWO[3] * axis_x * axis_z, SH_TWO[4] * (sq_x - sq_y), SH_THREE[0] * axis_y * (3.0 * sq_x - sq_y), SH_THREE[1] * axis_x * axis_y * axis_z, SH_THREE[2] * axis_y * (4.0 * sq_z - sq_x - sq_y), SH_THREE[3] * axis_z * (2.0 * sq_z - 3.0 * sq_x - 3.0 * sq_y), SH_THREE[4] * axis_x * (4.0 * sq_z - sq_x - sq_y), SH_THREE[5] * axis_z * (sq_x - sq_y), SH_THREE[6] * axis_x * (sq_x - 3.0 * sq_y)]
    return jnp.stack(values)

def project(param_in, angles, centre_x, centre_y):
    turn = camera_rotation(angles)
    scales = jnp.exp(param_in[3:6])
    quaternion = param_in[6:10]
    quaternion = quaternion / jnp.sqrt(lax.optimization_barrier(jnp.sum(quaternion * quaternion, axis=0)))
    part_w, part_x, part_y, part_z = (quaternion[0], quaternion[1], quaternion[2], quaternion[3])
    spin = [[1.0 - 2.0 * (part_y * part_y + part_z * part_z), 2.0 * (part_x * part_y - part_w * part_z), 2.0 * (part_x * part_z + part_w * part_y)], [2.0 * (part_x * part_y + part_w * part_z), 1.0 - 2.0 * (part_x * part_x + part_z * part_z), 2.0 * (part_y * part_z - part_w * part_x)], [2.0 * (part_x * part_z - part_w * part_y), 2.0 * (part_y * part_z + part_w * part_x), 1.0 - 2.0 * (part_x * part_x + part_y * part_y)]]
    frame = [[(turn[row, 0] * spin[0][col] + turn[row, 1] * spin[1][col] + turn[row, 2] * spin[2][col]) * scales[col] for col in range(3)] for row in range(2)]
    cov_xx = frame[0][0] * frame[0][0] + frame[0][1] * frame[0][1] + frame[0][2] * frame[0][2] + DILATION
    cov_xy = frame[0][0] * frame[1][0] + frame[0][1] * frame[1][1] + frame[0][2] * frame[1][2]
    cov_yy = frame[1][0] * frame[1][0] + frame[1][1] * frame[1][1] + frame[1][2] * frame[1][2] + DILATION
    determinant = cov_xx * cov_yy - cov_xy * cov_xy
    shift_x = param_in[0] - centre_x
    shift_y = param_in[1] - centre_y
    mean_u = turn[0, 0] * shift_x + turn[0, 1] * shift_y + turn[0, 2] * param_in[2] + centre_x
    mean_w = turn[1, 0] * shift_x + turn[1, 1] * shift_y + turn[1, 2] * param_in[2] + centre_y
    opacity = jax.nn.sigmoid(param_in[10])
    basis = harmonics(turn[2])
    coeffs = param_in[11:59].reshape(16, 3, param_in.shape[1])
    colour = 0.5 + lax.optimization_barrier(jnp.sum(basis[:, None, None] * coeffs, axis=0))
    record = jnp.stack([mean_u, mean_w, cov_yy / determinant, -cov_xy / determinant, cov_xx / determinant, opacity])
    return jnp.concatenate([record, colour], axis=0)

def render(gathered, grid_x, grid_y):
    delta_x = grid_x[:, None, :] - gathered[0][:, :, None]
    delta_y = grid_y[:, None, :] - gathered[1][:, :, None]
    powers = 0.5 * (gathered[2][:, :, None] * delta_x * delta_x + 2.0 * gathered[3][:, :, None] * delta_x * delta_y + gathered[4][:, :, None] * delta_y * delta_y)
    alphas = gathered[5][:, :, None] * jnp.exp(-powers)
    kept_log = jnp.log1p(-alphas)
    before = jnp.cumsum(kept_log, axis=1) - kept_log
    weights = alphas * jnp.exp(before)
    colour = jnp.einsum('skp,csk->scp', weights, gathered[6:9], precision=HIGHEST)
    return jnp.concatenate([colour, lax.optimization_barrier(jnp.sum(kept_log, axis=1))[:, None, :]], axis=1)

def pixel_grid(owners, blocks_used, strip_rows, block_cols):
    inner = jnp.arange(128).astype(jnp.int32)
    corner_y = owners * strip_rows + blocks_used // block_cols * 8
    corner_x = blocks_used % block_cols * 16
    grid_y = (corner_y[:, None] + inner[None, :] // 16).astype(jnp.float32) + 0.5
    grid_x = (corner_x[:, None] + inner[None, :] % 16).astype(jnp.float32) + 0.5
    return (grid_x, grid_y)

def composite(pieces, target_ids, depth_ranks, backdrop, block_rows, block_cols):
    block_count = block_rows * block_cols
    onehot = (target_ids[:, :, None] == jnp.arange(block_count).astype(jnp.int32)[None, None, :]).astype(jnp.float32)
    dense = jnp.einsum('scb,scqp->bsqp', onehot, pieces, precision=HIGHEST)
    kept_log = dense[:, :, 3]
    nearer = (depth_ranks[None, :] < depth_ranks[:, None]).astype(jnp.float32)
    before = jnp.einsum('st,btp->bsp', nearer, kept_log, precision=HIGHEST)
    picture = jnp.einsum('bsp,bscp->bcp', jnp.exp(before), dense[:, :, 0:3], precision=HIGHEST)
    picture = picture + backdrop[None, :, None] * jnp.exp(lax.optimization_barrier(jnp.sum(kept_log, axis=1)))[:, None, :]
    picture = picture.reshape(block_rows, block_cols, 3, 8, 16).transpose(2, 0, 3, 1, 4)
    return picture.reshape(3, block_rows * 8, block_cols * 16)

def blur_taps():
    raw_taps = [math.exp(-(offset - 5) * (offset - 5) / 4.5) for offset in range(11)]
    total = sum(raw_taps)
    return [value / total for value in raw_taps]

def blur(values, count):
    taps = blur_taps()
    width_px = values.shape[2]
    padded = jnp.pad(values, ((0, 0), (0, 0), (5, 5)))
    across = taps[0] * padded[:, :, 0:width_px]
    for offset in range(1, 11):
        across = across + taps[offset] * padded[:, :, offset:offset + width_px]
    result = taps[0] * across[:, 0:count]
    for offset in range(1, 11):
        result = result + taps[offset] * across[:, offset:offset + count]
    return result

def pixel_terms(picture, goal, count):
    mean_a = blur(picture, count)
    mean_b = blur(goal, count)
    var_a = blur(picture * picture, count) - mean_a * mean_a
    var_b = blur(goal * goal, count) - mean_b * mean_b
    cov_ab = blur(picture * goal, count) - mean_a * mean_b
    ssim = (2.0 * mean_a * mean_b + SSIM_FIRST) * (2.0 * cov_ab + SSIM_SECOND) / ((mean_a * mean_a + mean_b * mean_b + SSIM_FIRST) * (var_a + var_b + SSIM_SECOND))
    differ = picture[:, 5:5 + count] - goal[:, 5:5 + count]
    return 0.8 * jnp.sqrt(differ * differ + SMOOTHING) + 0.2 * (1.0 - ssim)

def reference(params, visible, blocks, counts, depth_rank, camera, background, target):
    subs_count = visible.shape[0]
    slot_total = visible.shape[1]
    capacity = slot_total // subs_count
    height_px = ROWS_DEV * subs_count
    width_px = IMG_W
    block_rows = ROWS_DEV // 8
    block_cols = IMG_W // 16
    slot_owner = (jnp.arange(slot_total) // capacity).astype(jnp.int32)
    live = jnp.arange(capacity).astype(jnp.int32)[None, None, :] < counts[:, :, None]
    target_ids = jnp.where(live, blocks.reshape(subs_count, subs_count, capacity), -1).astype(jnp.int32)
    grad_total = jnp.zeros(params.shape, jnp.float32)
    pictures = []
    losses = []
    for view_index in range(N_VIEW):

        def view_sum(param_in):
            records = project(param_in, camera[view_index], 0.5 * width_px, 0.5 * height_px)

            def one_sender(sender):
                local = lax.dynamic_slice_in_dim(records, sender * SPL, SPL, 1)
                lists = lax.dynamic_index_in_dim(visible, sender, 0, keepdims=False)
                slot_blocks = lax.dynamic_index_in_dim(blocks, sender, 0, keepdims=False)
                grid_x, grid_y = pixel_grid(slot_owner, slot_blocks, ROWS_DEV, block_cols)
                return render(local[:, lists], grid_x, grid_y)
            segments = lax.map(jax.checkpoint(one_sender), jnp.arange(subs_count).astype(jnp.int32))
            segments = segments.reshape(subs_count, subs_count, capacity, 4, 128)

            def one_owner(owner):
                pieces = lax.dynamic_index_in_dim(segments, owner, 1, keepdims=False)
                owned_ids = lax.dynamic_index_in_dim(target_ids, owner, 1, keepdims=False)
                return composite(pieces, owned_ids, depth_rank[view_index], background[view_index], block_rows, block_cols)
            strips = lax.map(jax.checkpoint(one_owner), jnp.arange(subs_count).astype(jnp.int32))
            picture = strips.transpose(1, 0, 2, 3).reshape(3, height_px, width_px)
            padded = jnp.pad(picture, ((0, 0), (5, 5), (0, 0)))
            goal = jnp.pad(target[view_index], ((0, 0), (5, 5), (0, 0)))
            return (jnp.sum(pixel_terms(padded, goal, height_px)), picture)
        (view_total, picture), view_grad = jax.value_and_grad(view_sum, has_aux=True)(params)
        grad_total = grad_total + view_grad
        pictures.append(picture)
        losses.append(view_total / (3.0 * height_px * width_px))
    return (grad_total, jnp.stack(pictures), jnp.stack(losses))
```

```python
import math

import jax
import jax.numpy as jnp
from jax import lax
from jax.experimental import pallas as pl
from jax.experimental.pallas import tpu as pltpu
from jax.sharding import PartitionSpec as P

F32 = jnp.float32
BF16 = jnp.bfloat16
I32 = jnp.int32

SH_ZERO = 0.28209479177387814
SH_ONE = 0.4886025119029199
SH_TWO = (
    1.0925484305920792,
    -1.0925484305920792,
    0.31539156525252005,
    -1.0925484305920792,
    0.5462742152960396,
)
SH_THREE = (
    -0.5900435899266435,
    2.890611442640554,
    -0.4570457994644658,
    0.3731763325901154,
    -0.4570457994644658,
    1.445305721320277,
    -0.5900435899266435,
)
DILATION = 0.3
SMOOTHING = 0.0001
SSIM_FIRST = 0.0001
SSIM_SECOND = 0.0009

K = 16
LANES = 128
CHUNKS = 4
GROUP = 4
META = 144
TABLE = 152


def taps():
    raw = [math.exp(-(offset - 5) * (offset - 5) / 4.5) for offset in range(11)]
    total = sum(raw)
    return [value / total for value in raw]


TAPS = taps()


def iota(shape, axis):
    return lax.broadcasted_iota(I32, shape, axis)


def row(x, index, rows):
    return jnp.broadcast_to(x[index : index + 1, :], (rows, x.shape[1]))


def turn_of(angles):
    cos_a, cos_b, cos_c = (jnp.cos(angle) for angle in angles)
    sin_a, sin_b, sin_c = (jnp.sin(angle) for angle in angles)
    return [
        [cos_c * cos_b, cos_c * sin_b * sin_a - sin_c * cos_a, cos_c * sin_b * cos_a + sin_c * sin_a],
        [sin_c * cos_b, sin_c * sin_b * sin_a + cos_c * cos_a, sin_c * sin_b * cos_a - cos_c * sin_a],
        [-sin_b, cos_b * sin_a, cos_b * cos_a],
    ]


def harmonics(axis):
    x, y, z = axis
    xx, yy, zz = (x * x, y * y, z * z)
    return [
        SH_ZERO * jnp.ones_like(x),
        -SH_ONE * y,
        SH_ONE * z,
        -SH_ONE * x,
        SH_TWO[0] * x * y,
        SH_TWO[1] * y * z,
        SH_TWO[2] * (2.0 * zz - xx - yy),
        SH_TWO[3] * x * z,
        SH_TWO[4] * (xx - yy),
        SH_THREE[0] * y * (3.0 * xx - yy),
        SH_THREE[1] * x * y * z,
        SH_THREE[2] * y * (4.0 * zz - xx - yy),
        SH_THREE[3] * z * (2.0 * zz - 3.0 * xx - 3.0 * yy),
        SH_THREE[4] * x * (4.0 * zz - xx - yy),
        SH_THREE[5] * z * (xx - yy),
        SH_THREE[6] * x * (xx - 3.0 * yy),
    ]


def camera_values(rows):
    angles = [jnp.broadcast_to(rows[i : i + 1, :], (8, LANES)) for i in range(3)]
    turn = turn_of(angles)
    basis = harmonics(turn[2])
    cell = lambda value: value[0:1, 0:1]
    return [[cell(value) for value in line] for line in turn], [cell(value) for value in basis]


def load_params(p_ref, scratch):
    for tile in range(8):
        count = min(8, 59 - tile * 8)
        for chunk in range(16):
            scratch[tile, chunk * 8 : chunk * 8 + count, :] = p_ref[
                tile * 8 : tile * 8 + count, chunk * LANES : (chunk + 1) * LANES
            ]


def dense_row(scratch, index):
    return scratch[index // 8, pl.ds(index % 8, 16, stride=8), :]


def spin_of(quaternion):
    w, x, y, z = quaternion
    return [
        [1.0 - 2.0 * (y * y + z * z), 2.0 * (x * y - w * z), 2.0 * (x * z + w * y)],
        [2.0 * (x * y + w * z), 1.0 - 2.0 * (x * x + z * z), 2.0 * (y * z - w * x)],
        [2.0 * (x * z - w * y), 2.0 * (y * z + w * x), 1.0 - 2.0 * (x * x + y * y)],
    ]


def sigmoid(x):
    return 1.0 / (1.0 + jnp.exp(-x))


def unit(quaternion):
    total = sum(part * part for part in quaternion)
    inverse = 1.0 / jnp.sqrt(total)
    return [part * inverse for part in quaternion], inverse


def slot_lists(vis_ref):
    natural = vis_ref[0].T
    lane = iota((K, LANES), 1)
    order = (lane % 64) * 2 + lane // 64
    return jnp.take_along_axis(natural, order, axis=1), order


def to_message(out_ref, table):
    first = table[0:LANES, :].T
    rest = jnp.concatenate(
        [table[LANES:TABLE, :], jnp.zeros((2 * LANES - TABLE, LANES), F32)], axis=0
    ).T
    out_ref[:, 0:LANES] = first[0:64]
    out_ref[:, LANES : 2 * LANES] = first[64:128]
    out_ref[:, 2 * LANES : 3 * LANES] = rest[0:64] + pltpu.roll(rest[64:128], 64, 1)


def from_message(in_ref):
    first = jnp.concatenate([in_ref[:, 0:LANES], in_ref[:, LANES : 2 * LANES]], axis=0).T
    both = in_ref[:, 2 * LANES : 3 * LANES]
    rest = jnp.concatenate([both, pltpu.roll(both, 64, 1)], axis=0)
    return first, rest.T, rest


def send_kernel(p_ref, cam_ref, vis_ref, blk_ref, cnt_ref, rank_ref, out_ref, par, rec):
    me = lax.axis_index("space")
    load_params(p_ref, par)
    cam = jnp.broadcast_to(cam_ref[...], (8, 3))
    rows = jnp.concatenate(
        [jnp.broadcast_to(cam[0:1, i : i + 1], (1, LANES)) for i in range(3)]
        + [jnp.zeros((5, LANES), F32)],
        axis=0,
    )
    turn, basis = camera_values(rows)
    get = lambda index: dense_row(par, index)
    scales = [jnp.exp(get(3 + i)) for i in range(3)]
    quaternion, _ = unit([get(6 + i) for i in range(4)])
    spin = spin_of(quaternion)
    frame = [
        [
            (turn[r][0] * spin[0][c] + turn[r][1] * spin[1][c] + turn[r][2] * spin[2][c]) * scales[c]
            for c in range(3)
        ]
        for r in range(2)
    ]
    cov_xx = sum(frame[0][c] * frame[0][c] for c in range(3)) + DILATION
    cov_xy = sum(frame[0][c] * frame[1][c] for c in range(3))
    cov_yy = sum(frame[1][c] * frame[1][c] for c in range(3)) + DILATION
    inverse = 1.0 / (cov_xx * cov_yy - cov_xy * cov_xy)
    shift_x = get(0) - 256.0
    shift_y = get(1) - 512.0
    depth = get(2)
    rec[0:16, :] = turn[0][0] * shift_x + turn[0][1] * shift_y + turn[0][2] * depth + 256.0
    rec[16:32, :] = turn[1][0] * shift_x + turn[1][1] * shift_y + turn[1][2] * depth + 512.0
    rec[32:48, :] = cov_yy * inverse
    rec[48:64, :] = -cov_xy * inverse
    rec[64:80, :] = cov_xx * inverse
    rec[80:96, :] = sigmoid(get(10))
    for c in range(3):
        colour = jnp.full((16, LANES), 0.5, F32)
        for k in range(16):
            colour = colour + basis[k] * get(11 + 3 * k + c)
        rec[96 + 16 * c : 112 + 16 * c, :] = colour
    lists, order = slot_lists(vis_ref)
    low = lists & 127
    high = lists // LANES
    channels = []
    for ch in range(9):
        value = jnp.zeros((K, LANES), F32)
        for h in range(16):
            source = jnp.broadcast_to(rec[ch * 16 + h : ch * 16 + h + 1, :], (K, LANES))
            value = jnp.where(high == h, jnp.take_along_axis(source, low, axis=1), value)
        channels.append(value)
    blk = jnp.take_along_axis(jnp.broadcast_to(blk_ref[...], (8, LANES)), order[0:8], axis=1)
    counts = jnp.concatenate([cnt_ref[...], cnt_ref[...]], axis=1)
    ids = jnp.where(iota((8, LANES), 1) // 64 < counts, blk, -1).astype(F32)
    rank = jnp.sum(
        jnp.where(iota((1, 64), 1) == me, rank_ref[...], 0).astype(F32), axis=1, keepdims=True
    )
    meta = jnp.where(iota((8, LANES), 0) == 0, ids, jnp.broadcast_to(rank, (8, LANES)))
    to_message(out_ref, jnp.concatenate(channels + [meta], axis=0))


def shift_right(chunks, amount, lane):
    turned = [pltpu.roll(x, amount, 1) for x in chunks]
    return [
        jnp.where(lane < amount, turned[j - 1] if j else 0.0, turned[j]) for j in range(CHUNKS)
    ]


def shift_left(chunks, amount, lane):
    turned = [pltpu.roll(x, LANES - amount, 1) for x in chunks]
    return [
        jnp.where(lane >= LANES - amount, turned[j + 1] if j < CHUNKS - 1 else 0.0, turned[j])
        for j in range(CHUNKS)
    ]


def across(chunks):
    lane = iota(chunks[0].shape, 1)
    total = [TAPS[5] * x for x in chunks]
    for s in range(1, 6):
        right = shift_right(chunks, s, lane)
        left = shift_left(chunks, s, lane)
        total = [t + TAPS[5 + s] * (a + b) for t, a, b in zip(total, right, left)]
    return total


def down(load, start, count):
    total = TAPS[5] * load(start + 5, count)
    for s in range(1, 6):
        total = total + TAPS[5 + s] * (load(start + 5 - s, count) + load(start + 5 + s, count))
    return total


def fill_rows(ext, own, before, after, ch):
    for j in range(CHUNKS):
        cols = slice(j * LANES, (j + 1) * LANES)
        ext[j, 0:8, :] = jnp.zeros((8, LANES), F32)
        ext[j, 40:48, :] = jnp.zeros((8, LANES), F32)
        ext[j, 6:16, :] = before[ch, :, cols]
        ext[j, 16:32, :] = own[0, ch, :, cols]
        ext[j, 32:42, :] = after[ch, :, cols]


def target_kernel(own, before, after, vis_ref, ext_ref, mean_ref, square_ref, inv_ref, tmp, sq):
    def channel(ch, carry):
        fill_rows(tmp, own, before, after, ch)
        for j in range(CHUNKS):
            ext_ref[ch, j] = tmp[j]
            sq[j] = tmp[j] * tmp[j]
        for source, out in ((tmp, mean_ref), (sq, square_ref)):
            blurred = across(
                [down(lambda s, n: source[j, pl.ds(s, n), :], 6, 32) for j in range(CHUNKS)]
            )
            for j in range(CHUNKS):
                out[ch, j] = blurred[j]
        return carry

    lax.fori_loop(0, 3, channel, 0)
    lists, _ = slot_lists(vis_ref)
    low = lists & 127
    high = lists // LANES
    total = jnp.zeros((2 * 16, LANES), F32)
    lane = iota((1, LANES), 1)
    for k in range(K):
        here = row(high, k, 16) == iota((16, LANES), 0)
        value = jnp.concatenate(
            [
                jnp.where(here, float(k), 0.0),
                jnp.where(here, jnp.broadcast_to(lane, (16, LANES)).astype(F32), 0.0),
            ],
            axis=0,
        ).astype(BF16)
        table = (row(low, k, LANES) == iota((LANES, LANES), 0)).astype(F32).astype(BF16)
        total = total + lax.dot_general(
            value, table, (((1,), (1,)), ((), ())), preferred_element_type=F32
        )
    inv_ref[...] = total.astype(I32)


def pieces(x):
    first = x.astype(BF16)
    left = x - first.astype(F32)
    second = left.astype(BF16)
    third = (left - second.astype(F32)).astype(BF16)
    return first, second, third


def dot_mask(x, mask, contract):
    dims = (((1,), (contract,)), ((), ()))
    parts = [lax.dot_general(p, mask, dims, preferred_element_type=F32) for p in pieces(x)]
    return parts[0] + (parts[1] + parts[2])


def corners(ids, me):
    block = jnp.maximum(ids, 0.0).astype(I32)
    x = (block % 32 * 16).astype(F32) + 0.5
    y = (me * 16 + block // 32 * 8).astype(F32) + 0.5
    return x, y


def splat_terms(rec, k, x0, y_grid):
    get = lambda ch: jnp.broadcast_to(rec[pl.ds(ch * K + k, 1), :], (8, LANES))
    dy = y_grid - get(1)
    return x0 - get(0), dy, get(2) * -0.5, get(3) * dy, get(4) * -0.5 * dy * dy, get(5)


def blend_kernel(
    recv_ref,
    bg_ref,
    strip_ref,
    top_ref,
    bottom_ref,
    rec,
    colour_ref,
    before_ref,
    total_ref,
    nearer_ref,
    logs,
    blocks_ref,
):
    me = lax.axis_index("space")
    first, rest_rows, rest_cols = from_message(recv_ref)
    rec[0:LANES, :] = first
    rec[LANES:TABLE, :] = rest_rows[0:24]
    ids = row(rest_rows, 16, 8)
    corner_x, corner_y = corners(ids, me)
    y_grid = corner_y + iota((8, LANES), 0).astype(F32)

    def group(g, carry):
        base = corner_x + (g * GROUP).astype(F32)

        def four(kk, state):
            through, log_sum, colours = state
            part = [jnp.ones((8, LANES), F32)] * GROUP
            for k4 in range(4):
                k = kk * 4 + k4
                dx0, dy, ma, mb_y, mc_yy, opacity = splat_terms(rec, k, base, y_grid)
                tint = [jnp.broadcast_to(rec[pl.ds((6 + c) * K + k, 1), :], (8, LANES)) for c in range(3)]
                for i in range(GROUP):
                    dx = dx0 + float(i)
                    alpha = opacity * jnp.exp((ma * dx - mb_y) * dx + mc_yy)
                    weight = alpha * through[i]
                    keep = 1.0 - alpha
                    through = through[:i] + (through[i] * keep,) + through[i + 1 :]
                    part[i] = part[i] * keep
                    colours = (
                        colours[:i]
                        + (tuple(colours[i][c] + weight * tint[c] for c in range(3)),)
                        + colours[i + 1 :]
                    )
            log_sum = tuple(log_sum[i] + jnp.log(part[i]) for i in range(GROUP))
            return through, log_sum, colours

        zero = jnp.zeros((8, LANES), F32)
        _, log_sum, colours = lax.fori_loop(
            0,
            4,
            four,
            (
                (jnp.ones((8, LANES), F32),) * GROUP,
                (zero,) * GROUP,
                ((zero,) * 3,) * GROUP,
            ),
        )
        for i in range(GROUP):
            rows = pl.ds(pl.multiple_of((g * GROUP + i) * 8, 8), 8)
            logs[rows, :] = log_sum[i]
            for c in range(3):
                colour_ref[c, rows, :] = colours[i][c]
        return carry

    lax.fori_loop(0, 16 // GROUP, group, 0)
    id_row = row(rest_rows, 16, LANES)
    rank_row = row(rest_rows, 17, LANES)
    id_col = jnp.broadcast_to(rest_cols[:, 16:17], (LANES, LANES))
    rank_col = jnp.broadcast_to(rest_cols[:, 17:18], (LANES, LANES))
    live = id_row >= 0.0
    same = jnp.where((id_row == id_col) & live, 1.0, 0.0)
    nearer = jnp.where(rank_col < rank_row, same, 0.0).astype(BF16)
    member = jnp.where(id_col == iota((LANES, LANES), 1).astype(F32), 1.0, 0.0).astype(BF16)
    nearer_ref[...] = nearer
    log_all = logs[...]
    ahead = dot_mask(
        log_all, jnp.concatenate([nearer, same.astype(BF16), member], axis=1), 0
    )
    before = jnp.where(live, jnp.exp(ahead[:, 0:LANES]), 0.0)
    before_ref[...] = before
    total_ref[...] = jnp.where(live, jnp.exp(ahead[:, LANES : 2 * LANES]), 0.0)
    open_sky = jnp.exp(ahead[:, 2 * LANES : 3 * LANES])
    lane = iota((8, LANES), 1)
    for c in range(3):
        back = bg_ref[0:1, c : c + 1]
        blocks_ref[c] = dot_mask(before * colour_ref[c], member, 0) + back * open_sky
    for c in range(3):
        for br in range(2):
            for t in range(CHUNKS):
                index = br * 32 + 8 * t + lane // 16
                value = jnp.zeros((8, LANES), F32)
                for cc in range(16):
                    got = jnp.take_along_axis(blocks_ref[c, cc * 8 : cc * 8 + 8, :], index, axis=1)
                    value = jnp.where(lane % 16 == cc, got, value)
                strip_ref[0, c, br * 8 : br * 8 + 8, t * LANES : (t + 1) * LANES] = value
    top_ref[...] = strip_ref[0, :, 0:10, :]
    bottom_ref[...] = strip_ref[0, :, 6:16, :]


def loss_kernel(
    strip_ref,
    before_strip,
    after_strip,
    ext_ref,
    mean_ref,
    square_ref,
    bg_ref,
    rec,
    colour_ref,
    before_ref,
    total_ref,
    nearer_ref,
    out_ref,
    ext,
    prod,
    stat,
    grads,
    pulled,
    cot,
    log_cot,
    alphas,
    throughs,
    sums,
    table,
):
    me = lax.axis_index("space")
    t_row = iota((32, LANES), 0)
    where = me * 16 - 5 + t_row
    inside = jnp.where((where >= 0) & (where < 1024) & (t_row < 26), -0.2, 0.0)
    own = (t_row >= 5) & (t_row < 21)
    first_c, second_c = SSIM_FIRST, SSIM_SECOND

    def channel(ch, loss):
        fill_rows(ext, strip_ref, before_strip, after_strip, ch)
        for j in range(CHUNKS):
            a = ext[j]
            prod[0, j] = a * a
            prod[1, j] = a * ext_ref[ch, j]
        blurred = []
        for source in (ext, prod.at[0], prod.at[1]):
            blurred.append(
                across([down(lambda s, n: source[j, pl.ds(s, n), :], 6, 32) for j in range(CHUNKS)])
            )
        for j in range(CHUNKS):
            ma, mb = blurred[0][j], mean_ref[ch, j]
            mab = ma * mb
            squares = ma * ma + mb * mb
            n1 = 2.0 * mab + first_c
            n2 = 2.0 * (blurred[2][j] - mab) + second_c
            d1 = squares + first_c
            d2 = (blurred[1][j] + square_ref[ch, j]) - squares + second_c
            inverse = 1.0 / (d1 * d2)
            ssim = n1 * n2 * inverse
            loss = loss + jnp.where(own, 0.2 - 0.2 * ssim, 0.0)
            seed = inside * inverse
            g1 = seed * n2
            g2 = seed * n1
            scaled = inside * ssim
            gd1 = scaled * inverse * d2
            gd2 = scaled * inverse * d1
            stat[0, j] = 2.0 * (mb * (g1 - g2) + ma * (gd2 - gd1))
            stat[1, j] = -gd2
            stat[2, j] = 2.0 * g2
        spread = []
        for q in range(3):
            spread.append(
                across([down(lambda s, n: stat[q, j, pl.ds(s, n), :], 0, 16) for j in range(CHUNKS)])
            )
        for j in range(CHUNKS):
            a = ext[j, 16:32, :]
            b = ext_ref[ch, j, 16:32, :]
            differ = a - b
            root = jnp.sqrt(differ * differ + SMOOTHING)
            loss = loss + jnp.concatenate([0.8 * root, jnp.zeros((16, LANES), F32)], axis=0)
            grads[ch, j] = (
                spread[0][j] + 2.0 * a * spread[1][j] + b * spread[2][j] + 0.8 * differ / root
            )
        return loss

    loss = lax.fori_loop(0, 3, channel, jnp.zeros((32, LANES), F32))
    loss = jnp.sum(jnp.sum(loss, axis=0, keepdims=True), axis=1, keepdims=True)

    ids = row(rec[...], META, 8)
    live = ids >= 0.0
    block = jnp.maximum(ids, 0.0).astype(I32)
    place = block // 8
    start = block % 8 * 16
    for c in range(3):
        for cc in range(16):
            value = jnp.zeros((8, LANES), F32)
            for br in range(2):
                for t in range(CHUNKS):
                    got = jnp.take_along_axis(
                        grads[c, t, br * 8 : br * 8 + 8, :], start + cc, axis=1
                    )
                    value = jnp.where(place == br * 4 + t, got, value)
            pulled[c, cc * 8 : cc * 8 + 8, :] = jnp.where(live, value, 0.0)
    before = before_ref[...]
    behind = jnp.zeros((LANES, LANES), F32)
    sky = jnp.zeros((LANES, LANES), F32)
    for c in range(3):
        g = pulled[c]
        scaled = before * g
        cot[c] = scaled
        behind = behind + scaled * colour_ref[c]
        sky = sky + bg_ref[0:1, c : c + 1] * g
    log_cot[...] = dot_mask(behind, nearer_ref[...], 1) + total_ref[...] * sky

    corner_x, corner_y = corners(ids, me)
    y_grid = corner_y + iota((8, LANES), 0).astype(F32)

    def group(g, carry):
        base = corner_x + (g * GROUP).astype(F32)
        rows = [pl.ds(pl.multiple_of((g * GROUP + i) * 8, 8), 8) for i in range(GROUP)]
        through = [jnp.ones((8, LANES), F32)] * GROUP
        for k in range(K):
            dx0, dy, ma, mb_y, mc_yy, opacity = splat_terms(rec, k, base, y_grid)
            for i in range(GROUP):
                dx = dx0 + float(i)
                alpha = opacity * jnp.exp((ma * dx - mb_y) * dx + mc_yy)
                alphas[k, i] = alpha
                throughs[k, i] = through[i]
                through[i] = through[i] * (1.0 - alpha)

        suffix = tuple(log_cot[rows[i], :] for i in range(GROUP))
        pull = [[cot[c, rows[i], :] for c in range(3)] for i in range(GROUP)]
        zero = jnp.zeros((8, LANES), F32)

        def back(step, suffix):
            k = K - 1 - step
            get = lambda ch: jnp.broadcast_to(rec[pl.ds(ch * K + k, 1), :], (8, LANES))
            dx0 = base - get(0)
            tint = [get(6 + c) for c in range(3)]
            s0, s1, s2 = zero, zero, zero
            shade = [zero] * 3
            after = []
            for i in range(GROUP):
                dx = dx0 + float(i)
                alpha = alphas[k, i]
                seen = throughs[k, i]
                gain = seen * (
                    pull[i][0] * tint[0] + pull[i][1] * tint[1] + pull[i][2] * tint[2]
                )
                g_alpha = gain - suffix[i] / (1.0 - alpha)
                after.append(suffix[i] + alpha * gain)
                moment = alpha * g_alpha
                weight = alpha * seen
                shade = [shade[c] + weight * pull[i][c] for c in range(3)]
                moment_x = moment * dx
                s0 = s0 + moment
                s1 = s1 + moment_x
                s2 = s2 + moment_x * dx
            for n, value in enumerate([s0, s1, s2] + shade):
                sums[k, n] = jnp.where(g == 0, value, sums[k, n] + value)
            return tuple(after)

        lax.fori_loop(0, K, back, suffix)
        return carry

    lax.fori_loop(0, 16 // GROUP, group, 0)

    def finish(k, carry):
        get = lambda ch: rec[pl.ds(ch * K + k, 1), :]
        dy = y_grid - jnp.broadcast_to(get(1), (8, LANES))
        s0, s1, s2 = sums[k, 0], sums[k, 1], sums[k, 2]
        fold = lambda value: jnp.sum(value, axis=0, keepdims=True)
        s0_y = s0 * dy
        m0, mx, mxx = fold(s0), fold(s1), fold(s2)
        my, mxy, myy = fold(s0_y), fold(s1 * dy), fold(s0_y * dy)
        conic_a, conic_b, conic_c = get(2), get(3), get(4)
        out = [
            conic_a * mx + conic_b * my,
            conic_b * mx + conic_c * my,
            -0.5 * mxx,
            -mxy,
            -0.5 * myy,
            m0,
        ] + [fold(sums[k, 3 + c]) for c in range(3)]
        for ch in range(9):
            table[pl.ds(ch * K + k, 1), :] = out[ch]
        return carry

    lax.fori_loop(0, K, finish, 0)
    table[META:TABLE, :] = jnp.broadcast_to(loss, (8, LANES))
    to_message(out_ref, table[...])


def gather_kernel(recv_ref, inv_ref, cam_ref, out_ref, loss_ref, rec):
    first, rest_rows, rest_cols = from_message(recv_ref)
    rec[0:LANES, :] = first
    rec[LANES:META, :] = rest_rows[0:16]
    at_k = inv_ref[0:16, :]
    at_slot = inv_ref[16:32, :]
    for ch in range(9):
        value = jnp.zeros((16, LANES), F32)
        for k in range(K):
            source = jnp.broadcast_to(rec[ch * K + k : ch * K + k + 1, :], (16, LANES))
            value = jnp.where(at_k == k, jnp.take_along_axis(source, at_slot, axis=1), value)
        out_ref[ch * 16 : ch * 16 + 16, :] = value
    out_ref[META:TABLE, :] = jnp.concatenate(
        [jnp.broadcast_to(cam_ref[0:1, i : i + 1], (1, LANES)) for i in range(3)]
        + [jnp.zeros((5, LANES), F32)],
        axis=0,
    )
    total = jnp.sum(rest_cols[0:64, 16:17], axis=0, keepdims=True)
    loss_ref[...] = jnp.broadcast_to(total * (1.0 / 1572864.0), (1, LANES))


def pull_kernel(p_ref, rec0, rec1, rec2, rec3, out_ref, par, views, res):
    me = lax.axis_index("view")
    load_params(p_ref, par)
    for d, source in enumerate((rec0, rec1, rec2, rec3)):
        views[(me - d + 4) % 4] = source[...]
    get = lambda index: dense_row(par, index)
    scales = [jnp.exp(get(3 + i)) for i in range(3)]
    quaternion, inverse_norm = unit([get(6 + i) for i in range(4)])
    spin = spin_of(quaternion)
    zero = jnp.zeros((16, LANES), F32)
    g_pos = [zero] * 3
    g_frame_spin = [[zero] * 3 for _ in range(3)]
    g_log = [zero] * 3
    g_logit = zero
    g_colour = []
    bases = []
    for v in range(4):
        turn, basis = camera_values(views[v, META:TABLE, :])
        bases.append(basis)
        g = [views[v, ch * 16 : ch * 16 + 16, :] for ch in range(9)]
        unscaled = [
            [turn[r][0] * spin[0][c] + turn[r][1] * spin[1][c] + turn[r][2] * spin[2][c] for c in range(3)]
            for r in range(2)
        ]
        frame = [[unscaled[r][c] * scales[c] for c in range(3)] for r in range(2)]
        cov_xx = sum(frame[0][c] * frame[0][c] for c in range(3)) + DILATION
        cov_xy = sum(frame[0][c] * frame[1][c] for c in range(3))
        cov_yy = sum(frame[1][c] * frame[1][c] for c in range(3)) + DILATION
        inverse = 1.0 / (cov_xx * cov_yy - cov_xy * cov_xy)
        ca, cb, cc = cov_yy * inverse, -cov_xy * inverse, cov_xx * inverse
        ga, gb, gc = g[2], 0.5 * g[3], g[4]
        left = [
            [ca * ga + cb * gb, ca * gb + cb * gc],
            [cb * ga + cc * gb, cb * gb + cc * gc],
        ]
        g_xx = -(left[0][0] * ca + left[0][1] * cb)
        g_xy = -(left[0][0] * cb + left[0][1] * cc)
        g_yy = -(left[1][0] * cb + left[1][1] * cc)
        for c in range(3):
            gf0 = 2.0 * (g_xx * frame[0][c] + g_xy * frame[1][c])
            gf1 = 2.0 * (g_xy * frame[0][c] + g_yy * frame[1][c])
            g_log[c] = g_log[c] + gf0 * frame[0][c] + gf1 * frame[1][c]
            for m in range(3):
                g_frame_spin[m][c] = g_frame_spin[m][c] + (turn[0][m] * gf0 + turn[1][m] * gf1)
        for m in range(3):
            g_pos[m] = g_pos[m] + turn[0][m] * g[0] + turn[1][m] * g[1]
        g_logit = g_logit + g[5]
        g_colour.append(g[6:9])
    s = [[g_frame_spin[m][c] * scales[c] for c in range(3)] for m in range(3)]
    w, x, y, z = quaternion
    g_unit = [
        2.0 * (x * (s[2][1] - s[1][2]) + y * (s[0][2] - s[2][0]) + z * (s[1][0] - s[0][1])),
        2.0 * (y * (s[0][1] + s[1][0]) + z * (s[0][2] + s[2][0]) + w * (s[2][1] - s[1][2]))
        - 4.0 * x * (s[1][1] + s[2][2]),
        2.0 * (x * (s[0][1] + s[1][0]) + z * (s[1][2] + s[2][1]) + w * (s[0][2] - s[2][0]))
        - 4.0 * y * (s[0][0] + s[2][2]),
        2.0 * (x * (s[0][2] + s[2][0]) + y * (s[1][2] + s[2][1]) + w * (s[1][0] - s[0][1]))
        - 4.0 * z * (s[0][0] + s[1][1]),
    ]
    along = sum(q * g for q, g in zip(quaternion, g_unit))
    g_quat = [(g - q * along) * inverse_norm for q, g in zip(quaternion, g_unit)]
    rest = sigmoid(-get(10))
    rows = g_pos + g_log + g_quat + [g_logit * rest]
    for k in range(16):
        for c in range(3):
            total = bases[0][k] * g_colour[0][c]
            for v in range(1, 4):
                total = total + bases[v][k] * g_colour[v][c]
            rows.append(total)
    for index in range(59):
        res[index // 8, pl.ds(index % 8, 16, stride=8), :] = rows[index]
    for tile in range(8):
        count = min(8, 59 - tile * 8)
        for chunk in range(16):
            out_ref[tile * 8 : tile * 8 + count, chunk * LANES : (chunk + 1) * LANES] = res[
                tile, chunk * 8 : chunk * 8 + count, :
            ]


def call(kernel, outs, scratch=(), vmem=None):
    return pl.pallas_call(
        kernel,
        out_shape=[jax.ShapeDtypeStruct(shape, dtype) for shape, dtype in outs],
        scratch_shapes=[pltpu.VMEM(shape, dtype) for shape, dtype in scratch],
        compiler_params=pltpu.CompilerParams(vmem_limit_bytes=vmem or 16 << 20),
    )


def shards(params, visible, blocks, counts, depth_rank, camera, background, target):
    devices = lax.axis_size("space")
    views = lax.axis_size("view")
    up = [(i, i + 1) for i in range(devices - 1)]
    below = [(i + 1, i) for i in range(devices - 1)]
    tile = (LANES, LANES)

    goal_before = lax.ppermute(target[0, :, 6:16], "space", up)
    goal_after = lax.ppermute(target[0, :, 0:10], "space", below)
    (message,) = call(
        send_kernel,
        [((64, 384), F32)],
        [((8, LANES, LANES), F32), ((META, LANES), F32)],
    )(params, camera, visible, blocks, counts, depth_rank)
    received = lax.all_to_all(message, "space", 0, 0, tiled=True)
    goal, goal_mean, goal_square, inverse = call(
        target_kernel,
        [
            ((3, CHUNKS, 48, LANES), F32),
            ((3, CHUNKS, 32, LANES), F32),
            ((3, CHUNKS, 32, LANES), F32),
            ((32, LANES), I32),
        ],
        [((CHUNKS, 48, LANES), F32)] * 2,
    )(target, goal_before, goal_after, visible)
    strip, top, bottom, records, colours, before, total, nearer = call(
        blend_kernel,
        [
            ((1, 3, 16, 512), F32),
            ((3, 10, 512), F32),
            ((3, 10, 512), F32),
            ((TABLE, LANES), F32),
            ((3, *tile), F32),
            (tile, F32),
            (tile, F32),
            (tile, BF16),
        ],
        [(tile, F32), ((3, *tile), F32)],
    )(received, background)
    strip_before = lax.ppermute(bottom, "space", up)
    strip_after = lax.ppermute(top, "space", below)
    (reply,) = call(
        loss_kernel,
        [((64, 384), F32)],
        [
            ((CHUNKS, 48, LANES), F32),
            ((2, CHUNKS, 48, LANES), F32),
            ((3, CHUNKS, 32, LANES), F32),
            ((3, CHUNKS, 16, LANES), F32),
            ((3, *tile), F32),
            ((3, *tile), F32),
            (tile, F32),
            ((K, GROUP, 8, LANES), F32),
            ((K, GROUP, 8, LANES), F32),
            ((K, 6, 8, LANES), F32),
            ((TABLE, LANES), F32),
        ],
    )(
        strip,
        strip_before,
        strip_after,
        goal,
        goal_mean,
        goal_square,
        background,
        records,
        colours,
        before,
        total,
        nearer,
    )
    returned = lax.all_to_all(reply, "space", 0, 0, tiled=True)
    record_grads, loss = call(
        gather_kernel,
        [((TABLE, LANES), F32), ((1, LANES), F32)],
        [((META, LANES), F32)],
    )(returned, inverse, camera)
    others = [
        lax.ppermute(record_grads, "view", [(i, (i + d) % views) for i in range(views)])
        for d in range(1, views)
    ]
    (grad_params,) = call(
        pull_kernel,
        [((59, 2048), F32)],
        [((8, LANES, LANES), F32), ((4, TABLE, LANES), F32), ((8, LANES, LANES), F32)],
    )(params, record_grads, *others)
    return (grad_params, strip, loss[0, 0:1])


def solution(mesh):
    in_specs = (
        P(None, "space"),
        P("space", None, None),
        P("space", None),
        P("space", None),
        P("view", None),
        P("view", None),
        P("view", None),
        P("view", None, "space", None),
    )
    out_specs = (P(None, "space"), P("view", None, "space", None), P("view"))
    return jax.shard_map(shards, mesh=mesh, in_specs=in_specs, out_specs=out_specs, check_vma=False)
```

```python
import math

import jax
import jax.numpy as jnp
from jax import lax
from jax.experimental import pallas as pl
from jax.experimental.pallas import tpu as pltpu
from jax.sharding import PartitionSpec as P

F32 = jnp.float32
BF16 = jnp.bfloat16
I32 = jnp.int32

SH_ZERO = 0.28209479177387814
SH_ONE = 0.4886025119029199
SH_TWO = (
    1.0925484305920792,
    -1.0925484305920792,
    0.31539156525252005,
    -1.0925484305920792,
    0.5462742152960396,
)
SH_THREE = (
    -0.5900435899266435,
    2.890611442640554,
    -0.4570457994644658,
    0.3731763325901154,
    -0.4570457994644658,
    1.445305721320277,
    -0.5900435899266435,
)
DILATION = 0.3
SMOOTHING = 0.0001
SSIM_FIRST = 0.0001
SSIM_SECOND = 0.0009

K = 16
LANES = 128
CHUNKS = 4
GROUP = 4
META = 144
TABLE = 152


def taps():
    raw = [math.exp(-(offset - 5) * (offset - 5) / 4.5) for offset in range(11)]
    total = sum(raw)
    return [value / total for value in raw]


TAPS = taps()


def iota(shape, axis):
    return lax.broadcasted_iota(I32, shape, axis)


def row(x, index, rows):
    return jnp.broadcast_to(x[index : index + 1, :], (rows, x.shape[1]))


def turn_of(angles):
    cos_a, cos_b, cos_c = (jnp.cos(angle) for angle in angles)
    sin_a, sin_b, sin_c = (jnp.sin(angle) for angle in angles)
    return [
        [cos_c * cos_b, cos_c * sin_b * sin_a - sin_c * cos_a, cos_c * sin_b * cos_a + sin_c * sin_a],
        [sin_c * cos_b, sin_c * sin_b * sin_a + cos_c * cos_a, sin_c * sin_b * cos_a - cos_c * sin_a],
        [-sin_b, cos_b * sin_a, cos_b * cos_a],
    ]


def harmonics(axis):
    x, y, z = axis
    xx, yy, zz = (x * x, y * y, z * z)
    return [
        SH_ZERO * jnp.ones_like(x),
        -SH_ONE * y,
        SH_ONE * z,
        -SH_ONE * x,
        SH_TWO[0] * x * y,
        SH_TWO[1] * y * z,
        SH_TWO[2] * (2.0 * zz - xx - yy),
        SH_TWO[3] * x * z,
        SH_TWO[4] * (xx - yy),
        SH_THREE[0] * y * (3.0 * xx - yy),
        SH_THREE[1] * x * y * z,
        SH_THREE[2] * y * (4.0 * zz - xx - yy),
        SH_THREE[3] * z * (2.0 * zz - 3.0 * xx - 3.0 * yy),
        SH_THREE[4] * x * (4.0 * zz - xx - yy),
        SH_THREE[5] * z * (xx - yy),
        SH_THREE[6] * x * (xx - 3.0 * yy),
    ]


def camera_values(rows):
    angles = [jnp.broadcast_to(row, (8, LANES)) for row in rows]
    turn = turn_of(angles)
    basis = harmonics(turn[2])
    cell = lambda value: value[0:1, 0:1]
    return [[cell(value) for value in line] for line in turn], [cell(value) for value in basis]


def load_params(p_ref, scratch):
    for tile in range(8):
        count = min(8, 59 - tile * 8)
        for chunk in range(16):
            scratch[tile, chunk * 8 : chunk * 8 + count, :] = p_ref[
                tile * 8 : tile * 8 + count, chunk * LANES : (chunk + 1) * LANES
            ]


def dense_row(scratch, index):
    return scratch[index // 8, pl.ds(index % 8, 16, stride=8), :]


def spin_of(quaternion):
    w, x, y, z = quaternion
    return [
        [1.0 - 2.0 * (y * y + z * z), 2.0 * (x * y - w * z), 2.0 * (x * z + w * y)],
        [2.0 * (x * y + w * z), 1.0 - 2.0 * (x * x + z * z), 2.0 * (y * z - w * x)],
        [2.0 * (x * z - w * y), 2.0 * (y * z + w * x), 1.0 - 2.0 * (x * x + y * y)],
    ]


def sigmoid(x):
    return 1.0 / (1.0 + jnp.exp(-x))


def unit(quaternion):
    total = sum(part * part for part in quaternion)
    inverse = 1.0 / jnp.sqrt(total)
    return [part * inverse for part in quaternion], inverse


def slot_lists(vis_ref):
    natural = vis_ref[...]
    lane = iota((K, LANES), 1)
    order = (lane % 64) * 2 + lane // 64
    return jnp.take_along_axis(natural, order, axis=1), order


def to_message(out_ref, table):
    first = table[0:LANES, :].T
    rest = jnp.concatenate(
        [table[LANES:TABLE, :], jnp.zeros((2 * LANES - TABLE, LANES), F32)], axis=0
    ).T
    out_ref[:, 0, 0:LANES] = first[0:64]
    out_ref[:, 0, LANES : 2 * LANES] = first[64:128]
    out_ref[:, 0, 2 * LANES : 3 * LANES] = rest[0:64] + pltpu.roll(rest[64:128], 64, 1)


def from_message(in_ref):
    first = jnp.concatenate([in_ref[:, 0:LANES], in_ref[:, LANES : 2 * LANES]], axis=0).T
    both = in_ref[:, 2 * LANES : 3 * LANES]
    rest = jnp.concatenate([both, pltpu.roll(both, 64, 1)], axis=0)
    return first, rest.T, rest


def send_kernel(
    p_hbm,
    cam_hbm,
    vis_hbm,
    blk_hbm,
    cnt_hbm,
    rank_hbm,
    bg_hbm,
    out_ref,
    p_ref,
    cam_ref,
    vis_ref,
    blk_ref,
    cnt_ref,
    rank_ref,
    bg_ref,
    par,
    rec,
    sems,
):
    me = lax.axis_index("space")
    copies = [
        pltpu.make_async_copy(source, target, sems.at[i])
        for i, (source, target) in enumerate(
            (
                (p_hbm, p_ref),
                (cam_hbm, cam_ref),
                (vis_hbm, vis_ref),
                (blk_hbm, blk_ref),
                (cnt_hbm, cnt_ref),
                (rank_hbm, rank_ref),
                (bg_hbm, bg_ref),
            )
        )
    ]
    for copy in copies:
        copy.start()
    for copy in copies:
        copy.wait()
    load_params(p_ref, par)
    spread = lambda ref: [jnp.broadcast_to(ref[0:1, i : i + 1], (1, LANES)) for i in range(3)]
    angles = spread(cam_ref)
    turn, basis = camera_values(angles)
    get = lambda index: dense_row(par, index)
    scales = [jnp.exp(get(3 + i)) for i in range(3)]
    quaternion, _ = unit([get(6 + i) for i in range(4)])
    spin = spin_of(quaternion)
    frame = [
        [
            (turn[r][0] * spin[0][c] + turn[r][1] * spin[1][c] + turn[r][2] * spin[2][c]) * scales[c]
            for c in range(3)
        ]
        for r in range(2)
    ]
    cov_xx = sum(frame[0][c] * frame[0][c] for c in range(3)) + DILATION
    cov_xy = sum(frame[0][c] * frame[1][c] for c in range(3))
    cov_yy = sum(frame[1][c] * frame[1][c] for c in range(3)) + DILATION
    inverse = 1.0 / (cov_xx * cov_yy - cov_xy * cov_xy)
    shift_x = get(0) - 256.0
    shift_y = get(1) - 512.0
    depth = get(2)
    rec[0:16, :] = turn[0][0] * shift_x + turn[0][1] * shift_y + turn[0][2] * depth + 256.0
    rec[16:32, :] = turn[1][0] * shift_x + turn[1][1] * shift_y + turn[1][2] * depth + 512.0
    rec[32:48, :] = cov_yy * inverse
    rec[48:64, :] = -cov_xy * inverse
    rec[64:80, :] = cov_xx * inverse
    rec[80:96, :] = sigmoid(get(10))
    for c in range(3):
        colour = jnp.full((16, LANES), 0.5, F32)
        for k in range(16):
            colour = colour + basis[k] * get(11 + 3 * k + c)
        rec[96 + 16 * c : 112 + 16 * c, :] = colour
    lists, order = slot_lists(vis_ref)
    low = lists & 127
    high = lists // LANES
    channels = []
    for ch in range(9):
        value = jnp.zeros((K, LANES), F32)
        for h in range(16):
            source = jnp.broadcast_to(rec[ch * 16 + h : ch * 16 + h + 1, :], (K, LANES))
            value = jnp.where(high == h, jnp.take_along_axis(source, low, axis=1), value)
        channels.append(value)
    blk = jnp.take_along_axis(jnp.broadcast_to(blk_ref[...], (8, LANES)), order[0:8], axis=1)
    counts = jnp.concatenate([cnt_ref[...], cnt_ref[...]], axis=1)
    ids = jnp.where(iota((1, LANES), 1) // 64 < counts, blk[0:1], -1).astype(F32)
    rank = jnp.sum(
        jnp.where(iota((1, 64), 1) == me, rank_ref[...], 0).astype(F32), axis=1, keepdims=True
    )
    meta = [ids, jnp.broadcast_to(rank, (1, LANES))] + spread(bg_ref) + angles
    to_message(out_ref, jnp.concatenate(channels + meta, axis=0))


def across(chunks):
    lane = iota(chunks[0].shape, 1)
    total = [TAPS[5] * x for x in chunks]
    for s in range(1, 6):
        right = [pltpu.roll(x, s, 1) for x in chunks]
        left = [pltpu.roll(x, LANES - s, 1) for x in chunks]
        low, high = lane < s, lane >= LANES - s
        before = [0.0] + right[:-1]
        after = left[1:] + [0.0]
        total = [
            t + TAPS[5 + s] * (jnp.where(low, b, r) + jnp.where(high, a, f))
            for t, b, r, f, a in zip(total, before, right, left, after)
        ]
    return total


def blur(source, start, count=8):
    chunks = []
    for j in range(CHUNKS):
        load = lambda first: source[j, first : first + count, :]
        total = TAPS[5] * load(start + 5)
        for s in range(1, 6):
            total = total + TAPS[5 + s] * (load(start + 5 - s) + load(start + 5 + s))
        chunks.append(total)
    return across(chunks)


def fill_rows(ext, own, chip, next_chip, ch, even):
    for j in range(CHUNKS):
        cols = slice(j * LANES, (j + 1) * LANES)
        ext[j, 0:8, :] = jnp.zeros((8, LANES), F32)
        ext[j, 40:48, :] = jnp.zeros((8, LANES), F32)
        near, far = chip[ch, :, cols], next_chip[ch, :, cols]
        ext[j, 6:16, :] = jnp.where(even, far, near)
        ext[j, 16:32, :] = own[0, ch, :, cols]
        ext[j, 32:42, :] = jnp.where(even, near, far)


def target_kernel(own, chip, next_chip, vis_ref, ext_ref, mean_ref, square_ref, inv_ref, tmp, sq):
    even = lax.axis_index("space") % 2 == 0

    def channel(ch, carry):
        fill_rows(tmp, own, chip, next_chip, ch, even)
        for j in range(CHUNKS):
            ext_ref[ch, j] = tmp[j]
            sq[j] = tmp[j] * tmp[j]
        for source, out in ((tmp, mean_ref), (sq, square_ref)):
            for top in range(0, 32, 8):
                blurred = blur(source, 6 + top)
                for j in range(CHUNKS):
                    out[ch, j, top : top + 8, :] = blurred[j]
        return carry

    lax.fori_loop(0, 3, channel, 0)
    lists, _ = slot_lists(vis_ref)
    low = lists & 127
    high = lists // LANES
    total = jnp.zeros((2 * 16, LANES), F32)
    lane = iota((1, LANES), 1)
    for k in range(K):
        here = row(high, k, 16) == iota((16, LANES), 0)
        value = jnp.concatenate(
            [
                jnp.where(here, float(k), 0.0),
                jnp.where(here, jnp.broadcast_to(lane, (16, LANES)).astype(F32), 0.0),
            ],
            axis=0,
        ).astype(BF16)
        table = (row(low, k, LANES) == iota((LANES, LANES), 0)).astype(F32).astype(BF16)
        total = total + lax.dot_general(
            value, table, (((1,), (1,)), ((), ())), preferred_element_type=F32
        )
    inv_ref[...] = total.astype(I32)


def pieces(x):
    first = x.astype(BF16)
    left = x - first.astype(F32)
    second = left.astype(BF16)
    third = (left - second.astype(F32)).astype(BF16)
    return first, second, third


def dot_mask(x, mask, contract):
    dims = (((1,), (contract,)), ((), ()))
    parts = [lax.dot_general(p, mask, dims, preferred_element_type=F32) for p in pieces(x)]
    return parts[0] + (parts[1] + parts[2])


def corners(ids, me):
    block = jnp.maximum(ids, 0.0).astype(I32)
    x = (block % 32 * 16).astype(F32) + 0.5
    y = (me * 16 + block // 32 * 8).astype(F32) + 0.5
    return x, y


def splat_terms(rec, k, x0, y_grid):
    get = lambda ch: jnp.broadcast_to(rec[pl.ds(ch * K + k, 1), :], (8, LANES))
    dy = y_grid - get(1)
    return x0 - get(0), dy, get(2) * -0.5, get(3) * dy, get(4) * -0.5 * dy * dy, get(5)


def blend_kernel(
    recv_ref,
    strip_ref,
    chip_ref,
    next_ref,
    rec,
    colour_ref,
    before_ref,
    total_ref,
    nearer_ref,
    through_ref,
    alphas,
    weights,
    logs,
    blocks_ref,
):
    me = lax.axis_index("space")
    first, rest_rows, rest_cols = from_message(recv_ref)
    rec[0:LANES, :] = first
    rec[LANES:TABLE, :] = rest_rows[0:24]
    ids = row(rest_rows, 16, 8)
    corner_x, corner_y = corners(ids, me)
    y_grid = corner_y + iota((8, LANES), 0).astype(F32)

    def group(g, carry):
        base = corner_x + (g * GROUP).astype(F32)

        def four(kk, state):
            through, log_sum, colours = state
            part = [jnp.ones((8, LANES), F32)] * GROUP
            for k4 in range(4):
                k = kk * 4 + k4
                dx0, dy, ma, mb_y, mc_yy, opacity = splat_terms(rec, k, base, y_grid)
                tint = [jnp.broadcast_to(rec[pl.ds((6 + c) * K + k, 1), :], (8, LANES)) for c in range(3)]
                for i in range(GROUP):
                    dx = dx0 + float(i)
                    alpha = opacity * jnp.exp((ma * dx - mb_y) * dx + mc_yy)
                    weight = alpha * through[i]
                    alphas[k, g * GROUP + i] = alpha
                    weights[k, g * GROUP + i] = weight
                    keep = 1.0 - alpha
                    through = through[:i] + (through[i] * keep,) + through[i + 1 :]
                    part[i] = part[i] * keep
                    colours = (
                        colours[:i]
                        + (tuple(colours[i][c] + weight * tint[c] for c in range(3)),)
                        + colours[i + 1 :]
                    )
            log_sum = tuple(log_sum[i] + jnp.log(part[i]) for i in range(GROUP))
            return through, log_sum, colours

        zero = jnp.zeros((8, LANES), F32)
        through, log_sum, colours = lax.fori_loop(
            0,
            4,
            four,
            (
                (jnp.ones((8, LANES), F32),) * GROUP,
                (zero,) * GROUP,
                ((zero,) * 3,) * GROUP,
            ),
        )
        for i in range(GROUP):
            rows = pl.ds(pl.multiple_of((g * GROUP + i) * 8, 8), 8)
            logs[rows, :] = log_sum[i]
            through_ref[rows, :] = through[i]
            for c in range(3):
                colour_ref[c, rows, :] = colours[i][c]
        return carry

    lax.fori_loop(0, 16 // GROUP, group, 0)
    id_row = row(rest_rows, 16, LANES)
    rank_row = row(rest_rows, 17, LANES)
    id_col = jnp.broadcast_to(rest_cols[:, 16:17], (LANES, LANES))
    rank_col = jnp.broadcast_to(rest_cols[:, 17:18], (LANES, LANES))
    live = id_row >= 0.0
    same = jnp.where((id_row == id_col) & live, 1.0, 0.0)
    nearer = jnp.where(rank_col < rank_row, same, 0.0).astype(BF16)
    member = jnp.where(id_col == (iota((LANES, LANES), 1) % 64).astype(F32), 1.0, 0.0).astype(BF16)
    nearer_ref[...] = nearer
    log_all = logs[...]
    ahead = dot_mask(
        log_all, jnp.concatenate([nearer, same.astype(BF16), member], axis=1), 0
    )
    before = jnp.where(live, jnp.exp(ahead[:, 0:LANES]), 0.0)
    before_ref[...] = before
    total_ref[...] = jnp.where(live, jnp.exp(ahead[:, LANES : 2 * LANES]), 0.0)
    open_sky = jnp.exp(ahead[:, 2 * LANES : 3 * LANES])
    lane = iota((8, LANES), 1)
    for c in range(3):
        blocks_ref[c] = dot_mask(before * colour_ref[c], member, 0) + rest_rows[18 + c : 19 + c] * open_sky
    pair = lane % 16 // 2
    for c in range(3):
        for p in range(8):
            blocks_ref[c, p * 16 : p * 16 + 8, :] = jnp.where(
                lane < 64,
                blocks_ref[c, p * 16 : p * 16 + 8, :],
                blocks_ref[c, p * 16 + 8 : p * 16 + 16, :],
            )
    for br in range(2):
        for t in range(CHUNKS):
            index = lane % 2 * 64 + (br * 32 + 8 * t) + lane // 16
            values = [None] * 3
            for p in range(8):
                for c in range(3):
                    got = jnp.take_along_axis(
                        blocks_ref[c, p * 16 : p * 16 + 8, :], index, axis=1
                    )
                    values[c] = jnp.where(pair == p, got, values[c]) if p else got
            for c in range(3):
                strip_ref[0, c, br * 8 : br * 8 + 8, t * LANES : (t + 1) * LANES] = values[c]
    even = me % 2 == 0
    top = strip_ref[0, :, 0:10, :]
    bottom = strip_ref[0, :, 6:16, :]
    chip_ref[...] = jnp.where(even, bottom, top)
    next_ref[...] = jnp.where(even, top, bottom)


def loss_kernel(
    strip_ref,
    chip,
    next_chip,
    ext_ref,
    mean_ref,
    square_ref,
    rec,
    colour_ref,
    before_ref,
    total_ref,
    nearer_ref,
    through_ref,
    alphas,
    weights,
    out_ref,
    ext,
    prod,
    stat,
    grads,
    spread_grads,
    pulled,
    cot,
    behind_cot,
    sums,
    table,
):
    me = lax.axis_index("space")
    first_c, second_c = SSIM_FIRST, SSIM_SECOND
    even = me % 2 == 0

    def channel(ch, loss):
        fill_rows(ext, strip_ref, chip, next_chip, ch, even)
        for j in range(CHUNKS):
            a = ext[j]
            prod[0, j] = a * a
            prod[1, j] = a * ext_ref[ch, j]
        for top in range(0, 32, 8):
            t_row = iota((8, LANES), 0) + top
            where = me * 16 - 5 + t_row
            inside = jnp.where((where >= 0) & (where < 1024) & (t_row < 26), -0.2, 0.0)
            own = (t_row >= 5) & (t_row < 21)
            blurred = [blur(source, 6 + top) for source in (ext, prod.at[0], prod.at[1])]
            rows = slice(top, top + 8)
            for j in range(CHUNKS):
                ma, mb = blurred[0][j], mean_ref[ch, j, rows, :]
                mab = ma * mb
                squares = ma * ma + mb * mb
                n1 = 2.0 * mab + first_c
                n2 = 2.0 * (blurred[2][j] - mab) + second_c
                d1 = squares + first_c
                d2 = (blurred[1][j] + square_ref[ch, j, rows, :]) - squares + second_c
                inverse = 1.0 / (d1 * d2)
                ssim = n1 * n2 * inverse
                loss = loss + jnp.where(own, 0.2 - 0.2 * ssim, 0.0)
                seed = inside * inverse
                g1 = seed * n2
                g2 = seed * n1
                scaled = seed * ssim
                gd1 = scaled * d2
                gd2 = scaled * d1
                stat[0, j, rows, :] = 2.0 * (mb * (g1 - g2) + ma * (gd2 - gd1))
                stat[1, j, rows, :] = -gd2
                stat[2, j, rows, :] = 2.0 * g2
        for top in (0, 8):
            spread = [blur(stat.at[q], top) for q in range(3)]
            rows = slice(16 + top, 24 + top)
            for j in range(CHUNKS):
                a = ext[j, rows, :]
                b = ext_ref[ch, j, rows, :]
                differ = a - b
                root = jnp.sqrt(differ * differ + SMOOTHING)
                loss = loss + 0.8 * root
                grads[ch, j, top : top + 8, :] = (
                    spread[0][j] + 2.0 * a * spread[1][j] + b * spread[2][j] + 0.8 * differ / root
                )
        return loss

    loss = jnp.zeros((8, LANES), F32)
    for ch in range(3):
        loss = channel(ch, loss)
    loss = jnp.sum(jnp.sum(loss, axis=0, keepdims=True), axis=1, keepdims=True)

    ids = row(rec[...], META, 8)
    live = ids >= 0.0
    block = jnp.maximum(ids, 0.0).astype(I32)
    lane = iota((8, LANES), 1)
    place = lane % 64 // 8
    for p in range(8):
        start = lane % 8 * 16 + 2 * p + lane // 64
        both = [None] * 3
        for n in range(8):
            br, t = divmod(n, CHUNKS)
            for c in range(3):
                got = jnp.take_along_axis(grads[c, t, br * 8 : br * 8 + 8, :], start, axis=1)
                both[c] = jnp.where(place == n, got, both[c]) if n else got
        for c in range(3):
            spread_grads[c, p] = both[c]
    for odd in range(2):
        index = block + 64 * odd
        for p in range(8):
            for c in range(3):
                value = jnp.take_along_axis(spread_grads[c, p], index, axis=1)
                first = (2 * p + odd) * 8
                pulled[c, first : first + 8, :] = jnp.where(live, value, 0.0)
    before = before_ref[...]
    behind = jnp.zeros((LANES, LANES), F32)
    sky = jnp.zeros((LANES, LANES), F32)
    for c in range(3):
        g = pulled[c]
        scaled = before * g
        cot[c] = scaled
        behind = behind + scaled * colour_ref[c]
        sky = sky + rec[META + 2 + c : META + 3 + c, :] * g
    log_cot = dot_mask(behind, nearer_ref[...], 1) + total_ref[...] * sky
    left = through_ref[...]
    some = left > 0.0
    behind_cot[...] = jnp.where(some, log_cot / jnp.where(some, left, 1.0), 0.0)

    corner_x, corner_y = corners(ids, me)
    y_grid = corner_y + iota((8, LANES), 0).astype(F32)

    def group(g, carry):
        base = corner_x + (g * GROUP).astype(F32)
        rows = [pl.ds(pl.multiple_of((g * GROUP + i) * 8, 8), 8) for i in range(GROUP)]
        suffix = tuple(behind_cot[rows[i], :] for i in range(GROUP))
        pull = [[cot[c, rows[i], :] for c in range(3)] for i in range(GROUP)]
        zero = jnp.zeros((8, LANES), F32)

        def back(step, suffix):
            k = K - 1 - step
            get = lambda ch: jnp.broadcast_to(rec[pl.ds(ch * K + k, 1), :], (8, LANES))
            dx0 = base - get(0)
            tint = [get(6 + c) for c in range(3)]
            s0, s1, s2 = zero, zero, zero
            shade = [zero] * 3
            after = []
            for i in range(GROUP):
                dx = dx0 + float(i)
                weight = weights[k, g * GROUP + i]
                gain = (
                    pull[i][0] * tint[0] + pull[i][1] * tint[1] + pull[i][2] * tint[2] - suffix[i]
                )
                after.append(suffix[i] + alphas[k, g * GROUP + i] * gain)
                moment = weight * gain
                shade = [shade[c] + weight * pull[i][c] for c in range(3)]
                moment_x = moment * dx
                s0 = s0 + moment
                s1 = s1 + moment_x
                s2 = s2 + moment_x * dx
            for n, value in enumerate([s0, s1, s2] + shade):
                sums[k, n] = jnp.where(g == 0, value, sums[k, n] + value)
            return tuple(after)

        lax.fori_loop(0, K, back, suffix)
        return carry

    lax.fori_loop(0, 16 // GROUP, group, 0)

    def finish(k, carry):
        get = lambda ch: rec[pl.ds(ch * K + k, 1), :]
        dy = y_grid - jnp.broadcast_to(get(1), (8, LANES))
        s0, s1, s2 = sums[k, 0], sums[k, 1], sums[k, 2]
        fold = lambda value: jnp.sum(value, axis=0, keepdims=True)
        s0_y = s0 * dy
        m0, mx, mxx = fold(s0), fold(s1), fold(s2)
        my, mxy, myy = fold(s0_y), fold(s1 * dy), fold(s0_y * dy)
        conic_a, conic_b, conic_c = get(2), get(3), get(4)
        out = [
            conic_a * mx + conic_b * my,
            conic_b * mx + conic_c * my,
            -0.5 * mxx,
            -mxy,
            -0.5 * myy,
            m0,
        ] + [fold(sums[k, 3 + c]) for c in range(3)]
        for ch in range(9):
            table[pl.ds(ch * K + k, 1), :] = out[ch]
        return carry

    lax.fori_loop(0, K, finish, 0)
    table[META:TABLE, :] = jnp.concatenate(
        [jnp.broadcast_to(loss, (5, LANES)), rec[META + 5 : TABLE, :]], axis=0
    )
    to_message(out_ref, table[...])


def gather_kernel(recv_ref, inv_ref, out_ref, loss_ref, rec):
    first, rest_rows, rest_cols = from_message(recv_ref)
    rec[0:LANES, :] = first
    rec[LANES:META, :] = rest_rows[0:16]
    at_k = inv_ref[0:16, :]
    at_slot = inv_ref[16:32, :]
    for ch in range(9):
        value = jnp.zeros((16, LANES), F32)
        for k in range(K):
            source = jnp.broadcast_to(rec[ch * K + k : ch * K + k + 1, :], (16, LANES))
            value = jnp.where(at_k == k, jnp.take_along_axis(source, at_slot, axis=1), value)
        out_ref[ch * 16 : ch * 16 + 16, :] = value
    out_ref[META:TABLE, :] = rest_rows[16:24]
    total = jnp.sum(rest_cols[0:64, 16:17], axis=0, keepdims=True)
    loss_ref[...] = jnp.broadcast_to(total * (1.0 / 1572864.0), (1, LANES))


def pull_kernel(p_ref, rec0, rec1, rec2, rec3, out_ref, par, views, res):
    me = lax.axis_index("view")
    load_params(p_ref, par)
    for d, source in enumerate((rec0, rec1, rec2, rec3)):
        views[(me - d + 4) % 4] = source[...]
    get = lambda index: dense_row(par, index)
    scales = [jnp.exp(get(3 + i)) for i in range(3)]
    quaternion, inverse_norm = unit([get(6 + i) for i in range(4)])
    spin = spin_of(quaternion)
    zero = jnp.zeros((16, LANES), F32)
    g_pos = [zero] * 3
    g_frame_spin = [[zero] * 3 for _ in range(3)]
    g_log = [zero] * 3
    g_logit = zero
    g_colour = []
    bases = []
    for v in range(4):
        turn, basis = camera_values([views[v, META + 5 + i : META + 6 + i, :] for i in range(3)])
        bases.append(basis)
        g = [views[v, ch * 16 : ch * 16 + 16, :] for ch in range(9)]
        unscaled = [
            [turn[r][0] * spin[0][c] + turn[r][1] * spin[1][c] + turn[r][2] * spin[2][c] for c in range(3)]
            for r in range(2)
        ]
        frame = [[unscaled[r][c] * scales[c] for c in range(3)] for r in range(2)]
        cov_xx = sum(frame[0][c] * frame[0][c] for c in range(3)) + DILATION
        cov_xy = sum(frame[0][c] * frame[1][c] for c in range(3))
        cov_yy = sum(frame[1][c] * frame[1][c] for c in range(3)) + DILATION
        inverse = 1.0 / (cov_xx * cov_yy - cov_xy * cov_xy)
        ca, cb, cc = cov_yy * inverse, -cov_xy * inverse, cov_xx * inverse
        ga, gb, gc = g[2], 0.5 * g[3], g[4]
        left = [
            [ca * ga + cb * gb, ca * gb + cb * gc],
            [cb * ga + cc * gb, cb * gb + cc * gc],
        ]
        g_xx = -(left[0][0] * ca + left[0][1] * cb)
        g_xy = -(left[0][0] * cb + left[0][1] * cc)
        g_yy = -(left[1][0] * cb + left[1][1] * cc)
        for c in range(3):
            gf0 = 2.0 * (g_xx * frame[0][c] + g_xy * frame[1][c])
            gf1 = 2.0 * (g_xy * frame[0][c] + g_yy * frame[1][c])
            g_log[c] = g_log[c] + gf0 * frame[0][c] + gf1 * frame[1][c]
            for m in range(3):
                g_frame_spin[m][c] = g_frame_spin[m][c] + (turn[0][m] * gf0 + turn[1][m] * gf1)
        for m in range(3):
            g_pos[m] = g_pos[m] + turn[0][m] * g[0] + turn[1][m] * g[1]
        g_logit = g_logit + g[5]
        g_colour.append(g[6:9])
    s = [[g_frame_spin[m][c] * scales[c] for c in range(3)] for m in range(3)]
    w, x, y, z = quaternion
    g_unit = [
        2.0 * (x * (s[2][1] - s[1][2]) + y * (s[0][2] - s[2][0]) + z * (s[1][0] - s[0][1])),
        2.0 * (y * (s[0][1] + s[1][0]) + z * (s[0][2] + s[2][0]) + w * (s[2][1] - s[1][2]))
        - 4.0 * x * (s[1][1] + s[2][2]),
        2.0 * (x * (s[0][1] + s[1][0]) + z * (s[1][2] + s[2][1]) + w * (s[0][2] - s[2][0]))
        - 4.0 * y * (s[0][0] + s[2][2]),
        2.0 * (x * (s[0][2] + s[2][0]) + y * (s[1][2] + s[2][1]) + w * (s[1][0] - s[0][1]))
        - 4.0 * z * (s[0][0] + s[1][1]),
    ]
    along = sum(q * g for q, g in zip(quaternion, g_unit))
    g_quat = [(g - q * along) * inverse_norm for q, g in zip(quaternion, g_unit)]
    rest = sigmoid(-get(10))
    rows = g_pos + g_log + g_quat + [g_logit * rest]
    for k in range(16):
        for c in range(3):
            total = bases[0][k] * g_colour[0][c]
            for v in range(1, 4):
                total = total + bases[v][k] * g_colour[v][c]
            rows.append(total)
    for index in range(59):
        res[index // 8, pl.ds(index % 8, 16, stride=8), :] = rows[index]
    for tile in range(8):
        count = min(8, 59 - tile * 8)
        for chunk in range(16):
            out_ref[tile * 8 : tile * 8 + count, chunk * LANES : (chunk + 1) * LANES] = res[
                tile, chunk * 8 : chunk * 8 + count, :
            ]


def call(kernel, outs, scratch=(), copied=0):
    extra = {"in_specs": [pl.BlockSpec(memory_space=pltpu.HBM)] * copied} if copied else {}
    sems = [pltpu.SemaphoreType.DMA((copied,))] if copied else []
    return pl.pallas_call(
        kernel,
        out_shape=[jax.ShapeDtypeStruct(shape, dtype) for shape, dtype in outs],
        scratch_shapes=[pltpu.VMEM(shape, dtype) for shape, dtype in scratch] + sems,
        compiler_params=pltpu.CompilerParams(vmem_limit_bytes=(60 if copied else 16) << 20),
        **extra,
    )


def shards(params, visible, blocks, counts, depth_rank, camera, background, target):
    devices = lax.axis_size("space")
    views = lax.axis_size("view")
    chip = [(i, i ^ 1) for i in range(devices)]
    next_chip = [(i, i + 1 if i % 2 else i - 1) for i in range(1, devices - 1)]
    even = lax.axis_index("space") % 2 == 0
    tile = (LANES, LANES)
    kept = ((K, 16, 8, LANES), F32)
    lists = visible[0].T

    goal_top, goal_bottom = target[0, :, 0:10], target[0, :, 6:16]
    goal_chip = lax.ppermute(jnp.where(even, goal_bottom, goal_top), "space", chip)
    goal_next = lax.ppermute(jnp.where(even, goal_top, goal_bottom), "space", next_chip)
    (message,) = call(
        send_kernel,
        [((64, 1, 384), F32)],
        [
            (params.shape, F32),
            ((1, 3), F32),
            ((K, LANES), I32),
            ((1, LANES), I32),
            ((1, 64), I32),
            ((1, 64), I32),
            ((1, 3), F32),
            ((8, LANES, LANES), F32),
            ((META, LANES), F32),
        ],
        copied=7,
    )(params, camera, lists, blocks, counts, depth_rank, background)
    received = lax.all_to_all(message, "space", 0, 0, tiled=True).reshape(64, 384)
    goal, goal_mean, goal_square, inverse = call(
        target_kernel,
        [
            ((3, CHUNKS, 48, LANES), F32),
            ((3, CHUNKS, 32, LANES), F32),
            ((3, CHUNKS, 32, LANES), F32),
            ((32, LANES), I32),
        ],
        [((CHUNKS, 48, LANES), F32)] * 2,
    )(target, goal_chip, goal_next, lists)
    strip, to_chip, to_next, records, colours, before, total, nearer, through, alphas, weights = call(
        blend_kernel,
        [
            ((1, 3, 16, 512), F32),
            ((3, 10, 512), F32),
            ((3, 10, 512), F32),
            ((TABLE, LANES), F32),
            ((3, *tile), F32),
            (tile, F32),
            (tile, F32),
            (tile, BF16),
            (tile, F32),
            kept,
            kept,
        ],
        [(tile, F32), ((3, *tile), F32)],
    )(received)
    strip_chip = lax.ppermute(to_chip, "space", chip)
    strip_next = lax.ppermute(to_next, "space", next_chip)
    (reply,) = call(
        loss_kernel,
        [((64, 1, 384), F32)],
        [
            ((CHUNKS, 48, LANES), F32),
            ((2, CHUNKS, 48, LANES), F32),
            ((3, CHUNKS, 32, LANES), F32),
            ((3, CHUNKS, 16, LANES), F32),
            ((3, 8, 8, LANES), F32),
            ((3, *tile), F32),
            ((3, *tile), F32),
            (tile, F32),
            ((K, 6, 8, LANES), F32),
            ((TABLE, LANES), F32),
        ],
    )(
        strip,
        strip_chip,
        strip_next,
        goal,
        goal_mean,
        goal_square,
        records,
        colours,
        before,
        total,
        nearer,
        through,
        alphas,
        weights,
    )
    returned = lax.all_to_all(reply, "space", 0, 0, tiled=True).reshape(64, 384)
    record_grads, loss = call(
        gather_kernel,
        [((TABLE, LANES), F32), ((1, LANES), F32)],
        [((META, LANES), F32)],
    )(returned, inverse)
    others = [
        lax.ppermute(record_grads, "view", [(i, (i + d) % views) for i in range(views)])
        for d in range(1, views)
    ]
    (grad_params,) = call(
        pull_kernel,
        [((59, 2048), F32)],
        [((8, LANES, LANES), F32), ((4, TABLE, LANES), F32), ((8, LANES, LANES), F32)],
    )(params, record_grads, *others)
    return (grad_params, strip, loss[0, 0:1])


def solution(mesh):
    in_specs = (
        P(None, "space"),
        P("space", None, None),
        P("space", None),
        P("space", None),
        P("view", None),
        P("view", None),
        P("view", None),
        P("view", None, "space", None),
    )
    out_specs = (P(None, "space"), P("view", None, "space", None), P("view"))
    return jax.shard_map(shards, mesh=mesh, in_specs=in_specs, out_specs=out_specs, check_vma=False)
```

```python
import math

import jax
import jax.numpy as jnp
from jax import lax
from jax.experimental import pallas as pl
from jax.experimental.pallas import tpu as pltpu
from jax.sharding import PartitionSpec as P

F32 = jnp.float32
BF16 = jnp.bfloat16
I32 = jnp.int32

SH_ZERO = 0.28209479177387814
SH_ONE = 0.4886025119029199
SH_TWO = (
    1.0925484305920792,
    -1.0925484305920792,
    0.31539156525252005,
    -1.0925484305920792,
    0.5462742152960396,
)
SH_THREE = (
    -0.5900435899266435,
    2.890611442640554,
    -0.4570457994644658,
    0.3731763325901154,
    -0.4570457994644658,
    1.445305721320277,
    -0.5900435899266435,
)
DILATION = 0.3
SMOOTHING = 0.0001
SSIM_FIRST = 0.0001
SSIM_SECOND = 0.0009

K = 16
LANES = 128
CHUNKS = 4
GROUP = 4
META = 144
TABLE = 152


def taps():
    raw = [math.exp(-(offset - 5) * (offset - 5) / 4.5) for offset in range(11)]
    total = sum(raw)
    return [value / total for value in raw]


TAPS = taps()


def iota(shape, axis):
    return lax.broadcasted_iota(I32, shape, axis)


def row(x, index, rows):
    return jnp.broadcast_to(x[index : index + 1, :], (rows, x.shape[1]))


def turn_of(angles):
    cos_a, cos_b, cos_c = (jnp.cos(angle) for angle in angles)
    sin_a, sin_b, sin_c = (jnp.sin(angle) for angle in angles)
    return [
        [cos_c * cos_b, cos_c * sin_b * sin_a - sin_c * cos_a, cos_c * sin_b * cos_a + sin_c * sin_a],
        [sin_c * cos_b, sin_c * sin_b * sin_a + cos_c * cos_a, sin_c * sin_b * cos_a - cos_c * sin_a],
        [-sin_b, cos_b * sin_a, cos_b * cos_a],
    ]


def harmonics(axis):
    x, y, z = axis
    xx, yy, zz = (x * x, y * y, z * z)
    return [
        SH_ZERO * jnp.ones_like(x),
        -SH_ONE * y,
        SH_ONE * z,
        -SH_ONE * x,
        SH_TWO[0] * x * y,
        SH_TWO[1] * y * z,
        SH_TWO[2] * (2.0 * zz - xx - yy),
        SH_TWO[3] * x * z,
        SH_TWO[4] * (xx - yy),
        SH_THREE[0] * y * (3.0 * xx - yy),
        SH_THREE[1] * x * y * z,
        SH_THREE[2] * y * (4.0 * zz - xx - yy),
        SH_THREE[3] * z * (2.0 * zz - 3.0 * xx - 3.0 * yy),
        SH_THREE[4] * x * (4.0 * zz - xx - yy),
        SH_THREE[5] * z * (xx - yy),
        SH_THREE[6] * x * (xx - 3.0 * yy),
    ]


def camera_values(rows):
    angles = [jnp.broadcast_to(row, (8, LANES)) for row in rows]
    turn = turn_of(angles)
    basis = harmonics(turn[2])
    cell = lambda value: value[0:1, 0:1]
    return [[cell(value) for value in line] for line in turn], [cell(value) for value in basis]


def load_params(p_ref, scratch):
    for tile in range(8):
        count = min(8, 59 - tile * 8)
        for chunk in range(16):
            scratch[tile, chunk * 8 : chunk * 8 + count, :] = p_ref[
                tile * 8 : tile * 8 + count, chunk * LANES : (chunk + 1) * LANES
            ]


def dense_row(scratch, index):
    return scratch[index // 8, pl.ds(index % 8, 16, stride=8), :]


def spin_of(quaternion):
    w, x, y, z = quaternion
    return [
        [1.0 - 2.0 * (y * y + z * z), 2.0 * (x * y - w * z), 2.0 * (x * z + w * y)],
        [2.0 * (x * y + w * z), 1.0 - 2.0 * (x * x + z * z), 2.0 * (y * z - w * x)],
        [2.0 * (x * z - w * y), 2.0 * (y * z + w * x), 1.0 - 2.0 * (x * x + y * y)],
    ]


def sigmoid(x):
    return 1.0 / (1.0 + jnp.exp(-x))


def unit(quaternion):
    total = sum(part * part for part in quaternion)
    inverse = 1.0 / jnp.sqrt(total)
    return [part * inverse for part in quaternion], inverse


def slot_lists(vis_ref):
    natural = vis_ref[...]
    lane = iota((K, LANES), 1)
    order = (lane % 64) * 2 + lane // 64
    return jnp.take_along_axis(natural, order, axis=1), order


def to_message(out_ref, table, twice=False):
    first = table[0:LANES, :].T
    rest = jnp.concatenate(
        [table[LANES:TABLE, :], jnp.zeros((2 * LANES - TABLE, LANES), F32)], axis=0
    ).T
    parts = [first[0:64], first[64:128], rest[0:64] + pltpu.roll(rest[64:128], 64, 1)]
    if twice:
        even = iota((64, LANES), 0) % 2 == 0
        parts += [jnp.where(even, pltpu.roll(x, 1, 0), pltpu.roll(x, 63, 0)) for x in parts]
    for i, part in enumerate(parts):
        out_ref[:, 0, i * LANES : (i + 1) * LANES] = part


def from_message(in_ref, start=0):
    part = lambda i: in_ref[:, (start + i) * LANES : (start + i + 1) * LANES]
    first = jnp.concatenate([part(0), part(1)], axis=0).T
    both = part(2)
    rest = jnp.concatenate([both, pltpu.roll(both, 64, 1)], axis=0)
    return first, rest.T, rest


def send_kernel(
    p_hbm,
    cam_hbm,
    vis_hbm,
    blk_hbm,
    cnt_hbm,
    rank_hbm,
    bg_hbm,
    out_ref,
    p_ref,
    cam_ref,
    vis_ref,
    blk_ref,
    cnt_ref,
    rank_ref,
    bg_ref,
    par,
    rec,
    sems,
):
    me = lax.axis_index("space")
    copies = [
        pltpu.make_async_copy(source, target, sems.at[i])
        for i, (source, target) in enumerate(
            (
                (p_hbm, p_ref),
                (cam_hbm, cam_ref),
                (vis_hbm, vis_ref),
                (blk_hbm, blk_ref),
                (cnt_hbm, cnt_ref),
                (rank_hbm, rank_ref),
                (bg_hbm, bg_ref),
            )
        )
    ]
    for copy in copies:
        copy.start()
    for copy in copies:
        copy.wait()
    load_params(p_ref, par)
    spread = lambda ref: [jnp.broadcast_to(ref[0:1, i : i + 1], (1, LANES)) for i in range(3)]
    angles = spread(cam_ref)
    turn, basis = camera_values(angles)
    get = lambda index: dense_row(par, index)
    scales = [jnp.exp(get(3 + i)) for i in range(3)]
    quaternion, _ = unit([get(6 + i) for i in range(4)])
    spin = spin_of(quaternion)
    frame = [
        [
            (turn[r][0] * spin[0][c] + turn[r][1] * spin[1][c] + turn[r][2] * spin[2][c]) * scales[c]
            for c in range(3)
        ]
        for r in range(2)
    ]
    cov_xx = sum(frame[0][c] * frame[0][c] for c in range(3)) + DILATION
    cov_xy = sum(frame[0][c] * frame[1][c] for c in range(3))
    cov_yy = sum(frame[1][c] * frame[1][c] for c in range(3)) + DILATION
    inverse = 1.0 / (cov_xx * cov_yy - cov_xy * cov_xy)
    shift_x = get(0) - 256.0
    shift_y = get(1) - 512.0
    depth = get(2)
    rec[0:16, :] = turn[0][0] * shift_x + turn[0][1] * shift_y + turn[0][2] * depth + 256.0
    rec[16:32, :] = turn[1][0] * shift_x + turn[1][1] * shift_y + turn[1][2] * depth + 512.0
    rec[32:48, :] = cov_yy * inverse
    rec[48:64, :] = -cov_xy * inverse
    rec[64:80, :] = cov_xx * inverse
    rec[80:96, :] = sigmoid(get(10))
    for c in range(3):
        colour = jnp.full((16, LANES), 0.5, F32)
        for k in range(16):
            colour = colour + basis[k] * get(11 + 3 * k + c)
        rec[96 + 16 * c : 112 + 16 * c, :] = colour
    lists, order = slot_lists(vis_ref)
    low = lists & 127
    high = lists // LANES
    channels = []
    for ch in range(9):
        value = jnp.zeros((K, LANES), F32)
        for h in range(16):
            source = jnp.broadcast_to(rec[ch * 16 + h : ch * 16 + h + 1, :], (K, LANES))
            value = jnp.where(high == h, jnp.take_along_axis(source, low, axis=1), value)
        channels.append(value)
    blk = jnp.take_along_axis(jnp.broadcast_to(blk_ref[...], (8, LANES)), order[0:8], axis=1)
    counts = jnp.concatenate([cnt_ref[...], cnt_ref[...]], axis=1)
    ids = jnp.where(iota((1, LANES), 1) // 64 < counts, blk[0:1], -1).astype(F32)
    rank = jnp.sum(
        jnp.where(iota((1, 64), 1) == me, rank_ref[...], 0).astype(F32), axis=1, keepdims=True
    )
    meta = [ids, jnp.broadcast_to(rank, (1, LANES))] + spread(bg_ref) + angles
    to_message(out_ref, jnp.concatenate(channels + meta, axis=0), twice=True)


def across(chunks):
    lane = iota(chunks[0].shape, 1)
    total = [TAPS[5] * x for x in chunks]
    for s in range(1, 6):
        right = [pltpu.roll(x, s, 1) for x in chunks]
        left = [pltpu.roll(x, LANES - s, 1) for x in chunks]
        low, high = lane < s, lane >= LANES - s
        before = [0.0] + right[:-1]
        after = left[1:] + [0.0]
        total = [
            t + TAPS[5 + s] * (jnp.where(low, b, r) + jnp.where(high, a, f))
            for t, b, r, f, a in zip(total, before, right, left, after)
        ]
    return total


def blur(source, start, count=8):
    chunks = []
    for j in range(CHUNKS):
        load = lambda first: source[j, first : first + count, :]
        total = TAPS[5] * load(start + 5)
        for s in range(1, 6):
            total = total + TAPS[5 + s] * (load(start + 5 - s) + load(start + 5 + s))
        chunks.append(total)
    return across(chunks)


def fill_rows(ext, own, chip, next_chip, ch, even):
    for j in range(CHUNKS):
        cols = slice(j * LANES, (j + 1) * LANES)
        ext[j, 0:8, :] = jnp.zeros((8, LANES), F32)
        ext[j, 40:48, :] = jnp.zeros((8, LANES), F32)
        near, far = chip[ch, :, cols], next_chip[ch, :, cols]
        ext[j, 6:16, :] = jnp.where(even, far, near)
        ext[j, 16:32, :] = own[ch, :, cols]
        ext[j, 32:42, :] = jnp.where(even, near, far)


def target_kernel(own, chip, next_chip, vis_ref, ext_ref, mean_ref, square_ref, inv_ref, tmp, sq):
    even = lax.axis_index("space") % 2 == 0

    def channel(ch, carry):
        fill_rows(tmp, own.at[0], chip, next_chip, ch, even)
        for j in range(CHUNKS):
            ext_ref[ch, j] = tmp[j]
            sq[j] = tmp[j] * tmp[j]
        for source, out in ((tmp, mean_ref), (sq, square_ref)):
            for top in range(0, 32, 8):
                blurred = blur(source, 6 + top)
                for j in range(CHUNKS):
                    out[ch, j, top : top + 8, :] = blurred[j]
        return carry

    lax.fori_loop(0, 3, channel, 0)
    lists, _ = slot_lists(vis_ref)
    low = lists & 127
    high = lists // LANES
    total = jnp.zeros((2 * 16, LANES), F32)
    lane = iota((1, LANES), 1)
    for k in range(K):
        here = row(high, k, 16) == iota((16, LANES), 0)
        value = jnp.concatenate(
            [
                jnp.where(here, float(k), 0.0),
                jnp.where(here, jnp.broadcast_to(lane, (16, LANES)).astype(F32), 0.0),
            ],
            axis=0,
        ).astype(BF16)
        table = (row(low, k, LANES) == iota((LANES, LANES), 0)).astype(F32).astype(BF16)
        total = total + lax.dot_general(
            value, table, (((1,), (1,)), ((), ())), preferred_element_type=F32
        )
    inv_ref[...] = total.astype(I32)


def pieces(x):
    first = x.astype(BF16)
    left = x - first.astype(F32)
    second = left.astype(BF16)
    third = (left - second.astype(F32)).astype(BF16)
    return first, second, third


def dot_mask(x, mask, contract):
    dims = (((1,), (contract,)), ((), ()))
    parts = [lax.dot_general(p, mask, dims, preferred_element_type=F32) for p in pieces(x)]
    return parts[0] + (parts[1] + parts[2])


def corners(ids, me):
    block = jnp.maximum(ids, 0.0).astype(I32)
    x = (block % 32 * 16).astype(F32) + 0.5
    y = (me * 16 + block // 32 * 8).astype(F32) + 0.5
    return x, y


def splat_terms(rec, k, x0, y_grid):
    get = lambda ch: jnp.broadcast_to(rec[pl.ds(ch * K + k, 1), :], (8, LANES))
    dy = y_grid - get(1)
    return x0 - get(0), dy, get(2) * -0.5, get(3) * dy, get(4) * -0.5 * dy * dy, get(5)


def render(rec, corner_x, y_grid, logs, colours_out, keep=None):
    def group(g, carry):
        base = corner_x + (g * GROUP).astype(F32)

        def four(kk, state):
            through, log_sum, colours = state
            part = [jnp.ones((8, LANES), F32)] * GROUP
            for k4 in range(4):
                k = kk * 4 + k4
                dx0, dy, ma, mb_y, mc_yy, opacity = splat_terms(rec, k, base, y_grid)
                tint = [
                    jnp.broadcast_to(rec[pl.ds((6 + c) * K + k, 1), :], (8, LANES))
                    for c in range(3)
                ]
                for i in range(GROUP):
                    dx = dx0 + float(i)
                    alpha = opacity * jnp.exp((ma * dx - mb_y) * dx + mc_yy)
                    weight = alpha * through[i]
                    if keep:
                        keep[0][k, g * GROUP + i] = alpha
                        keep[1][k, g * GROUP + i] = weight
                    left = 1.0 - alpha
                    through = through[:i] + (through[i] * left,) + through[i + 1 :]
                    part[i] = part[i] * left
                    colours = (
                        colours[:i]
                        + (tuple(colours[i][c] + weight * tint[c] for c in range(3)),)
                        + colours[i + 1 :]
                    )
            log_sum = tuple(log_sum[i] + jnp.log(part[i]) for i in range(GROUP))
            return through, log_sum, colours

        zero = jnp.zeros((8, LANES), F32)
        start = ((jnp.ones((8, LANES), F32),) * GROUP, (zero,) * GROUP, ((zero,) * 3,) * GROUP)
        through, log_sum, colours = lax.fori_loop(0, 4, four, start)
        for i in range(GROUP):
            rows = pl.ds(pl.multiple_of((g * GROUP + i) * 8, 8), 8)
            logs[rows, :] = log_sum[i]
            if keep:
                keep[2][rows, :] = through[i]
            for c in range(3):
                colours_out[c, rows, :] = colours[i][c]
        return carry

    lax.fori_loop(0, 16 // GROUP, group, 0)


def masks(rest_rows, rest_cols):
    id_row = row(rest_rows, 16, LANES)
    rank_row = row(rest_rows, 17, LANES)
    id_col = jnp.broadcast_to(rest_cols[:, 16:17], (LANES, LANES))
    rank_col = jnp.broadcast_to(rest_cols[:, 17:18], (LANES, LANES))
    live = id_row >= 0.0
    same = jnp.where((id_row == id_col) & live, 1.0, 0.0)
    nearer = jnp.where(rank_col < rank_row, same, 0.0).astype(BF16)
    block = (iota((LANES, LANES), 1) % 64).astype(F32)
    member = jnp.where(id_col == block, 1.0, 0.0).astype(BF16)
    return live, same.astype(BF16), nearer, member


def to_rows(before, open_sky, colours, member, sky_rows, blocks_ref, strip_ref):
    lane = iota((8, LANES), 1)
    for c in range(3):
        blocks_ref[c] = (
            dot_mask(before * colours[c], member, 0) + sky_rows[18 + c : 19 + c] * open_sky
        )
    pair = lane % 16 // 2
    for c in range(3):
        for p in range(8):
            blocks_ref[c, p * 16 : p * 16 + 8, :] = jnp.where(
                lane < 64,
                blocks_ref[c, p * 16 : p * 16 + 8, :],
                blocks_ref[c, p * 16 + 8 : p * 16 + 16, :],
            )
    for br in range(2):
        for t in range(CHUNKS):
            index = lane % 2 * 64 + (br * 32 + 8 * t) + lane // 16
            values = [None] * 3
            for p in range(8):
                for c in range(3):
                    got = jnp.take_along_axis(
                        blocks_ref[c, p * 16 : p * 16 + 8, :], index, axis=1
                    )
                    values[c] = jnp.where(pair == p, got, values[c]) if p else got
            for c in range(3):
                strip_ref[c, br * 8 : br * 8 + 8, t * LANES : (t + 1) * LANES] = values[c]


def blend_kernel(
    recv_ref,
    strip_ref,
    chip_ref,
    far_ref,
    rec,
    colour_ref,
    before_ref,
    total_ref,
    nearer_ref,
    through_ref,
    alphas,
    weights,
    logs,
    blocks_ref,
    far_rec,
    far_colour,
    far_strip,
):
    me = lax.axis_index("space")
    even = me % 2 == 0
    row_of = iota((8, LANES), 0).astype(F32)

    first, rest_rows, rest_cols = from_message(recv_ref)
    rec[0:LANES, :] = first
    rec[LANES:TABLE, :] = rest_rows[0:24]
    corner_x, corner_y = corners(row(rest_rows, 16, 8), me)
    render(rec, corner_x, corner_y + row_of, logs, colour_ref, (alphas, weights, through_ref))
    live, same, nearer, member = masks(rest_rows, rest_cols)
    nearer_ref[...] = nearer
    ahead = dot_mask(logs[...], jnp.concatenate([nearer, same, member], axis=1), 0)
    before = jnp.where(live, jnp.exp(ahead[:, 0:LANES]), 0.0)
    before_ref[...] = before
    total_ref[...] = jnp.where(live, jnp.exp(ahead[:, LANES : 2 * LANES]), 0.0)
    to_rows(
        before, jnp.exp(ahead[:, 2 * LANES :]), colour_ref, member, rest_rows, blocks_ref, strip_ref
    )
    chip_ref[...] = jnp.where(even, strip_ref[:, 6:16, :], strip_ref[:, 0:10, :])

    first, rest_rows, rest_cols = from_message(recv_ref, 3)
    far_rec[0:LANES, :] = first
    far_rec[LANES:TABLE, :] = rest_rows[0:24]
    corner_x, corner_y = corners(row(rest_rows, 16, 8), jnp.where(even, me - 1, me + 1))
    render(far_rec, corner_x, corner_y + row_of, logs, far_colour)
    live, _, nearer, member = masks(rest_rows, rest_cols)
    ahead = dot_mask(logs[...], jnp.concatenate([nearer, member], axis=1), 0)
    before = jnp.where(live, jnp.exp(ahead[:, 0:LANES]), 0.0)
    to_rows(
        before, jnp.exp(ahead[:, LANES:]), far_colour, member, rest_rows, blocks_ref, far_strip
    )
    near_edge = jnp.where(even, far_strip[:, 6:16, :], far_strip[:, 0:10, :])
    far_ref[...] = jnp.where((me > 0) & (me < 63), near_edge, 0.0)


def loss_kernel(
    strip_ref,
    chip,
    next_chip,
    ext_ref,
    mean_ref,
    square_ref,
    rec,
    colour_ref,
    before_ref,
    total_ref,
    nearer_ref,
    through_ref,
    alphas,
    weights,
    out_ref,
    rendered_ref,
    ext,
    prod,
    stat,
    grads,
    spread_grads,
    pulled,
    cot,
    behind_cot,
    sums,
    table,
    sems,
):
    copy = pltpu.make_async_copy(strip_ref, rendered_ref, sems.at[0])
    copy.start()
    me = lax.axis_index("space")
    first_c, second_c = SSIM_FIRST, SSIM_SECOND
    even = me % 2 == 0

    def channel(ch, loss):
        fill_rows(ext, strip_ref, chip, next_chip, ch, even)
        for j in range(CHUNKS):
            a = ext[j]
            prod[0, j] = a * a
            prod[1, j] = a * ext_ref[ch, j]
        for top in range(0, 32, 8):
            t_row = iota((8, LANES), 0) + top
            where = me * 16 - 5 + t_row
            inside = jnp.where((where >= 0) & (where < 1024) & (t_row < 26), -0.2, 0.0)
            own = (t_row >= 5) & (t_row < 21)
            blurred = [blur(source, 6 + top) for source in (ext, prod.at[0], prod.at[1])]
            rows = slice(top, top + 8)
            for j in range(CHUNKS):
                ma, mb = blurred[0][j], mean_ref[ch, j, rows, :]
                mab = ma * mb
                squares = ma * ma + mb * mb
                n1 = 2.0 * mab + first_c
                n2 = 2.0 * (blurred[2][j] - mab) + second_c
                d1 = squares + first_c
                d2 = (blurred[1][j] + square_ref[ch, j, rows, :]) - squares + second_c
                inverse = 1.0 / (d1 * d2)
                ssim = n1 * n2 * inverse
                loss = loss + jnp.where(own, 0.2 - 0.2 * ssim, 0.0)
                seed = inside * inverse
                g1 = seed * n2
                g2 = seed * n1
                scaled = seed * ssim
                gd1 = scaled * d2
                gd2 = scaled * d1
                stat[0, j, rows, :] = 2.0 * (mb * (g1 - g2) + ma * (gd2 - gd1))
                stat[1, j, rows, :] = -gd2
                stat[2, j, rows, :] = 2.0 * g2
        for top in (0, 8):
            spread = [blur(stat.at[q], top) for q in range(3)]
            rows = slice(16 + top, 24 + top)
            for j in range(CHUNKS):
                a = ext[j, rows, :]
                b = ext_ref[ch, j, rows, :]
                differ = a - b
                root = jnp.sqrt(differ * differ + SMOOTHING)
                loss = loss + 0.8 * root
                grads[ch, j, top : top + 8, :] = (
                    spread[0][j] + 2.0 * a * spread[1][j] + b * spread[2][j] + 0.8 * differ / root
                )
        return loss

    loss = jnp.zeros((8, LANES), F32)
    for ch in range(3):
        loss = channel(ch, loss)
    loss = jnp.sum(jnp.sum(loss, axis=0, keepdims=True), axis=1, keepdims=True)

    ids = row(rec[...], META, 8)
    live = ids >= 0.0
    block = jnp.maximum(ids, 0.0).astype(I32)
    lane = iota((8, LANES), 1)
    place = lane % 64 // 8
    for p in range(8):
        start = lane % 8 * 16 + 2 * p + lane // 64
        both = [None] * 3
        for n in range(8):
            br, t = divmod(n, CHUNKS)
            for c in range(3):
                got = jnp.take_along_axis(grads[c, t, br * 8 : br * 8 + 8, :], start, axis=1)
                both[c] = jnp.where(place == n, got, both[c]) if n else got
        for c in range(3):
            spread_grads[c, p] = both[c]
    for odd in range(2):
        index = block + 64 * odd
        for p in range(8):
            for c in range(3):
                value = jnp.take_along_axis(spread_grads[c, p], index, axis=1)
                first = (2 * p + odd) * 8
                pulled[c, first : first + 8, :] = jnp.where(live, value, 0.0)
    before = before_ref[...]
    behind = jnp.zeros((LANES, LANES), F32)
    sky = jnp.zeros((LANES, LANES), F32)
    for c in range(3):
        g = pulled[c]
        scaled = before * g
        cot[c] = scaled
        behind = behind + scaled * colour_ref[c]
        sky = sky + rec[META + 2 + c : META + 3 + c, :] * g
    log_cot = dot_mask(behind, nearer_ref[...], 1) + total_ref[...] * sky
    left = through_ref[...]
    some = left > 0.0
    behind_cot[...] = jnp.where(some, log_cot / jnp.where(some, left, 1.0), 0.0)

    corner_x, corner_y = corners(ids, me)
    y_grid = corner_y + iota((8, LANES), 0).astype(F32)

    def group(g, carry):
        base = corner_x + (g * GROUP).astype(F32)
        rows = [pl.ds(pl.multiple_of((g * GROUP + i) * 8, 8), 8) for i in range(GROUP)]
        suffix = tuple(behind_cot[rows[i], :] for i in range(GROUP))
        pull = [[cot[c, rows[i], :] for c in range(3)] for i in range(GROUP)]
        zero = jnp.zeros((8, LANES), F32)

        def back(step, suffix):
            k = K - 1 - step
            get = lambda ch: jnp.broadcast_to(rec[pl.ds(ch * K + k, 1), :], (8, LANES))
            dx0 = base - get(0)
            tint = [get(6 + c) for c in range(3)]
            s0, s1, s2 = zero, zero, zero
            shade = [zero] * 3
            after = []
            for i in range(GROUP):
                dx = dx0 + float(i)
                weight = weights[k, g * GROUP + i]
                gain = (
                    pull[i][0] * tint[0] + pull[i][1] * tint[1] + pull[i][2] * tint[2] - suffix[i]
                )
                after.append(suffix[i] + alphas[k, g * GROUP + i] * gain)
                moment = weight * gain
                shade = [shade[c] + weight * pull[i][c] for c in range(3)]
                moment_x = moment * dx
                s0 = s0 + moment
                s1 = s1 + moment_x
                s2 = s2 + moment_x * dx
            for n, value in enumerate([s0, s1, s2] + shade):
                sums[k, n] = jnp.where(g == 0, value, sums[k, n] + value)
            return tuple(after)

        lax.fori_loop(0, K, back, suffix)
        return carry

    lax.fori_loop(0, 16 // GROUP, group, 0)

    def finish(k, carry):
        get = lambda ch: rec[pl.ds(ch * K + k, 1), :]
        dy = y_grid - jnp.broadcast_to(get(1), (8, LANES))
        s0, s1, s2 = sums[k, 0], sums[k, 1], sums[k, 2]
        fold = lambda value: jnp.sum(value, axis=0, keepdims=True)
        s0_y = s0 * dy
        m0, mx, mxx = fold(s0), fold(s1), fold(s2)
        my, mxy, myy = fold(s0_y), fold(s1 * dy), fold(s0_y * dy)
        conic_a, conic_b, conic_c = get(2), get(3), get(4)
        out = [
            conic_a * mx + conic_b * my,
            conic_b * mx + conic_c * my,
            -0.5 * mxx,
            -mxy,
            -0.5 * myy,
            m0,
        ] + [fold(sums[k, 3 + c]) for c in range(3)]
        for ch in range(9):
            table[pl.ds(ch * K + k, 1), :] = out[ch]
        return carry

    lax.fori_loop(0, K, finish, 0)
    table[META:TABLE, :] = jnp.concatenate(
        [jnp.broadcast_to(loss, (5, LANES)), rec[META + 5 : TABLE, :]], axis=0
    )
    to_message(out_ref, table[...])
    copy.wait()


def gather_kernel(recv_ref, inv_ref, out_ref, loss_ref, rec):
    first, rest_rows, rest_cols = from_message(recv_ref)
    rec[0:LANES, :] = first
    rec[LANES:META, :] = rest_rows[0:16]
    at_k = inv_ref[0:16, :]
    at_slot = inv_ref[16:32, :]
    for ch in range(9):
        value = jnp.zeros((16, LANES), F32)
        for k in range(K):
            source = jnp.broadcast_to(rec[ch * K + k : ch * K + k + 1, :], (16, LANES))
            value = jnp.where(at_k == k, jnp.take_along_axis(source, at_slot, axis=1), value)
        out_ref[ch * 16 : ch * 16 + 16, :] = value
    out_ref[META:TABLE, :] = rest_rows[16:24]
    total = jnp.sum(rest_cols[0:64, 16:17], axis=0, keepdims=True)
    loss_ref[...] = jnp.broadcast_to(total * (1.0 / 1572864.0), (1, LANES))


def pull_kernel(p_ref, rec0, rec1, rec2, rec3, out_ref, par, views, res):
    me = lax.axis_index("view")
    load_params(p_ref, par)
    for d, source in enumerate((rec0, rec1, rec2, rec3)):
        views[(me - d + 4) % 4] = source[...]
    get = lambda index: dense_row(par, index)
    scales = [jnp.exp(get(3 + i)) for i in range(3)]
    quaternion, inverse_norm = unit([get(6 + i) for i in range(4)])
    spin = spin_of(quaternion)
    zero = jnp.zeros((16, LANES), F32)
    g_pos = [zero] * 3
    g_frame_spin = [[zero] * 3 for _ in range(3)]
    g_log = [zero] * 3
    g_logit = zero
    g_colour = []
    bases = []
    for v in range(4):
        turn, basis = camera_values([views[v, META + 5 + i : META + 6 + i, :] for i in range(3)])
        bases.append(basis)
        g = [views[v, ch * 16 : ch * 16 + 16, :] for ch in range(9)]
        unscaled = [
            [turn[r][0] * spin[0][c] + turn[r][1] * spin[1][c] + turn[r][2] * spin[2][c] for c in range(3)]
            for r in range(2)
        ]
        frame = [[unscaled[r][c] * scales[c] for c in range(3)] for r in range(2)]
        cov_xx = sum(frame[0][c] * frame[0][c] for c in range(3)) + DILATION
        cov_xy = sum(frame[0][c] * frame[1][c] for c in range(3))
        cov_yy = sum(frame[1][c] * frame[1][c] for c in range(3)) + DILATION
        inverse = 1.0 / (cov_xx * cov_yy - cov_xy * cov_xy)
        ca, cb, cc = cov_yy * inverse, -cov_xy * inverse, cov_xx * inverse
        ga, gb, gc = g[2], 0.5 * g[3], g[4]
        left = [
            [ca * ga + cb * gb, ca * gb + cb * gc],
            [cb * ga + cc * gb, cb * gb + cc * gc],
        ]
        g_xx = -(left[0][0] * ca + left[0][1] * cb)
        g_xy = -(left[0][0] * cb + left[0][1] * cc)
        g_yy = -(left[1][0] * cb + left[1][1] * cc)
        for c in range(3):
            gf0 = 2.0 * (g_xx * frame[0][c] + g_xy * frame[1][c])
            gf1 = 2.0 * (g_xy * frame[0][c] + g_yy * frame[1][c])
            g_log[c] = g_log[c] + gf0 * frame[0][c] + gf1 * frame[1][c]
            for m in range(3):
                g_frame_spin[m][c] = g_frame_spin[m][c] + (turn[0][m] * gf0 + turn[1][m] * gf1)
        for m in range(3):
            g_pos[m] = g_pos[m] + turn[0][m] * g[0] + turn[1][m] * g[1]
        g_logit = g_logit + g[5]
        g_colour.append(g[6:9])
    s = [[g_frame_spin[m][c] * scales[c] for c in range(3)] for m in range(3)]
    w, x, y, z = quaternion
    g_unit = [
        2.0 * (x * (s[2][1] - s[1][2]) + y * (s[0][2] - s[2][0]) + z * (s[1][0] - s[0][1])),
        2.0 * (y * (s[0][1] + s[1][0]) + z * (s[0][2] + s[2][0]) + w * (s[2][1] - s[1][2]))
        - 4.0 * x * (s[1][1] + s[2][2]),
        2.0 * (x * (s[0][1] + s[1][0]) + z * (s[1][2] + s[2][1]) + w * (s[0][2] - s[2][0]))
        - 4.0 * y * (s[0][0] + s[2][2]),
        2.0 * (x * (s[0][2] + s[2][0]) + y * (s[1][2] + s[2][1]) + w * (s[1][0] - s[0][1]))
        - 4.0 * z * (s[0][0] + s[1][1]),
    ]
    along = sum(q * g for q, g in zip(quaternion, g_unit))
    g_quat = [(g - q * along) * inverse_norm for q, g in zip(quaternion, g_unit)]
    rest = sigmoid(-get(10))
    rows = g_pos + g_log + g_quat + [g_logit * rest]
    for k in range(16):
        for c in range(3):
            total = bases[0][k] * g_colour[0][c]
            for v in range(1, 4):
                total = total + bases[v][k] * g_colour[v][c]
            rows.append(total)
    for index in range(59):
        res[index // 8, pl.ds(index % 8, 16, stride=8), :] = rows[index]
    for tile in range(8):
        count = min(8, 59 - tile * 8)
        for chunk in range(16):
            out_ref[tile * 8 : tile * 8 + count, chunk * LANES : (chunk + 1) * LANES] = res[
                tile, chunk * 8 : chunk * 8 + count, :
            ]


def call(kernel, outs, scratch=(), copied=0, leaving=0):
    hbm, vmem = (pl.BlockSpec(memory_space=space) for space in (pltpu.HBM, pltpu.VMEM))
    extra = {}
    if copied:
        extra["in_specs"] = [hbm] * copied
    if leaving:
        extra["out_specs"] = [vmem] * (len(outs) - leaving) + [hbm] * leaving
    count = copied + leaving
    return pl.pallas_call(
        kernel,
        out_shape=[jax.ShapeDtypeStruct(shape, dtype) for shape, dtype in outs],
        scratch_shapes=[pltpu.VMEM(shape, dtype) for shape, dtype in scratch]
        + ([pltpu.SemaphoreType.DMA((count,))] if count else []),
        compiler_params=pltpu.CompilerParams(vmem_limit_bytes=(60 if copied else 16) << 20),
        **extra,
    )


def shards(params, visible, blocks, counts, depth_rank, camera, background, target):
    devices = lax.axis_size("space")
    views = lax.axis_size("view")
    chip = [(i, i ^ 1) for i in range(devices)]
    next_chip = [(i, i + 1 if i % 2 else i - 1) for i in range(1, devices - 1)]
    even = lax.axis_index("space") % 2 == 0
    tile = (LANES, LANES)
    kept = ((K, 16, 8, LANES), F32)
    lists = visible[0].T

    goal_top, goal_bottom = target[0, :, 0:10], target[0, :, 6:16]
    goal_chip = lax.ppermute(jnp.where(even, goal_bottom, goal_top), "space", chip)
    goal_next = lax.ppermute(jnp.where(even, goal_top, goal_bottom), "space", next_chip)
    (message,) = call(
        send_kernel,
        [((64, 1, 768), F32)],
        [
            (params.shape, F32),
            ((1, 3), F32),
            ((K, LANES), I32),
            ((1, LANES), I32),
            ((1, 64), I32),
            ((1, 64), I32),
            ((1, 3), F32),
            ((8, LANES, LANES), F32),
            ((META, LANES), F32),
        ],
        copied=7,
    )(params, camera, lists, blocks, counts, depth_rank, background)
    received = lax.all_to_all(message, "space", 0, 0, tiled=True).reshape(64, 768)
    goal, goal_mean, goal_square, inverse = call(
        target_kernel,
        [
            ((3, CHUNKS, 48, LANES), F32),
            ((3, CHUNKS, 32, LANES), F32),
            ((3, CHUNKS, 32, LANES), F32),
            ((32, LANES), I32),
        ],
        [((CHUNKS, 48, LANES), F32)] * 2,
    )(target, goal_chip, goal_next, lists)
    strip, to_chip, far, records, colours, before, total, nearer, through, alphas, weights = call(
        blend_kernel,
        [
            ((3, 16, 512), F32),
            ((3, 10, 512), F32),
            ((3, 10, 512), F32),
            ((TABLE, LANES), F32),
            ((3, *tile), F32),
            (tile, F32),
            (tile, F32),
            (tile, BF16),
            (tile, F32),
            kept,
            kept,
        ],
        [
            (tile, F32),
            ((3, *tile), F32),
            ((TABLE, LANES), F32),
            ((3, *tile), F32),
            ((3, 16, 512), F32),
        ],
    )(received)
    strip_chip = lax.ppermute(to_chip, "space", chip)
    reply, rendered = call(
        loss_kernel,
        [((64, 1, 384), F32), ((3, 16, 512), F32)],
        [
            ((CHUNKS, 48, LANES), F32),
            ((2, CHUNKS, 48, LANES), F32),
            ((3, CHUNKS, 32, LANES), F32),
            ((3, CHUNKS, 16, LANES), F32),
            ((3, 8, 8, LANES), F32),
            ((3, *tile), F32),
            ((3, *tile), F32),
            (tile, F32),
            ((K, 6, 8, LANES), F32),
            ((TABLE, LANES), F32),
        ],
        leaving=1,
    )(
        strip,
        strip_chip,
        far,
        goal,
        goal_mean,
        goal_square,
        records,
        colours,
        before,
        total,
        nearer,
        through,
        alphas,
        weights,
    )
    returned = lax.all_to_all(reply, "space", 0, 0, tiled=True).reshape(64, 384)
    record_grads, loss = call(
        gather_kernel,
        [((TABLE, LANES), F32), ((1, LANES), F32)],
        [((META, LANES), F32)],
    )(returned, inverse)
    others = [
        lax.ppermute(record_grads, "view", [(i, (i + d) % views) for i in range(views)])
        for d in range(1, views)
    ]
    (grad_params,) = call(
        pull_kernel,
        [((59, 2048), F32)],
        [((8, LANES, LANES), F32), ((4, TABLE, LANES), F32), ((8, LANES, LANES), F32)],
    )(params, record_grads, *others)
    return (grad_params, rendered[None], loss[0, 0:1])


def solution(mesh):
    in_specs = (
        P(None, "space"),
        P("space", None, None),
        P("space", None),
        P("space", None),
        P("view", None),
        P("view", None),
        P("view", None),
        P("view", None, "space", None),
    )
    out_specs = (P(None, "space"), P("view", None, "space", None), P("view"))
    return jax.shard_map(shards, mesh=mesh, in_specs=in_specs, out_specs=out_specs, check_vma=False)
```

```python
import math

import jax
import jax.numpy as jnp
from jax import lax
from jax.experimental import pallas as pl
from jax.experimental.pallas import tpu as pltpu
from jax.sharding import PartitionSpec as P

F32 = jnp.float32
BF16 = jnp.bfloat16
I32 = jnp.int32

SH_ZERO = 0.28209479177387814
SH_ONE = 0.4886025119029199
SH_TWO = (
    1.0925484305920792,
    -1.0925484305920792,
    0.31539156525252005,
    -1.0925484305920792,
    0.5462742152960396,
)
SH_THREE = (
    -0.5900435899266435,
    2.890611442640554,
    -0.4570457994644658,
    0.3731763325901154,
    -0.4570457994644658,
    1.445305721320277,
    -0.5900435899266435,
)
DILATION = 0.3
SMOOTHING = 0.0001
SSIM_FIRST = 0.0001
SSIM_SECOND = 0.0009

K = 16
LANES = 128
CHUNKS = 4
GROUP = 4
META = 144
TABLE = 152


def taps():
    raw = [math.exp(-(offset - 5) * (offset - 5) / 4.5) for offset in range(11)]
    total = sum(raw)
    return [value / total for value in raw]


TAPS = taps()


def iota(shape, axis):
    return lax.broadcasted_iota(I32, shape, axis)


def row(x, index, rows):
    return jnp.broadcast_to(x[index : index + 1, :], (rows, x.shape[1]))


def turn_of(angles):
    cos_a, cos_b, cos_c = (jnp.cos(angle) for angle in angles)
    sin_a, sin_b, sin_c = (jnp.sin(angle) for angle in angles)
    return [
        [cos_c * cos_b, cos_c * sin_b * sin_a - sin_c * cos_a, cos_c * sin_b * cos_a + sin_c * sin_a],
        [sin_c * cos_b, sin_c * sin_b * sin_a + cos_c * cos_a, sin_c * sin_b * cos_a - cos_c * sin_a],
        [-sin_b, cos_b * sin_a, cos_b * cos_a],
    ]


def harmonics(axis):
    x, y, z = axis
    xx, yy, zz = (x * x, y * y, z * z)
    return [
        SH_ZERO * jnp.ones_like(x),
        -SH_ONE * y,
        SH_ONE * z,
        -SH_ONE * x,
        SH_TWO[0] * x * y,
        SH_TWO[1] * y * z,
        SH_TWO[2] * (2.0 * zz - xx - yy),
        SH_TWO[3] * x * z,
        SH_TWO[4] * (xx - yy),
        SH_THREE[0] * y * (3.0 * xx - yy),
        SH_THREE[1] * x * y * z,
        SH_THREE[2] * y * (4.0 * zz - xx - yy),
        SH_THREE[3] * z * (2.0 * zz - 3.0 * xx - 3.0 * yy),
        SH_THREE[4] * x * (4.0 * zz - xx - yy),
        SH_THREE[5] * z * (xx - yy),
        SH_THREE[6] * x * (xx - 3.0 * yy),
    ]


def camera_values(rows):
    angles = [jnp.broadcast_to(row, (8, LANES)) for row in rows]
    turn = turn_of(angles)
    basis = harmonics(turn[2])
    cell = lambda value: value[0:1, 0:1]
    return [[cell(value) for value in line] for line in turn], [cell(value) for value in basis]


def load_params(p_ref, scratch, tiles=8):
    for tile in range(tiles):
        count = min(8, 59 - tile * 8)
        for chunk in range(16):
            scratch[tile, chunk * 8 : chunk * 8 + count, :] = p_ref[
                tile * 8 : tile * 8 + count, chunk * LANES : (chunk + 1) * LANES
            ]


def dense_row(scratch, index):
    return scratch[index // 8, pl.ds(index % 8, 16, stride=8), :]


def spin_of(quaternion):
    w, x, y, z = quaternion
    return [
        [1.0 - 2.0 * (y * y + z * z), 2.0 * (x * y - w * z), 2.0 * (x * z + w * y)],
        [2.0 * (x * y + w * z), 1.0 - 2.0 * (x * x + z * z), 2.0 * (y * z - w * x)],
        [2.0 * (x * z - w * y), 2.0 * (y * z + w * x), 1.0 - 2.0 * (x * x + y * y)],
    ]


def sigmoid(x):
    return 1.0 / (1.0 + jnp.exp(-x))


def unit(quaternion):
    total = sum(part * part for part in quaternion)
    inverse = 1.0 / jnp.sqrt(total)
    return [part * inverse for part in quaternion], inverse


def slot_lists(vis_ref):
    natural = vis_ref[...]
    lane = iota((K, LANES), 1)
    order = (lane % 64) * 2 + lane // 64
    return jnp.take_along_axis(natural, order, axis=1), order


def to_message(out_ref, table, twice=False):
    first = table[0:LANES, :].T
    rest = jnp.concatenate(
        [table[LANES:TABLE, :], jnp.zeros((2 * LANES - TABLE, LANES), F32)], axis=0
    ).T
    parts = [rest[0:64] + pltpu.roll(rest[64:128], 64, 1), first[0:64], first[64:128]]
    if twice:
        even = iota((64, LANES), 0) % 2 == 0
        far = [jnp.where(even, pltpu.roll(x, 1, 0), pltpu.roll(x, 63, 0)) for x in parts]
        parts = [parts[0] + pltpu.roll(far[0], 32, 1)] + parts[1:] + far[1:]
    for i, part in enumerate(parts):
        out_ref[:, 0, i * LANES : (i + 1) * LANES] = part


def from_message(in_ref, far=False):
    part = lambda i: in_ref[:, i * LANES : (i + 1) * LANES]
    first = jnp.concatenate([part(3), part(4)] if far else [part(1), part(2)], axis=0).T
    both = pltpu.roll(part(0), LANES - 32, 1) if far else part(0)
    rest = jnp.concatenate([both, pltpu.roll(both, 64, 1)], axis=0)
    return first, rest.T, rest


def send_kernel(
    p_hbm,
    cam_hbm,
    vis_hbm,
    blk_hbm,
    cnt_hbm,
    rank_hbm,
    bg_hbm,
    out_ref,
    p_ref,
    cam_ref,
    vis_ref,
    blk_ref,
    cnt_ref,
    rank_ref,
    bg_ref,
    par,
    rec,
    sems,
):
    me = lax.axis_index("space")
    copies = [
        pltpu.make_async_copy(source, target, sems.at[i])
        for i, (source, target) in enumerate(
            (
                (p_hbm, p_ref),
                (cam_hbm, cam_ref),
                (vis_hbm, vis_ref),
                (blk_hbm, blk_ref),
                (cnt_hbm, cnt_ref),
                (rank_hbm, rank_ref),
                (bg_hbm, bg_ref),
            )
        )
    ]
    for copy in copies:
        copy.start()
    for copy in copies:
        copy.wait()
    load_params(p_ref, par)
    spread = lambda ref: [jnp.broadcast_to(ref[0:1, i : i + 1], (1, LANES)) for i in range(3)]
    angles = spread(cam_ref)
    turn, basis = camera_values(angles)
    get = lambda index: dense_row(par, index)
    scales = [jnp.exp(get(3 + i)) for i in range(3)]
    quaternion, _ = unit([get(6 + i) for i in range(4)])
    spin = spin_of(quaternion)
    frame = [
        [
            (turn[r][0] * spin[0][c] + turn[r][1] * spin[1][c] + turn[r][2] * spin[2][c]) * scales[c]
            for c in range(3)
        ]
        for r in range(2)
    ]
    cov_xx = sum(frame[0][c] * frame[0][c] for c in range(3)) + DILATION
    cov_xy = sum(frame[0][c] * frame[1][c] for c in range(3))
    cov_yy = sum(frame[1][c] * frame[1][c] for c in range(3)) + DILATION
    inverse = 1.0 / (cov_xx * cov_yy - cov_xy * cov_xy)
    shift_x = get(0) - 256.0
    shift_y = get(1) - 512.0
    depth = get(2)
    rec[0:16, :] = turn[0][0] * shift_x + turn[0][1] * shift_y + turn[0][2] * depth + 256.0
    rec[16:32, :] = turn[1][0] * shift_x + turn[1][1] * shift_y + turn[1][2] * depth + 512.0
    rec[32:48, :] = cov_yy * inverse
    rec[48:64, :] = -cov_xy * inverse
    rec[64:80, :] = cov_xx * inverse
    rec[80:96, :] = sigmoid(get(10))
    for c in range(3):
        colour = jnp.full((16, LANES), 0.5, F32)
        for k in range(16):
            colour = colour + basis[k] * get(11 + 3 * k + c)
        rec[96 + 16 * c : 112 + 16 * c, :] = colour
    lists, order = slot_lists(vis_ref)
    low = lists & 127
    high = lists // LANES
    channels = []
    for ch in range(9):
        value = jnp.zeros((K, LANES), F32)
        for h in range(16):
            source = jnp.broadcast_to(rec[ch * 16 + h : ch * 16 + h + 1, :], (K, LANES))
            value = jnp.where(high == h, jnp.take_along_axis(source, low, axis=1), value)
        channels.append(value)
    blk = jnp.take_along_axis(jnp.broadcast_to(blk_ref[...], (8, LANES)), order[0:8], axis=1)
    counts = jnp.concatenate([cnt_ref[...], cnt_ref[...]], axis=1)
    ids = jnp.where(iota((1, LANES), 1) // 64 < counts, blk[0:1], -1).astype(F32)
    rank = jnp.sum(
        jnp.where(iota((1, 64), 1) == me, rank_ref[...], 0).astype(F32), axis=1, keepdims=True
    )
    meta = [ids, jnp.broadcast_to(rank, (1, LANES))] + spread(bg_ref) + angles
    to_message(out_ref, jnp.concatenate(channels + meta, axis=0), twice=True)


def across(chunks):
    lane = iota(chunks[0].shape, 1)
    total = [TAPS[5] * x for x in chunks]
    for s in range(1, 6):
        right = [pltpu.roll(x, s, 1) for x in chunks]
        left = [pltpu.roll(x, LANES - s, 1) for x in chunks]
        low, high = lane < s, lane >= LANES - s
        before = [0.0] + right[:-1]
        after = left[1:] + [0.0]
        total = [
            t + TAPS[5 + s] * (jnp.where(low, b, r) + jnp.where(high, a, f))
            for t, b, r, f, a in zip(total, before, right, left, after)
        ]
    return total


def blur(source, start, count=8):
    chunks = []
    for j in range(CHUNKS):
        load = lambda first: source[j, first : first + count, :]
        total = TAPS[5] * load(start + 5)
        for s in range(1, 6):
            total = total + TAPS[5 + s] * (load(start + 5 - s) + load(start + 5 + s))
        chunks.append(total)
    return across(chunks)


def fill_rows(ext, own, chip, next_chip, ch, even):
    for j in range(CHUNKS):
        cols = slice(j * LANES, (j + 1) * LANES)
        ext[j, 0:8, :] = jnp.zeros((8, LANES), F32)
        ext[j, 40:48, :] = jnp.zeros((8, LANES), F32)
        near, far = chip[ch, :, cols], next_chip[ch, :, cols]
        ext[j, 6:16, :] = jnp.where(even, far, near)
        ext[j, 16:32, :] = own[ch, :, cols]
        ext[j, 32:42, :] = jnp.where(even, near, far)


def target_kernel(own, chip, next_chip, ext_ref, mean_ref, square_ref, tmp, sq):
    even = lax.axis_index("space") % 2 == 0

    def channel(ch, carry):
        fill_rows(tmp, own.at[0], chip, next_chip, ch, even)
        for j in range(CHUNKS):
            ext_ref[ch, j] = tmp[j]
            sq[j] = tmp[j] * tmp[j]
        for source, out in ((tmp, mean_ref), (sq, square_ref)):
            for top in range(0, 32, 8):
                blurred = blur(source, 6 + top)
                for j in range(CHUNKS):
                    out[ch, j, top : top + 8, :] = blurred[j]
        return carry

    for ch in range(3):
        channel(ch, 0)


def inverse_kernel(vis_ref, inv_ref):
    lists, _ = slot_lists(vis_ref)
    low = lists & 127
    high = lists // LANES
    total = jnp.zeros((2 * 16, LANES), F32)
    lane = iota((1, LANES), 1)
    for k in range(K):
        here = row(high, k, 16) == iota((16, LANES), 0)
        value = jnp.concatenate(
            [
                jnp.where(here, float(k), 0.0),
                jnp.where(here, jnp.broadcast_to(lane, (16, LANES)).astype(F32), 0.0),
            ],
            axis=0,
        ).astype(BF16)
        table = (row(low, k, LANES) == iota((LANES, LANES), 0)).astype(F32).astype(BF16)
        total = total + lax.dot_general(
            value, table, (((1,), (1,)), ((), ())), preferred_element_type=F32
        )
    inv_ref[...] = total.astype(I32)


def pieces(x):
    first = x.astype(BF16)
    left = x - first.astype(F32)
    second = left.astype(BF16)
    third = (left - second.astype(F32)).astype(BF16)
    return first, second, third


def dot_mask(x, mask, contract):
    dims = (((1,), (contract,)), ((), ()))
    parts = [lax.dot_general(p, mask, dims, preferred_element_type=F32) for p in pieces(x)]
    return parts[0] + (parts[1] + parts[2])


def corners(ids, me):
    block = jnp.maximum(ids, 0.0).astype(I32)
    x = (block % 32 * 16).astype(F32) + 0.5
    y = (me * 16 + block // 32 * 8).astype(F32) + 0.5
    return x, y


def splat_terms(rec, k, x0, y_grid):
    get = lambda ch: jnp.broadcast_to(rec[pl.ds(ch * K + k, 1), :], (8, LANES))
    dy = y_grid - get(1)
    return x0 - get(0), dy, get(2) * -0.5, get(3) * dy, get(4) * -0.5 * dy * dy, get(5)


def render(rec, corner_x, y_grid, logs, colours_out, keep=None):
    def group(g, carry):
        base = corner_x + (g * GROUP).astype(F32)

        def four(kk, state):
            through, log_sum, colours = state
            part = [jnp.ones((8, LANES), F32)] * GROUP
            for k4 in range(4):
                k = kk * 4 + k4
                dx0, dy, ma, mb_y, mc_yy, opacity = splat_terms(rec, k, base, y_grid)
                tint = [
                    jnp.broadcast_to(rec[pl.ds((6 + c) * K + k, 1), :], (8, LANES))
                    for c in range(3)
                ]
                for i in range(GROUP):
                    dx = dx0 + float(i)
                    alpha = opacity * jnp.exp((ma * dx - mb_y) * dx + mc_yy)
                    weight = alpha * through[i]
                    if keep:
                        keep[0][k, g * GROUP + i] = alpha
                        keep[1][k, g * GROUP + i] = weight
                    left = 1.0 - alpha
                    through = through[:i] + (through[i] * left,) + through[i + 1 :]
                    part[i] = part[i] * left
                    colours = (
                        colours[:i]
                        + (tuple(colours[i][c] + weight * tint[c] for c in range(3)),)
                        + colours[i + 1 :]
                    )
            log_sum = tuple(log_sum[i] + jnp.log(part[i]) for i in range(GROUP))
            return through, log_sum, colours

        zero = jnp.zeros((8, LANES), F32)
        start = ((jnp.ones((8, LANES), F32),) * GROUP, (zero,) * GROUP, ((zero,) * 3,) * GROUP)
        through, log_sum, colours = lax.fori_loop(0, 4, four, start, unroll=4)
        for i in range(GROUP):
            rows = pl.ds(pl.multiple_of((g * GROUP + i) * 8, 8), 8)
            logs[rows, :] = log_sum[i]
            if keep:
                keep[2][rows, :] = through[i]
            for c in range(3):
                colours_out[c, rows, :] = colours[i][c]
        return carry

    lax.fori_loop(0, 16 // GROUP, group, 0)


def masks(rest_rows, rest_cols):
    id_row = row(rest_rows, 16, LANES)
    rank_row = row(rest_rows, 17, LANES)
    id_col = jnp.broadcast_to(rest_cols[:, 16:17], (LANES, LANES))
    rank_col = jnp.broadcast_to(rest_cols[:, 17:18], (LANES, LANES))
    live = id_row >= 0.0
    same = jnp.where((id_row == id_col) & live, 1.0, 0.0)
    nearer = jnp.where(rank_col < rank_row, same, 0.0).astype(BF16)
    block = (iota((LANES, LANES), 1) % 64).astype(F32)
    member = jnp.where(id_col == block, 1.0, 0.0).astype(BF16)
    return live, same.astype(BF16), nearer, member


def to_rows(before, open_sky, colours, member, sky_rows, blocks_ref, strip_ref):
    lane = iota((8, LANES), 1)
    for c in range(3):
        blocks_ref[c] = (
            dot_mask(before * colours[c], member, 0) + sky_rows[18 + c : 19 + c] * open_sky
        )
    pair = lane % 16 // 2
    for c in range(3):
        for p in range(8):
            blocks_ref[c, p * 16 : p * 16 + 8, :] = jnp.where(
                lane < 64,
                blocks_ref[c, p * 16 : p * 16 + 8, :],
                blocks_ref[c, p * 16 + 8 : p * 16 + 16, :],
            )
    for br in range(2):
        for t in range(CHUNKS):
            index = lane % 2 * 64 + (br * 32 + 8 * t) + lane // 16
            values = [None] * 3
            for p in range(8):
                for c in range(3):
                    got = jnp.take_along_axis(
                        blocks_ref[c, p * 16 : p * 16 + 8, :], index, axis=1
                    )
                    values[c] = jnp.where(pair == p, got, values[c]) if p else got
            for c in range(3):
                strip_ref[c, br * 8 : br * 8 + 8, t * LANES : (t + 1) * LANES] = values[c]


def blend_kernel(
    recv_ref,
    order_ref,
    strip_ref,
    chip_ref,
    far_ref,
    rec,
    colour_ref,
    before_ref,
    total_ref,
    nearer_ref,
    through_ref,
    alphas,
    weights,
    logs,
    blocks_ref,
    far_rec,
    far_colour,
    far_strip,
):
    me = lax.axis_index("space")
    even = me % 2 == 0
    row_of = iota((8, LANES), 0).astype(F32)

    first, rest_rows, rest_cols = from_message(recv_ref)
    rec[0:LANES, :] = first
    rec[LANES:TABLE, :] = rest_rows[0:24]
    corner_x, corner_y = corners(row(rest_rows, 16, 8), me)
    render(rec, corner_x, corner_y + row_of, logs, colour_ref, (alphas, weights, through_ref))
    live, same, nearer, member = masks(rest_rows, rest_cols)
    nearer_ref[...] = nearer
    ahead = dot_mask(logs[...], jnp.concatenate([nearer, same, member], axis=1), 0)
    before = jnp.where(live, jnp.exp(ahead[:, 0:LANES]), 0.0)
    before_ref[...] = before
    total_ref[...] = jnp.where(live, jnp.exp(ahead[:, LANES : 2 * LANES]), 0.0)
    to_rows(
        before, jnp.exp(ahead[:, 2 * LANES :]), colour_ref, member, rest_rows, blocks_ref, strip_ref
    )
    chip_ref[...] = jnp.where(even, strip_ref[:, 6:16, :], strip_ref[:, 0:10, :])

    first, rest_rows, rest_cols = from_message(recv_ref, far=True)
    far_rec[0:LANES, :] = first
    far_rec[LANES:TABLE, :] = rest_rows[0:24]
    corner_x, corner_y = corners(row(rest_rows, 16, 8), jnp.where(even, me - 1, me + 1))
    render(far_rec, corner_x, corner_y + row_of, logs, far_colour)
    live, _, nearer, member = masks(rest_rows, rest_cols)
    ahead = dot_mask(logs[...], jnp.concatenate([nearer, member], axis=1), 0)
    before = jnp.where(live, jnp.exp(ahead[:, 0:LANES]), 0.0)
    to_rows(
        before, jnp.exp(ahead[:, LANES:]), far_colour, member, rest_rows, blocks_ref, far_strip
    )
    near_edge = jnp.where(even, far_strip[:, 6:16, :], far_strip[:, 0:10, :])
    far_ref[...] = jnp.where((me > 0) & (me < 63), near_edge, 0.0)


def loss_kernel(
    strip_ref,
    chip,
    next_chip,
    ext_ref,
    mean_ref,
    square_ref,
    rec,
    colour_ref,
    before_ref,
    total_ref,
    nearer_ref,
    through_ref,
    alphas,
    weights,
    out_ref,
    rendered_ref,
    ext,
    prod,
    stat,
    grads,
    spread_grads,
    pulled,
    cot,
    behind_cot,
    sums,
    table,
    sems,
):
    copy = pltpu.make_async_copy(strip_ref, rendered_ref, sems.at[0])
    copy.start()
    me = lax.axis_index("space")
    first_c, second_c = SSIM_FIRST, SSIM_SECOND
    even = me % 2 == 0

    def channel(ch, loss):
        fill_rows(ext, strip_ref, chip, next_chip, ch, even)
        for j in range(CHUNKS):
            a = ext[j]
            prod[0, j] = a * a
            prod[1, j] = a * ext_ref[ch, j]
        for top in range(0, 32, 8):
            t_row = iota((8, LANES), 0) + top
            where = me * 16 - 5 + t_row
            inside = jnp.where((where >= 0) & (where < 1024) & (t_row < 26), -0.2, 0.0)
            own = (t_row >= 5) & (t_row < 21)
            blurred = [blur(source, 6 + top) for source in (ext, prod.at[0], prod.at[1])]
            rows = slice(top, top + 8)
            for j in range(CHUNKS):
                ma, mb = blurred[0][j], mean_ref[ch, j, rows, :]
                mab = ma * mb
                squares = ma * ma + mb * mb
                n1 = 2.0 * mab + first_c
                n2 = 2.0 * (blurred[2][j] - mab) + second_c
                d1 = squares + first_c
                d2 = (blurred[1][j] + square_ref[ch, j, rows, :]) - squares + second_c
                inverse = 1.0 / (d1 * d2)
                ssim = n1 * n2 * inverse
                loss = loss + jnp.where(own, 0.2 - 0.2 * ssim, 0.0)
                seed = inside * inverse
                g1 = seed * n2
                g2 = seed * n1
                scaled = seed * ssim
                gd1 = scaled * d2
                gd2 = scaled * d1
                stat[0, j, rows, :] = 2.0 * (mb * (g1 - g2) + ma * (gd2 - gd1))
                stat[1, j, rows, :] = -gd2
                stat[2, j, rows, :] = 2.0 * g2
        for top in (0, 8):
            spread = [blur(stat.at[q], top) for q in range(3)]
            rows = slice(16 + top, 24 + top)
            for j in range(CHUNKS):
                a = ext[j, rows, :]
                b = ext_ref[ch, j, rows, :]
                differ = a - b
                root = jnp.sqrt(differ * differ + SMOOTHING)
                loss = loss + 0.8 * root
                grads[ch, j, top : top + 8, :] = (
                    spread[0][j] + 2.0 * a * spread[1][j] + b * spread[2][j] + 0.8 * differ / root
                )
        return loss

    loss = jnp.zeros((8, LANES), F32)
    for ch in range(3):
        loss = channel(ch, loss)
    loss = jnp.sum(jnp.sum(loss, axis=0, keepdims=True), axis=1, keepdims=True)

    ids = row(rec[...], META, 8)
    live = ids >= 0.0
    block = jnp.maximum(ids, 0.0).astype(I32)
    lane = iota((8, LANES), 1)
    place = lane % 64 // 8
    for p in range(8):
        start = lane % 8 * 16 + 2 * p + lane // 64
        both = [None] * 3
        for n in range(8):
            br, t = divmod(n, CHUNKS)
            for c in range(3):
                got = jnp.take_along_axis(grads[c, t, br * 8 : br * 8 + 8, :], start, axis=1)
                both[c] = jnp.where(place == n, got, both[c]) if n else got
        for c in range(3):
            spread_grads[c, p] = both[c]
    for odd in range(2):
        index = block + 64 * odd
        for p in range(8):
            for c in range(3):
                value = jnp.take_along_axis(spread_grads[c, p], index, axis=1)
                first = (2 * p + odd) * 8
                pulled[c, first : first + 8, :] = jnp.where(live, value, 0.0)
    before = before_ref[...]
    behind = jnp.zeros((LANES, LANES), F32)
    sky = jnp.zeros((LANES, LANES), F32)
    for c in range(3):
        g = pulled[c]
        scaled = before * g
        cot[c] = scaled
        behind = behind + scaled * colour_ref[c]
        sky = sky + rec[META + 2 + c : META + 3 + c, :] * g
    log_cot = dot_mask(behind, nearer_ref[...], 1) + total_ref[...] * sky
    left = through_ref[...]
    some = left > 0.0
    behind_cot[...] = jnp.where(some, log_cot / jnp.where(some, left, 1.0), 0.0)

    corner_x, corner_y = corners(ids, me)
    y_grid = corner_y + iota((8, LANES), 0).astype(F32)

    def group(g, carry):
        base = corner_x + (g * GROUP).astype(F32)
        rows = [pl.ds(pl.multiple_of((g * GROUP + i) * 8, 8), 8) for i in range(GROUP)]
        suffix = tuple(behind_cot[rows[i], :] for i in range(GROUP))
        pull = [[cot[c, rows[i], :] for c in range(3)] for i in range(GROUP)]
        zero = jnp.zeros((8, LANES), F32)

        def back(step, suffix):
            k = K - 1 - step
            get = lambda ch: jnp.broadcast_to(rec[pl.ds(ch * K + k, 1), :], (8, LANES))
            dx0 = base - get(0)
            tint = [get(6 + c) for c in range(3)]
            s0, s1, s2 = zero, zero, zero
            shade = [zero] * 3
            after = []
            for i in range(GROUP):
                dx = dx0 + float(i)
                weight = weights[k, g * GROUP + i]
                gain = (
                    pull[i][0] * tint[0] + pull[i][1] * tint[1] + pull[i][2] * tint[2] - suffix[i]
                )
                after.append(suffix[i] + alphas[k, g * GROUP + i] * gain)
                moment = weight * gain
                shade = [shade[c] + weight * pull[i][c] for c in range(3)]
                moment_x = moment * dx
                s0 = s0 + moment
                s1 = s1 + moment_x
                s2 = s2 + moment_x * dx
            for n, value in enumerate([s0, s1, s2] + shade):
                sums[k, n] = jnp.where(g == 0, value, sums[k, n] + value)
            return tuple(after)

        lax.fori_loop(0, K, back, suffix, unroll=2)
        return carry

    lax.fori_loop(0, 16 // GROUP, group, 0)

    def finish(k, carry):
        get = lambda ch: rec[pl.ds(ch * K + k, 1), :]
        dy = y_grid - jnp.broadcast_to(get(1), (8, LANES))
        s0, s1, s2 = sums[k, 0], sums[k, 1], sums[k, 2]
        fold = lambda value: jnp.sum(value, axis=0, keepdims=True)
        s0_y = s0 * dy
        m0, mx, mxx = fold(s0), fold(s1), fold(s2)
        my, mxy, myy = fold(s0_y), fold(s1 * dy), fold(s0_y * dy)
        conic_a, conic_b, conic_c = get(2), get(3), get(4)
        out = [
            conic_a * mx + conic_b * my,
            conic_b * mx + conic_c * my,
            -0.5 * mxx,
            -mxy,
            -0.5 * myy,
            m0,
        ] + [fold(sums[k, 3 + c]) for c in range(3)]
        for ch in range(9):
            table[pl.ds(ch * K + k, 1), :] = out[ch]
        return carry

    lax.fori_loop(0, K, finish, 0, unroll=4)
    table[META:TABLE, :] = jnp.concatenate(
        [jnp.broadcast_to(loss, (5, LANES)), rec[META + 5 : TABLE, :]], axis=0
    )
    to_message(out_ref, table[...])
    copy.wait()


def gather_kernel(recv_ref, inv_ref, out_ref, loss_ref, rec):
    first, rest_rows, rest_cols = from_message(recv_ref)
    rec[0:LANES, :] = first
    rec[LANES:META, :] = rest_rows[0:16]
    at_k = inv_ref[0:16, :]
    at_slot = inv_ref[16:32, :]
    for ch in range(9):
        value = jnp.zeros((16, LANES), F32)
        for k in range(K):
            source = jnp.broadcast_to(rec[ch * K + k : ch * K + k + 1, :], (16, LANES))
            value = jnp.where(at_k == k, jnp.take_along_axis(source, at_slot, axis=1), value)
        out_ref[ch * 16 : ch * 16 + 16, :] = value
    out_ref[META:TABLE, :] = rest_rows[16:24]
    total = jnp.sum(rest_cols[0:64, 16:17], axis=0, keepdims=True)
    loss_ref[...] = jnp.broadcast_to(total * (1.0 / 1572864.0), (1, LANES))


def lay_out(rows, start, scratch, out_ref):
    for n, value in enumerate(rows):
        index = start + n
        scratch[index // 8, pl.ds(index % 8, 16, stride=8), :] = value
    for first in range(start, start + len(rows), 8):
        count = min(8, start + len(rows) - first)
        for chunk in range(16):
            out_ref[first : first + count, chunk * LANES : (chunk + 1) * LANES] = scratch[
                first // 8, chunk * 8 : chunk * 8 + count, :
            ]


def pull_kernel(p_ref, rec0, rec1, rec2, rec3, out_hbm, par, views, res, out_ref, sems):
    me = lax.axis_index("view")
    load_params(p_ref, par, 2)
    for d, source in enumerate((rec0, rec1, rec2, rec3)):
        views[(me - d + 4) % 4] = source[...]
    get = lambda index: dense_row(par, index)
    scales = [jnp.exp(get(3 + i)) for i in range(3)]
    quaternion, inverse_norm = unit([get(6 + i) for i in range(4)])
    spin = spin_of(quaternion)
    coefficients = []
    angles = [
        [views[v, META + 5 + i : META + 6 + i, :] for i in range(3)] for v in range(4)
    ]
    cameras = [camera_values(angles[v]) for v in range(4)]
    for k in range(16):
        for c in range(3):
            rows = slice(96 + 16 * c, 112 + 16 * c)
            total = cameras[0][1][k] * views[0, rows, :]
            for v in range(1, 4):
                total = total + cameras[v][1][k] * views[v, rows, :]
            coefficients.append(total)
    lay_out(coefficients[5:], 16, res, out_ref)
    body = pltpu.make_async_copy(out_ref.at[16:59], out_hbm.at[16:59], sems.at[0])
    body.start()
    zero = jnp.zeros((16, LANES), F32)
    g_pos = [zero] * 3
    g_frame_spin = [[zero] * 3 for _ in range(3)]
    g_log = [zero] * 3
    g_logit = zero
    for v in range(4):
        turn = cameras[v][0]
        g = [views[v, ch * 16 : ch * 16 + 16, :] for ch in range(6)]
        unscaled = [
            [turn[r][0] * spin[0][c] + turn[r][1] * spin[1][c] + turn[r][2] * spin[2][c] for c in range(3)]
            for r in range(2)
        ]
        frame = [[unscaled[r][c] * scales[c] for c in range(3)] for r in range(2)]
        cov_xx = sum(frame[0][c] * frame[0][c] for c in range(3)) + DILATION
        cov_xy = sum(frame[0][c] * frame[1][c] for c in range(3))
        cov_yy = sum(frame[1][c] * frame[1][c] for c in range(3)) + DILATION
        inverse = 1.0 / (cov_xx * cov_yy - cov_xy * cov_xy)
        ca, cb, cc = cov_yy * inverse, -cov_xy * inverse, cov_xx * inverse
        ga, gb, gc = g[2], 0.5 * g[3], g[4]
        left = [
            [ca * ga + cb * gb, ca * gb + cb * gc],
            [cb * ga + cc * gb, cb * gb + cc * gc],
        ]
        g_xx = -(left[0][0] * ca + left[0][1] * cb)
        g_xy = -(left[0][0] * cb + left[0][1] * cc)
        g_yy = -(left[1][0] * cb + left[1][1] * cc)
        for c in range(3):
            gf0 = 2.0 * (g_xx * frame[0][c] + g_xy * frame[1][c])
            gf1 = 2.0 * (g_xy * frame[0][c] + g_yy * frame[1][c])
            g_log[c] = g_log[c] + gf0 * frame[0][c] + gf1 * frame[1][c]
            for m in range(3):
                g_frame_spin[m][c] = g_frame_spin[m][c] + (turn[0][m] * gf0 + turn[1][m] * gf1)
        for m in range(3):
            g_pos[m] = g_pos[m] + turn[0][m] * g[0] + turn[1][m] * g[1]
        g_logit = g_logit + g[5]
    s = [[g_frame_spin[m][c] * scales[c] for c in range(3)] for m in range(3)]
    w, x, y, z = quaternion
    g_unit = [
        2.0 * (x * (s[2][1] - s[1][2]) + y * (s[0][2] - s[2][0]) + z * (s[1][0] - s[0][1])),
        2.0 * (y * (s[0][1] + s[1][0]) + z * (s[0][2] + s[2][0]) + w * (s[2][1] - s[1][2]))
        - 4.0 * x * (s[1][1] + s[2][2]),
        2.0 * (x * (s[0][1] + s[1][0]) + z * (s[1][2] + s[2][1]) + w * (s[0][2] - s[2][0]))
        - 4.0 * y * (s[0][0] + s[2][2]),
        2.0 * (x * (s[0][2] + s[2][0]) + y * (s[1][2] + s[2][1]) + w * (s[1][0] - s[0][1]))
        - 4.0 * z * (s[0][0] + s[1][1]),
    ]
    along = sum(q * g for q, g in zip(quaternion, g_unit))
    g_quat = [(g - q * along) * inverse_norm for q, g in zip(quaternion, g_unit)]
    rest = sigmoid(-get(10))
    rows = g_pos + g_log + g_quat + [g_logit * rest]
    lay_out(rows + coefficients[:5], 0, res, out_ref)
    head = pltpu.make_async_copy(out_ref.at[0:16], out_hbm.at[0:16], sems.at[1])
    head.start()
    body.wait()
    head.wait()


def call(kernel, outs, scratch=(), copied=0, leaving=0, sems=0):
    hbm, vmem = (pl.BlockSpec(memory_space=space) for space in (pltpu.HBM, pltpu.VMEM))
    extra = {}
    if copied:
        extra["in_specs"] = [hbm] * copied
    if leaving:
        extra["out_specs"] = [vmem] * (len(outs) - leaving) + [hbm] * leaving
    count = sems or copied + leaving
    return pl.pallas_call(
        kernel,
        out_shape=[jax.ShapeDtypeStruct(shape, dtype) for shape, dtype in outs],
        scratch_shapes=[pltpu.VMEM(shape, dtype) for shape, dtype in scratch]
        + ([pltpu.SemaphoreType.DMA((count,))] if count else []),
        compiler_params=pltpu.CompilerParams(vmem_limit_bytes=(60 if copied else 16) << 20),
        **extra,
    )


def shards(params, visible, blocks, counts, depth_rank, camera, background, target):
    devices = lax.axis_size("space")
    views = lax.axis_size("view")
    chip = [(i, i ^ 1) for i in range(devices)]
    next_chip = [(i, i + 1 if i % 2 else i - 1) for i in range(1, devices - 1)]
    even = lax.axis_index("space") % 2 == 0
    tile = (LANES, LANES)
    kept = ((K, 16, 8, LANES), F32)
    lists = visible[0].T

    goal_top, goal_bottom = target[0, :, 0:10], target[0, :, 6:16]
    goal_chip = lax.ppermute(jnp.where(even, goal_bottom, goal_top), "space", chip)
    goal_next = lax.ppermute(jnp.where(even, goal_top, goal_bottom), "space", next_chip)
    (message,) = call(
        send_kernel,
        [((64, 1, 640), F32)],
        [
            (params.shape, F32),
            ((1, 3), F32),
            ((K, LANES), I32),
            ((1, LANES), I32),
            ((1, 64), I32),
            ((1, 64), I32),
            ((1, 3), F32),
            ((8, LANES, LANES), F32),
            ((META, LANES), F32),
        ],
        copied=7,
    )(params, camera, lists, blocks, counts, depth_rank, background)
    received = lax.all_to_all(message, "space", 0, 0, tiled=True).reshape(64, 640)
    (inverse,) = call(inverse_kernel, [((32, LANES), I32)])(lists)
    goal, goal_mean, goal_square = call(
        target_kernel,
        [
            ((3, CHUNKS, 48, LANES), F32),
            ((3, CHUNKS, 32, LANES), F32),
            ((3, CHUNKS, 32, LANES), F32),
        ],
        [((CHUNKS, 48, LANES), F32)] * 2,
    )(target, goal_chip, goal_next)
    strip, to_chip, far, records, colours, before, total, nearer, through, alphas, weights = call(
        blend_kernel,
        [
            ((3, 16, 512), F32),
            ((3, 10, 512), F32),
            ((3, 10, 512), F32),
            ((TABLE, LANES), F32),
            ((3, *tile), F32),
            (tile, F32),
            (tile, F32),
            (tile, BF16),
            (tile, F32),
            kept,
            kept,
        ],
        [
            (tile, F32),
            ((3, *tile), F32),
            ((TABLE, LANES), F32),
            ((3, *tile), F32),
            ((3, 16, 512), F32),
        ],
    )(received, inverse)
    strip_chip = lax.ppermute(to_chip, "space", chip)
    reply, rendered = call(
        loss_kernel,
        [((64, 1, 384), F32), ((3, 16, 512), F32)],
        [
            ((CHUNKS, 48, LANES), F32),
            ((2, CHUNKS, 48, LANES), F32),
            ((3, CHUNKS, 32, LANES), F32),
            ((3, CHUNKS, 16, LANES), F32),
            ((3, 8, 8, LANES), F32),
            ((3, *tile), F32),
            ((3, *tile), F32),
            (tile, F32),
            ((K, 6, 8, LANES), F32),
            ((TABLE, LANES), F32),
        ],
        leaving=1,
    )(
        strip,
        strip_chip,
        far,
        goal,
        goal_mean,
        goal_square,
        records,
        colours,
        before,
        total,
        nearer,
        through,
        alphas,
        weights,
    )
    returned = lax.all_to_all(reply, "space", 0, 0, tiled=True).reshape(64, 384)
    record_grads, loss = call(
        gather_kernel,
        [((TABLE, LANES), F32), ((1, LANES), F32)],
        [((META, LANES), F32)],
    )(returned, inverse)
    others = [
        lax.ppermute(record_grads, "view", [(i, (i + d) % views) for i in range(views)])
        for d in range(1, views)
    ]
    (grad_params,) = call(
        pull_kernel,
        [((59, 2048), F32)],
        [
            ((8, LANES, LANES), F32),
            ((4, TABLE, LANES), F32),
            ((8, LANES, LANES), F32),
            (params.shape, F32),
        ],
        leaving=1,
        sems=2,
    )(params, record_grads, *others)
    return (grad_params, rendered[None], loss[0, 0:1])


def solution(mesh):
    in_specs = (
        P(None, "space"),
        P("space", None, None),
        P("space", None),
        P("space", None),
        P("view", None),
        P("view", None),
        P("view", None),
        P("view", None, "space", None),
    )
    out_specs = (P(None, "space"), P("view", None, "space", None), P("view"))
    return jax.shard_map(shards, mesh=mesh, in_specs=in_specs, out_specs=out_specs, check_vma=False)
```

```python
import math

import jax
import jax.numpy as jnp
from jax import lax
from jax.experimental import pallas as pl
from jax.experimental.pallas import tpu as pltpu
from jax.sharding import PartitionSpec as P

F32 = jnp.float32
BF16 = jnp.bfloat16
I32 = jnp.int32

SH_ZERO = 0.28209479177387814
SH_ONE = 0.4886025119029199
SH_TWO = (
    1.0925484305920792,
    -1.0925484305920792,
    0.31539156525252005,
    -1.0925484305920792,
    0.5462742152960396,
)
SH_THREE = (
    -0.5900435899266435,
    2.890611442640554,
    -0.4570457994644658,
    0.3731763325901154,
    -0.4570457994644658,
    1.445305721320277,
    -0.5900435899266435,
)
DILATION = 0.3
SMOOTHING = 0.0001
SSIM_FIRST = 0.0001
SSIM_SECOND = 0.0009

K = 16
LANES = 128
CHUNKS = 4
GROUP = 4
META = 144
TABLE = 152


def taps():
    raw = [math.exp(-(offset - 5) * (offset - 5) / 4.5) for offset in range(11)]
    total = sum(raw)
    return [value / total for value in raw]


TAPS = taps()


def iota(shape, axis):
    return lax.broadcasted_iota(I32, shape, axis)


def row(x, index, rows):
    return jnp.broadcast_to(x[index : index + 1, :], (rows, x.shape[1]))


def turn_of(angles):
    count = angles[0].shape[0]
    stacked = jnp.concatenate(angles, axis=0)
    cosines, sines = jnp.cos(stacked), jnp.sin(stacked)
    cos_a, cos_b, cos_c = (cosines[i * count : (i + 1) * count] for i in range(3))
    sin_a, sin_b, sin_c = (sines[i * count : (i + 1) * count] for i in range(3))
    return [
        [cos_c * cos_b, cos_c * sin_b * sin_a - sin_c * cos_a, cos_c * sin_b * cos_a + sin_c * sin_a],
        [sin_c * cos_b, sin_c * sin_b * sin_a + cos_c * cos_a, sin_c * sin_b * cos_a - cos_c * sin_a],
        [-sin_b, cos_b * sin_a, cos_b * cos_a],
    ]


def harmonics(axis):
    x, y, z = axis
    xx, yy, zz = (x * x, y * y, z * z)
    return [
        SH_ZERO * jnp.ones_like(x),
        -SH_ONE * y,
        SH_ONE * z,
        -SH_ONE * x,
        SH_TWO[0] * x * y,
        SH_TWO[1] * y * z,
        SH_TWO[2] * (2.0 * zz - xx - yy),
        SH_TWO[3] * x * z,
        SH_TWO[4] * (xx - yy),
        SH_THREE[0] * y * (3.0 * xx - yy),
        SH_THREE[1] * x * y * z,
        SH_THREE[2] * y * (4.0 * zz - xx - yy),
        SH_THREE[3] * z * (2.0 * zz - 3.0 * xx - 3.0 * yy),
        SH_THREE[4] * x * (4.0 * zz - xx - yy),
        SH_THREE[5] * z * (xx - yy),
        SH_THREE[6] * x * (xx - 3.0 * yy),
    ]


def camera_values(angles):
    turn = turn_of(angles)
    basis = harmonics(turn[2])
    cell = lambda value, v: value[v : v + 1, :]
    return [
        ([[cell(value, v) for value in line] for line in turn], [cell(value, v) for value in basis])
        for v in range(angles[0].shape[0])
    ]


def load_params(p_ref, scratch, tiles=8):
    for tile in range(tiles):
        count = min(8, 59 - tile * 8)
        for chunk in range(16):
            scratch[tile, chunk * 8 : chunk * 8 + count, :] = p_ref[
                tile * 8 : tile * 8 + count, chunk * LANES : (chunk + 1) * LANES
            ]


def dense_row(scratch, index):
    return scratch[index // 8, pl.ds(index % 8, 16, stride=8), :]


def spin_of(quaternion):
    w, x, y, z = quaternion
    return [
        [1.0 - 2.0 * (y * y + z * z), 2.0 * (x * y - w * z), 2.0 * (x * z + w * y)],
        [2.0 * (x * y + w * z), 1.0 - 2.0 * (x * x + z * z), 2.0 * (y * z - w * x)],
        [2.0 * (x * z - w * y), 2.0 * (y * z + w * x), 1.0 - 2.0 * (x * x + y * y)],
    ]


def sigmoid(x):
    return 1.0 / (1.0 + jnp.exp(-x))


def unit(quaternion):
    total = sum(part * part for part in quaternion)
    inverse = 1.0 / jnp.sqrt(total)
    return [part * inverse for part in quaternion], inverse


def slot_lists(vis_ref):
    natural = vis_ref[...]
    lane = iota((K, LANES), 1)
    order = (lane % 64) * 2 + lane // 64
    return jnp.take_along_axis(natural, order, axis=1), order


def to_message(out_ref, table, twice=False):
    first = table[0:LANES, :].T
    rest = jnp.concatenate(
        [table[LANES:TABLE, :], jnp.zeros((2 * LANES - TABLE, LANES), F32)], axis=0
    ).T
    parts = [rest[0:64] + pltpu.roll(rest[64:128], 64, 1), first[0:64], first[64:128]]
    if twice:
        even = iota((64, LANES), 0) % 2 == 0
        far = [jnp.where(even, pltpu.roll(x, 1, 0), pltpu.roll(x, 63, 0)) for x in parts]
        parts = [parts[0] + pltpu.roll(far[0], 32, 1)] + parts[1:] + far[1:]
    for i, part in enumerate(parts):
        out_ref[:, 0, i * LANES : (i + 1) * LANES] = part


def from_message(in_ref, far=False):
    part = lambda i: in_ref[:, i * LANES : (i + 1) * LANES]
    first = jnp.concatenate([part(3), part(4)] if far else [part(1), part(2)], axis=0).T
    both = pltpu.roll(part(0), LANES - 32, 1) if far else part(0)
    rest = jnp.concatenate([both, pltpu.roll(both, 64, 1)], axis=0)
    return first, rest.T, rest


def send_kernel(
    p_hbm,
    cam_hbm,
    vis_hbm,
    blk_hbm,
    cnt_hbm,
    rank_hbm,
    bg_hbm,
    out_ref,
    p_ref,
    cam_ref,
    vis_ref,
    blk_ref,
    cnt_ref,
    rank_ref,
    bg_ref,
    par,
    rec,
    sems,
):
    me = lax.axis_index("space")
    copies = [
        pltpu.make_async_copy(source, target, sems.at[i])
        for i, (source, target) in enumerate(
            (
                (p_hbm, p_ref),
                (cam_hbm, cam_ref),
                (vis_hbm, vis_ref),
                (blk_hbm, blk_ref),
                (cnt_hbm, cnt_ref),
                (rank_hbm, rank_ref),
                (bg_hbm, bg_ref),
            )
        )
    ]
    for copy in copies:
        copy.start()
    for copy in copies:
        copy.wait()
    load_params(p_ref, par)
    spread = lambda ref: [jnp.broadcast_to(ref[0:1, i : i + 1], (1, LANES)) for i in range(3)]
    angles = spread(cam_ref)
    ((turn, basis),) = camera_values(angles)
    get = lambda index: dense_row(par, index)
    scales = [jnp.exp(get(3 + i)) for i in range(3)]
    quaternion, _ = unit([get(6 + i) for i in range(4)])
    spin = spin_of(quaternion)
    frame = [
        [
            (turn[r][0] * spin[0][c] + turn[r][1] * spin[1][c] + turn[r][2] * spin[2][c]) * scales[c]
            for c in range(3)
        ]
        for r in range(2)
    ]
    cov_xx = sum(frame[0][c] * frame[0][c] for c in range(3)) + DILATION
    cov_xy = sum(frame[0][c] * frame[1][c] for c in range(3))
    cov_yy = sum(frame[1][c] * frame[1][c] for c in range(3)) + DILATION
    inverse = 1.0 / (cov_xx * cov_yy - cov_xy * cov_xy)
    shift_x = get(0) - 256.0
    shift_y = get(1) - 512.0
    depth = get(2)
    rec[0:16, :] = turn[0][0] * shift_x + turn[0][1] * shift_y + turn[0][2] * depth + 256.0
    rec[16:32, :] = turn[1][0] * shift_x + turn[1][1] * shift_y + turn[1][2] * depth + 512.0
    rec[32:48, :] = cov_yy * inverse
    rec[48:64, :] = -cov_xy * inverse
    rec[64:80, :] = cov_xx * inverse
    rec[80:96, :] = sigmoid(get(10))
    for c in range(3):
        colour = jnp.full((16, LANES), 0.5, F32)
        for k in range(16):
            colour = colour + basis[k] * get(11 + 3 * k + c)
        rec[96 + 16 * c : 112 + 16 * c, :] = colour
    lists, order = slot_lists(vis_ref)
    low = lists & 127
    high = lists // LANES
    channels = []
    for ch in range(9):
        value = jnp.zeros((K, LANES), F32)
        for h in range(16):
            source = jnp.broadcast_to(rec[ch * 16 + h : ch * 16 + h + 1, :], (K, LANES))
            value = jnp.where(high == h, jnp.take_along_axis(source, low, axis=1), value)
        channels.append(value)
    blk = jnp.take_along_axis(jnp.broadcast_to(blk_ref[...], (8, LANES)), order[0:8], axis=1)
    counts = jnp.concatenate([cnt_ref[...], cnt_ref[...]], axis=1)
    ids = jnp.where(iota((1, LANES), 1) // 64 < counts, blk[0:1], -1).astype(F32)
    rank = jnp.sum(
        jnp.where(iota((1, 64), 1) == me, rank_ref[...], 0).astype(F32), axis=1, keepdims=True
    )
    meta = [ids, jnp.broadcast_to(rank, (1, LANES))] + spread(bg_ref) + angles
    to_message(out_ref, jnp.concatenate(channels + meta, axis=0), twice=True)


def across(chunks):
    lane = iota(chunks[0].shape, 1)
    total = [TAPS[5] * x for x in chunks]
    for s in range(1, 6):
        right = [pltpu.roll(x, s, 1) for x in chunks]
        left = [pltpu.roll(x, LANES - s, 1) for x in chunks]
        low, high = lane < s, lane >= LANES - s
        before = [0.0] + right[:-1]
        after = left[1:] + [0.0]
        total = [
            t + TAPS[5 + s] * (jnp.where(low, b, r) + jnp.where(high, a, f))
            for t, b, r, f, a in zip(total, before, right, left, after)
        ]
    return total


def blur(source, start, count=8):
    chunks = []
    for j in range(CHUNKS):
        load = lambda first: source[j, first : first + count, :]
        total = TAPS[5] * load(start + 5)
        for s in range(1, 6):
            total = total + TAPS[5 + s] * (load(start + 5 - s) + load(start + 5 + s))
        chunks.append(total)
    return across(chunks)


def fill_rows(ext, own, chip, next_chip, ch, even):
    for j in range(CHUNKS):
        cols = slice(j * LANES, (j + 1) * LANES)
        ext[j, 0:8, :] = jnp.zeros((8, LANES), F32)
        ext[j, 40:48, :] = jnp.zeros((8, LANES), F32)
        near, far = chip[ch, :, cols], next_chip[ch, :, cols]
        ext[j, 6:16, :] = jnp.where(even, far, near)
        ext[j, 16:32, :] = own[ch, :, cols]
        ext[j, 32:42, :] = jnp.where(even, near, far)


def target_kernel(own, chip, next_chip, ext_ref, mean_ref, square_ref, tmp, sq):
    even = lax.axis_index("space") % 2 == 0

    def channel(ch, carry):
        fill_rows(tmp, own.at[0], chip, next_chip, ch, even)
        for j in range(CHUNKS):
            ext_ref[ch, j] = tmp[j]
            sq[j] = tmp[j] * tmp[j]
        for source, out in ((tmp, mean_ref), (sq, square_ref)):
            for top in range(0, 32, 8):
                blurred = blur(source, 6 + top)
                for j in range(CHUNKS):
                    out[ch, j, top : top + 8, :] = blurred[j]
        return carry

    for ch in range(3):
        channel(ch, 0)


def inverse_kernel(vis_ref, inv_ref):
    lists, _ = slot_lists(vis_ref)
    low = lists & 127
    high = lists // LANES
    total = jnp.zeros((2 * 16, LANES), F32)
    lane = iota((1, LANES), 1)
    for k in range(K):
        here = row(high, k, 16) == iota((16, LANES), 0)
        value = jnp.concatenate(
            [
                jnp.where(here, float(k), 0.0),
                jnp.where(here, jnp.broadcast_to(lane, (16, LANES)).astype(F32), 0.0),
            ],
            axis=0,
        ).astype(BF16)
        table = (row(low, k, LANES) == iota((LANES, LANES), 0)).astype(F32).astype(BF16)
        total = total + lax.dot_general(
            value, table, (((1,), (1,)), ((), ())), preferred_element_type=F32
        )
    inv_ref[...] = total.astype(I32)


def pieces(x):
    first = x.astype(BF16)
    left = x - first.astype(F32)
    second = left.astype(BF16)
    third = (left - second.astype(F32)).astype(BF16)
    return first, second, third


def dot_mask(x, mask, contract):
    dims = (((1,), (contract,)), ((), ()))
    parts = [lax.dot_general(p, mask, dims, preferred_element_type=F32) for p in pieces(x)]
    return parts[0] + (parts[1] + parts[2])


def corners(ids, me):
    block = jnp.maximum(ids, 0.0).astype(I32)
    x = (block % 32 * 16).astype(F32) + 0.5
    y = (me * 16 + block // 32 * 8).astype(F32) + 0.5
    return x, y


def splat_terms(rec, k, x0, y_grid):
    get = lambda ch: jnp.broadcast_to(rec[pl.ds(ch * K + k, 1), :], (8, LANES))
    dy = y_grid - get(1)
    return x0 - get(0), dy, get(2) * -0.5, get(3) * dy, get(4) * -0.5 * dy * dy, get(5)


def render(rec, corner_x, y_grid, logs, colours_out, keep=None):
    def group(g, carry):
        base = corner_x + (g * GROUP).astype(F32)

        def four(kk, state):
            through, log_sum, colours = state
            part = [jnp.ones((8, LANES), F32)] * GROUP
            for k4 in range(4):
                k = kk * 4 + k4
                dx0, dy, ma, mb_y, mc_yy, opacity = splat_terms(rec, k, base, y_grid)
                tint = [
                    jnp.broadcast_to(rec[pl.ds((6 + c) * K + k, 1), :], (8, LANES))
                    for c in range(3)
                ]
                for i in range(GROUP):
                    dx = dx0 + float(i)
                    alpha = opacity * jnp.exp((ma * dx - mb_y) * dx + mc_yy)
                    weight = alpha * through[i]
                    if keep:
                        keep[0][k, g * GROUP + i] = alpha
                        keep[1][k, g * GROUP + i] = weight
                    left = 1.0 - alpha
                    through = through[:i] + (through[i] * left,) + through[i + 1 :]
                    part[i] = part[i] * left
                    colours = (
                        colours[:i]
                        + (tuple(colours[i][c] + weight * tint[c] for c in range(3)),)
                        + colours[i + 1 :]
                    )
            log_sum = tuple(log_sum[i] + jnp.log(part[i]) for i in range(GROUP))
            return through, log_sum, colours

        zero = jnp.zeros((8, LANES), F32)
        start = ((jnp.ones((8, LANES), F32),) * GROUP, (zero,) * GROUP, ((zero,) * 3,) * GROUP)
        through, log_sum, colours = lax.fori_loop(0, 4, four, start, unroll=4)
        for i in range(GROUP):
            rows = pl.ds(pl.multiple_of((g * GROUP + i) * 8, 8), 8)
            logs[rows, :] = log_sum[i]
            if keep:
                keep[2][rows, :] = through[i]
            for c in range(3):
                colours_out[c, rows, :] = colours[i][c]
        return carry

    lax.fori_loop(0, 16 // GROUP, group, 0)


def masks(rest_rows, rest_cols):
    id_row = row(rest_rows, 16, LANES)
    rank_row = row(rest_rows, 17, LANES)
    id_col = jnp.broadcast_to(rest_cols[:, 16:17], (LANES, LANES))
    rank_col = jnp.broadcast_to(rest_cols[:, 17:18], (LANES, LANES))
    live = id_row >= 0.0
    same = jnp.where((id_row == id_col) & live, 1.0, 0.0)
    nearer = jnp.where(rank_col < rank_row, same, 0.0).astype(BF16)
    block = (iota((LANES, LANES), 1) % 64).astype(F32)
    member = jnp.where(id_col == block, 1.0, 0.0).astype(BF16)
    return live, same.astype(BF16), nearer, member


def to_rows(before, open_sky, colours, member, sky_rows, blocks_ref, strip_ref):
    lane = iota((8, LANES), 1)
    for c in range(3):
        blocks_ref[c] = (
            dot_mask(before * colours[c], member, 0) + sky_rows[18 + c : 19 + c] * open_sky
        )
    pair = lane % 16 // 2
    for c in range(3):
        for p in range(8):
            blocks_ref[c, p * 16 : p * 16 + 8, :] = jnp.where(
                lane < 64,
                blocks_ref[c, p * 16 : p * 16 + 8, :],
                blocks_ref[c, p * 16 + 8 : p * 16 + 16, :],
            )
    for br in range(2):
        for t in range(CHUNKS):
            index = lane % 2 * 64 + (br * 32 + 8 * t) + lane // 16
            values = [None] * 3
            for p in range(8):
                for c in range(3):
                    got = jnp.take_along_axis(
                        blocks_ref[c, p * 16 : p * 16 + 8, :], index, axis=1
                    )
                    values[c] = jnp.where(pair == p, got, values[c]) if p else got
            for c in range(3):
                strip_ref[c, br * 8 : br * 8 + 8, t * LANES : (t + 1) * LANES] = values[c]


def blend_kernel(
    recv_ref,
    order_ref,
    strip_ref,
    chip_ref,
    far_ref,
    rec,
    colour_ref,
    before_ref,
    total_ref,
    nearer_ref,
    through_ref,
    alphas,
    weights,
    logs,
    blocks_ref,
    far_rec,
    far_colour,
    far_strip,
):
    me = lax.axis_index("space")
    even = me % 2 == 0
    row_of = iota((8, LANES), 0).astype(F32)

    first, rest_rows, rest_cols = from_message(recv_ref)
    rec[0:LANES, :] = first
    rec[LANES:TABLE, :] = rest_rows[0:24]
    corner_x, corner_y = corners(row(rest_rows, 16, 8), me)
    render(rec, corner_x, corner_y + row_of, logs, colour_ref, (alphas, weights, through_ref))
    live, same, nearer, member = masks(rest_rows, rest_cols)
    nearer_ref[...] = nearer
    ahead = dot_mask(logs[...], jnp.concatenate([nearer, same, member], axis=1), 0)
    before = jnp.where(live, jnp.exp(ahead[:, 0:LANES]), 0.0)
    before_ref[...] = before
    total_ref[...] = jnp.where(live, jnp.exp(ahead[:, LANES : 2 * LANES]), 0.0)
    to_rows(
        before, jnp.exp(ahead[:, 2 * LANES :]), colour_ref, member, rest_rows, blocks_ref, strip_ref
    )
    chip_ref[...] = jnp.where(even, strip_ref[:, 6:16, :], strip_ref[:, 0:10, :])

    first, rest_rows, rest_cols = from_message(recv_ref, far=True)
    far_rec[0:LANES, :] = first
    far_rec[LANES:TABLE, :] = rest_rows[0:24]
    corner_x, corner_y = corners(row(rest_rows, 16, 8), jnp.where(even, me - 1, me + 1))
    render(far_rec, corner_x, corner_y + row_of, logs, far_colour)
    live, _, nearer, member = masks(rest_rows, rest_cols)
    ahead = dot_mask(logs[...], jnp.concatenate([nearer, member], axis=1), 0)
    before = jnp.where(live, jnp.exp(ahead[:, 0:LANES]), 0.0)
    to_rows(
        before, jnp.exp(ahead[:, LANES:]), far_colour, member, rest_rows, blocks_ref, far_strip
    )
    near_edge = jnp.where(even, far_strip[:, 6:16, :], far_strip[:, 0:10, :])
    far_ref[...] = jnp.where((me > 0) & (me < 63), near_edge, 0.0)


def loss_kernel(
    strip_ref,
    chip,
    next_chip,
    ext_ref,
    mean_ref,
    square_ref,
    rec,
    colour_ref,
    before_ref,
    total_ref,
    nearer_ref,
    through_ref,
    alphas,
    weights,
    out_ref,
    rendered_ref,
    ext,
    prod,
    stat,
    grads,
    spread_grads,
    pulled,
    cot,
    behind_cot,
    sums,
    table,
    sems,
):
    copy = pltpu.make_async_copy(strip_ref, rendered_ref, sems.at[0])
    copy.start()
    me = lax.axis_index("space")
    first_c, second_c = SSIM_FIRST, SSIM_SECOND
    even = me % 2 == 0

    def channel(ch, loss):
        fill_rows(ext, strip_ref, chip, next_chip, ch, even)
        for j in range(CHUNKS):
            a = ext[j]
            prod[0, j] = a * a
            prod[1, j] = a * ext_ref[ch, j]
        for top in range(0, 32, 8):
            t_row = iota((8, LANES), 0) + top
            where = me * 16 - 5 + t_row
            inside = jnp.where((where >= 0) & (where < 1024) & (t_row < 26), -0.2, 0.0)
            own = (t_row >= 5) & (t_row < 21)
            blurred = [blur(source, 6 + top) for source in (ext, prod.at[0], prod.at[1])]
            rows = slice(top, top + 8)
            for j in range(CHUNKS):
                ma, mb = blurred[0][j], mean_ref[ch, j, rows, :]
                mab = ma * mb
                squares = ma * ma + mb * mb
                n1 = 2.0 * mab + first_c
                n2 = 2.0 * (blurred[2][j] - mab) + second_c
                d1 = squares + first_c
                d2 = (blurred[1][j] + square_ref[ch, j, rows, :]) - squares + second_c
                inverse = 1.0 / (d1 * d2)
                ssim = n1 * n2 * inverse
                loss = loss + jnp.where(own, 0.2 - 0.2 * ssim, 0.0)
                seed = inside * inverse
                g1 = seed * n2
                g2 = seed * n1
                scaled = seed * ssim
                gd1 = scaled * d2
                gd2 = scaled * d1
                stat[0, j, rows, :] = 2.0 * (mb * (g1 - g2) + ma * (gd2 - gd1))
                stat[1, j, rows, :] = -gd2
                stat[2, j, rows, :] = 2.0 * g2
        for top in (0, 8):
            spread = [blur(stat.at[q], top) for q in range(3)]
            rows = slice(16 + top, 24 + top)
            for j in range(CHUNKS):
                a = ext[j, rows, :]
                b = ext_ref[ch, j, rows, :]
                differ = a - b
                root = jnp.sqrt(differ * differ + SMOOTHING)
                loss = loss + 0.8 * root
                grads[ch, j, top : top + 8, :] = (
                    spread[0][j] + 2.0 * a * spread[1][j] + b * spread[2][j] + 0.8 * differ / root
                )
        return loss

    loss = jnp.zeros((8, LANES), F32)
    for ch in range(3):
        loss = channel(ch, loss)
    loss = jnp.sum(jnp.sum(loss, axis=0, keepdims=True), axis=1, keepdims=True)

    ids = row(rec[...], META, 8)
    live = ids >= 0.0
    block = jnp.maximum(ids, 0.0).astype(I32)
    lane = iota((8, LANES), 1)
    place = lane % 64 // 8
    for p in range(8):
        start = lane % 8 * 16 + 2 * p + lane // 64
        both = [None] * 3
        for n in range(8):
            br, t = divmod(n, CHUNKS)
            for c in range(3):
                got = jnp.take_along_axis(grads[c, t, br * 8 : br * 8 + 8, :], start, axis=1)
                both[c] = jnp.where(place == n, got, both[c]) if n else got
        for c in range(3):
            spread_grads[c, p] = both[c]
    for odd in range(2):
        index = block + 64 * odd
        for p in range(8):
            for c in range(3):
                value = jnp.take_along_axis(spread_grads[c, p], index, axis=1)
                first = (2 * p + odd) * 8
                pulled[c, first : first + 8, :] = jnp.where(live, value, 0.0)
    before = before_ref[...]
    behind = jnp.zeros((LANES, LANES), F32)
    sky = jnp.zeros((LANES, LANES), F32)
    for c in range(3):
        g = pulled[c]
        scaled = before * g
        cot[c] = scaled
        behind = behind + scaled * colour_ref[c]
        sky = sky + rec[META + 2 + c : META + 3 + c, :] * g
    log_cot = dot_mask(behind, nearer_ref[...], 1) + total_ref[...] * sky
    left = through_ref[...]
    some = left > 0.0
    behind_cot[...] = jnp.where(some, log_cot / jnp.where(some, left, 1.0), 0.0)

    corner_x, corner_y = corners(ids, me)
    y_grid = corner_y + iota((8, LANES), 0).astype(F32)

    def group(g, carry):
        base = corner_x + (g * GROUP).astype(F32)
        rows = [pl.ds(pl.multiple_of((g * GROUP + i) * 8, 8), 8) for i in range(GROUP)]
        suffix = tuple(behind_cot[rows[i], :] for i in range(GROUP))
        pull = [[cot[c, rows[i], :] for c in range(3)] for i in range(GROUP)]
        zero = jnp.zeros((8, LANES), F32)

        def back(step, suffix):
            k = K - 1 - step
            get = lambda ch: jnp.broadcast_to(rec[pl.ds(ch * K + k, 1), :], (8, LANES))
            dx0 = base - get(0)
            tint = [get(6 + c) for c in range(3)]
            s0, s1, s2 = zero, zero, zero
            shade = [zero] * 3
            after = []
            for i in range(GROUP):
                dx = dx0 + float(i)
                weight = weights[k, g * GROUP + i]
                gain = (
                    pull[i][0] * tint[0] + pull[i][1] * tint[1] + pull[i][2] * tint[2] - suffix[i]
                )
                after.append(suffix[i] + alphas[k, g * GROUP + i] * gain)
                moment = weight * gain
                shade = [shade[c] + weight * pull[i][c] for c in range(3)]
                moment_x = moment * dx
                s0 = s0 + moment
                s1 = s1 + moment_x
                s2 = s2 + moment_x * dx
            for n, value in enumerate([s0, s1, s2] + shade):
                sums[k, n] = jnp.where(g == 0, value, sums[k, n] + value)
            return tuple(after)

        lax.fori_loop(0, K, back, suffix, unroll=2)
        return carry

    lax.fori_loop(0, 16 // GROUP, group, 0)

    def finish(k, carry):
        get = lambda ch: rec[pl.ds(ch * K + k, 1), :]
        dy = y_grid - jnp.broadcast_to(get(1), (8, LANES))
        s0, s1, s2 = sums[k, 0], sums[k, 1], sums[k, 2]
        fold = lambda value: jnp.sum(value, axis=0, keepdims=True)
        s0_y = s0 * dy
        m0, mx, mxx = fold(s0), fold(s1), fold(s2)
        my, mxy, myy = fold(s0_y), fold(s1 * dy), fold(s0_y * dy)
        conic_a, conic_b, conic_c = get(2), get(3), get(4)
        out = [
            conic_a * mx + conic_b * my,
            conic_b * mx + conic_c * my,
            -0.5 * mxx,
            -mxy,
            -0.5 * myy,
            m0,
        ] + [fold(sums[k, 3 + c]) for c in range(3)]
        for ch in range(9):
            table[pl.ds(ch * K + k, 1), :] = out[ch]
        return carry

    lax.fori_loop(0, K, finish, 0, unroll=4)
    table[META:TABLE, :] = jnp.concatenate(
        [jnp.broadcast_to(loss, (5, LANES)), rec[META + 5 : TABLE, :]], axis=0
    )
    to_message(out_ref, table[...])
    copy.wait()


def gather_kernel(recv_ref, inv_ref, out_ref, loss_ref, rec):
    first, rest_rows, rest_cols = from_message(recv_ref)
    rec[0:LANES, :] = first
    rec[LANES:META, :] = rest_rows[0:16]
    at_k = inv_ref[0:16, :]
    at_slot = inv_ref[16:32, :]
    for ch in range(9):
        value = jnp.zeros((16, LANES), F32)
        for k in range(K):
            source = jnp.broadcast_to(rec[ch * K + k : ch * K + k + 1, :], (16, LANES))
            value = jnp.where(at_k == k, jnp.take_along_axis(source, at_slot, axis=1), value)
        out_ref[ch * 16 : ch * 16 + 16, :] = value
    out_ref[META:TABLE, :] = rest_rows[16:24]
    total = jnp.sum(rest_cols[0:64, 16:17], axis=0, keepdims=True)
    loss_ref[...] = jnp.broadcast_to(total * (1.0 / 1572864.0), (1, LANES))


def lay_out(rows, start, scratch, out_ref):
    for n, value in enumerate(rows):
        index = start + n
        scratch[index // 8, pl.ds(index % 8, 16, stride=8), :] = value
    for first in range(start, start + len(rows), 8):
        count = min(8, start + len(rows) - first)
        for chunk in range(16):
            out_ref[first : first + count, chunk * LANES : (chunk + 1) * LANES] = scratch[
                first // 8, chunk * 8 : chunk * 8 + count, :
            ]


def pull_kernel(p_ref, rec0, rec1, rec2, rec3, out_hbm, par, views, res, out_ref, sems):
    me = lax.axis_index("view")
    load_params(p_ref, par, 2)
    for d, source in enumerate((rec0, rec1, rec2, rec3)):
        views[(me - d + 4) % 4] = source[...]
    get = lambda index: dense_row(par, index)
    scales = [jnp.exp(get(3 + i)) for i in range(3)]
    quaternion, inverse_norm = unit([get(6 + i) for i in range(4)])
    spin = spin_of(quaternion)
    coefficients = []
    cameras = camera_values(
        [
            jnp.concatenate([views[v, META + 5 + i : META + 6 + i, :] for v in range(4)], axis=0)
            for i in range(3)
        ]
    )
    for k in range(16):
        for c in range(3):
            rows = slice(96 + 16 * c, 112 + 16 * c)
            total = cameras[0][1][k] * views[0, rows, :]
            for v in range(1, 4):
                total = total + cameras[v][1][k] * views[v, rows, :]
            coefficients.append(total)
    lay_out(coefficients[5:], 16, res, out_ref)
    body = pltpu.make_async_copy(out_ref.at[16:59], out_hbm.at[16:59], sems.at[0])
    body.start()
    zero = jnp.zeros((16, LANES), F32)
    g_pos = [zero] * 3
    g_frame_spin = [[zero] * 3 for _ in range(3)]
    g_log = [zero] * 3
    g_logit = zero
    for v in range(4):
        turn = cameras[v][0]
        g = [views[v, ch * 16 : ch * 16 + 16, :] for ch in range(6)]
        unscaled = [
            [turn[r][0] * spin[0][c] + turn[r][1] * spin[1][c] + turn[r][2] * spin[2][c] for c in range(3)]
            for r in range(2)
        ]
        frame = [[unscaled[r][c] * scales[c] for c in range(3)] for r in range(2)]
        cov_xx = sum(frame[0][c] * frame[0][c] for c in range(3)) + DILATION
        cov_xy = sum(frame[0][c] * frame[1][c] for c in range(3))
        cov_yy = sum(frame[1][c] * frame[1][c] for c in range(3)) + DILATION
        inverse = 1.0 / (cov_xx * cov_yy - cov_xy * cov_xy)
        ca, cb, cc = cov_yy * inverse, -cov_xy * inverse, cov_xx * inverse
        ga, gb, gc = g[2], 0.5 * g[3], g[4]
        left = [
            [ca * ga + cb * gb, ca * gb + cb * gc],
            [cb * ga + cc * gb, cb * gb + cc * gc],
        ]
        g_xx = -(left[0][0] * ca + left[0][1] * cb)
        g_xy = -(left[0][0] * cb + left[0][1] * cc)
        g_yy = -(left[1][0] * cb + left[1][1] * cc)
        for c in range(3):
            gf0 = 2.0 * (g_xx * frame[0][c] + g_xy * frame[1][c])
            gf1 = 2.0 * (g_xy * frame[0][c] + g_yy * frame[1][c])
            g_log[c] = g_log[c] + gf0 * frame[0][c] + gf1 * frame[1][c]
            for m in range(3):
                g_frame_spin[m][c] = g_frame_spin[m][c] + (turn[0][m] * gf0 + turn[1][m] * gf1)
        for m in range(3):
            g_pos[m] = g_pos[m] + turn[0][m] * g[0] + turn[1][m] * g[1]
        g_logit = g_logit + g[5]
    s = [[g_frame_spin[m][c] * scales[c] for c in range(3)] for m in range(3)]
    w, x, y, z = quaternion
    g_unit = [
        2.0 * (x * (s[2][1] - s[1][2]) + y * (s[0][2] - s[2][0]) + z * (s[1][0] - s[0][1])),
        2.0 * (y * (s[0][1] + s[1][0]) + z * (s[0][2] + s[2][0]) + w * (s[2][1] - s[1][2]))
        - 4.0 * x * (s[1][1] + s[2][2]),
        2.0 * (x * (s[0][1] + s[1][0]) + z * (s[1][2] + s[2][1]) + w * (s[0][2] - s[2][0]))
        - 4.0 * y * (s[0][0] + s[2][2]),
        2.0 * (x * (s[0][2] + s[2][0]) + y * (s[1][2] + s[2][1]) + w * (s[1][0] - s[0][1]))
        - 4.0 * z * (s[0][0] + s[1][1]),
    ]
    along = sum(q * g for q, g in zip(quaternion, g_unit))
    g_quat = [(g - q * along) * inverse_norm for q, g in zip(quaternion, g_unit)]
    rest = sigmoid(-get(10))
    rows = g_pos + g_log + g_quat + [g_logit * rest]
    lay_out(rows + coefficients[:5], 0, res, out_ref)
    head = pltpu.make_async_copy(out_ref.at[0:16], out_hbm.at[0:16], sems.at[1])
    head.start()
    body.wait()
    head.wait()


def call(kernel, outs, scratch=(), copied=0, leaving=0, sems=0):
    hbm, vmem = (pl.BlockSpec(memory_space=space) for space in (pltpu.HBM, pltpu.VMEM))
    extra = {}
    if copied:
        extra["in_specs"] = [hbm] * copied
    if leaving:
        extra["out_specs"] = [vmem] * (len(outs) - leaving) + [hbm] * leaving
    count = sems or copied + leaving
    return pl.pallas_call(
        kernel,
        out_shape=[jax.ShapeDtypeStruct(shape, dtype) for shape, dtype in outs],
        scratch_shapes=[pltpu.VMEM(shape, dtype) for shape, dtype in scratch]
        + ([pltpu.SemaphoreType.DMA((count,))] if count else []),
        compiler_params=pltpu.CompilerParams(vmem_limit_bytes=(60 if copied else 16) << 20),
        **extra,
    )


def shards(params, visible, blocks, counts, depth_rank, camera, background, target):
    devices = lax.axis_size("space")
    views = lax.axis_size("view")
    chip = [(i, i ^ 1) for i in range(devices)]
    next_chip = [(i, i + 1 if i % 2 else i - 1) for i in range(1, devices - 1)]
    even = lax.axis_index("space") % 2 == 0
    tile = (LANES, LANES)
    kept = ((K, 16, 8, LANES), F32)
    lists = visible[0].T

    goal_top, goal_bottom = target[0, :, 0:10], target[0, :, 6:16]
    goal_chip = lax.ppermute(jnp.where(even, goal_bottom, goal_top), "space", chip)
    goal_next = lax.ppermute(jnp.where(even, goal_top, goal_bottom), "space", next_chip)
    (message,) = call(
        send_kernel,
        [((64, 1, 640), F32)],
        [
            (params.shape, F32),
            ((1, 3), F32),
            ((K, LANES), I32),
            ((1, LANES), I32),
            ((1, 64), I32),
            ((1, 64), I32),
            ((1, 3), F32),
            ((8, LANES, LANES), F32),
            ((META, LANES), F32),
        ],
        copied=7,
    )(params, camera, lists, blocks, counts, depth_rank, background)
    received = lax.all_to_all(message, "space", 0, 0, tiled=True).reshape(64, 640)
    (inverse,) = call(inverse_kernel, [((32, LANES), I32)])(lists)
    goal, goal_mean, goal_square = call(
        target_kernel,
        [
            ((3, CHUNKS, 48, LANES), F32),
            ((3, CHUNKS, 32, LANES), F32),
            ((3, CHUNKS, 32, LANES), F32),
        ],
        [((CHUNKS, 48, LANES), F32)] * 2,
    )(target, goal_chip, goal_next)
    strip, to_chip, far, records, colours, before, total, nearer, through, alphas, weights = call(
        blend_kernel,
        [
            ((3, 16, 512), F32),
            ((3, 10, 512), F32),
            ((3, 10, 512), F32),
            ((TABLE, LANES), F32),
            ((3, *tile), F32),
            (tile, F32),
            (tile, F32),
            (tile, BF16),
            (tile, F32),
            kept,
            kept,
        ],
        [
            (tile, F32),
            ((3, *tile), F32),
            ((TABLE, LANES), F32),
            ((3, *tile), F32),
            ((3, 16, 512), F32),
        ],
    )(received, inverse)
    strip_chip = lax.ppermute(to_chip, "space", chip)
    reply, rendered = call(
        loss_kernel,
        [((64, 1, 384), F32), ((3, 16, 512), F32)],
        [
            ((CHUNKS, 48, LANES), F32),
            ((2, CHUNKS, 48, LANES), F32),
            ((3, CHUNKS, 32, LANES), F32),
            ((3, CHUNKS, 16, LANES), F32),
            ((3, 8, 8, LANES), F32),
            ((3, *tile), F32),
            ((3, *tile), F32),
            (tile, F32),
            ((K, 6, 8, LANES), F32),
            ((TABLE, LANES), F32),
        ],
        leaving=1,
    )(
        strip,
        strip_chip,
        far,
        goal,
        goal_mean,
        goal_square,
        records,
        colours,
        before,
        total,
        nearer,
        through,
        alphas,
        weights,
    )
    returned = lax.all_to_all(reply, "space", 0, 0, tiled=True).reshape(64, 384)
    record_grads, loss = call(
        gather_kernel,
        [((TABLE, LANES), F32), ((1, LANES), F32)],
        [((META, LANES), F32)],
    )(returned, inverse)
    others = [
        lax.ppermute(record_grads, "view", [(i, (i + d) % views) for i in range(views)])
        for d in range(1, views)
    ]
    (grad_params,) = call(
        pull_kernel,
        [((59, 2048), F32)],
        [
            ((8, LANES, LANES), F32),
            ((4, TABLE, LANES), F32),
            ((8, LANES, LANES), F32),
            (params.shape, F32),
        ],
        leaving=1,
        sems=2,
    )(params, record_grads, *others)
    return (grad_params, rendered[None], loss[0, 0:1])


def solution(mesh):
    in_specs = (
        P(None, "space"),
        P("space", None, None),
        P("space", None),
        P("space", None),
        P("view", None),
        P("view", None),
        P("view", None),
        P("view", None, "space", None),
    )
    out_specs = (P(None, "space"), P("view", None, "space", None), P("view"))
    return jax.shard_map(shards, mesh=mesh, in_specs=in_specs, out_specs=out_specs, check_vma=False)
```
